128 devices in a mesh: dp: 4 (over y), mp: 32 (over z, x, core).
Axes of the slice: x: 4, y: 4, z: 4, core: 2. Of those that a mesh axis runs over, the one named last changes fastest.
Arguments:
- queries: bfloat16 [32, 48, 2048], P('dp'), may hold values from -3 to 3
- new_keys: bfloat16 [32, 48, 2048], P('dp'), may hold values from -3 to 3
- new_values: bfloat16 [32, 48, 2048], P('dp'), may hold values from -6 to 6
- cache_keys: bfloat16 [32, 4096, 2048], P('dp', 'mp'), may hold values from -3 to 3
- cache_values: bfloat16 [32, 4096, 2048], P('dp', 'mp'), may hold values from -6 to 6
- lengths: int32 [32], P('dp'), may hold values from 64 to 4096, as said below
- parents: int32 [32, 48], P('dp'), may hold values from 0 to 46, as said below
- tree_tokens: int32 [32, 48], P('dp'), may hold values from 0 to 77823
- residual: bfloat16 [32, 48, 2048], P('dp'), may hold values from -6 to 6
- out_weight: bfloat16 [2048, 2048], P(('dp', 'mp')), may hold values from -0.125 to 0.125
- norm_gain: float32 [2048], replicated, may hold values from 0.25 to 1.75
- vocab_weight: bfloat16 [2048, 77824], P(None, 'mp'), may hold values from -0.375 to 0.375
Outputs:
- hidden: bfloat16 [32, 48, 2048], P('dp')
- node_logprob: float32 [32, 48], P('dp')
The draws below stay inside these ranges and needn't reach their ends.
Inputs may be any that keep to these rules, and one draw needn't show every extreme that they name: `lengths`: A request's cache length is 4096 or lies between 64 and 512; some request has length 4096 in every draw. parents[r, 0] is 0; for j > 0, parents[r, j] is j - 2 or j - 1 (0 for j = 1); some request's last node has parent 48 - 2 in every draw.
All inputs are finite; a program needn't handle non-finite values.
Results may differ from the reference program's by a relative error of at most 0.007.
Values may be sent and summed in bfloat16 or wider, within the bound.
No kernel may reach another device: no remote copies, remote signals or barrier semaphores. Data moves between devices by JAX's collectives and lax.ppermute only.
A program may use at most 128 MiB of HBM per device.

```python
import jax
import jax.numpy as jnp
from jax import lax

D = 2048
HEADS = 16
HEAD_DIM = 128
TREE = 48
SINK = 4
REQUESTS = 32
CAP = 4096
WINDOW = 2048
VOCAB = 77824


def draw_lengths(key, part):
    key_short = jax.random.fold_in(key, 11)
    key_flag = jax.random.fold_in(key, 12)
    key_pick = jax.random.fold_in(key, 13)
    short = jax.random.randint(key_short, (REQUESTS,), CAP // 64, CAP // 8 + 1)
    flagged = jax.random.randint(key_flag, (REQUESTS,), 0, 8) == 0
    chosen = jax.random.randint(key_pick, (), 0, REQUESTS)
    flagged = flagged | (jnp.arange(REQUESTS, dtype=jnp.int32) == chosen)
    return jnp.where(flagged, CAP, short).astype(jnp.int32)


def draw_parents(key, part):
    nodes = jnp.arange(TREE, dtype=jnp.int32)
    lower = jnp.maximum(nodes - 2, 0)
    upper = jnp.maximum(nodes, 1)
    drawn = jax.random.randint(jax.random.fold_in(key, 21), (REQUESTS, TREE), lower[None, :], upper[None, :])
    rows = jnp.arange(REQUESTS, dtype=jnp.int32)[:, None]
    fixed = (rows == 0) & (nodes[None, :] == TREE - 1)
    drawn = jnp.where(fixed, TREE - 2, drawn)
    return drawn.astype(jnp.int32)


def set_ends(array, stream_key, smallest, high):
    dims = array.shape
    spot = [jax.random.randint(jax.random.fold_in(stream_key, axis), (), 0, dims[axis]) for axis in range(len(dims))]
    array = array.at[tuple(spot)].set(smallest)
    longest = dims.index(max(dims))
    spot[longest] = (spot[longest] + 1) % dims[longest]
    return array.at[tuple(spot)].set(high)


def level_of(rng, extent, pieces, least, high):
    gain = 1.0
    for axis_at, parts in pieces:
        draws = jax.random.uniform(jax.random.fold_in(jax.random.fold_in(rng, 6), axis_at), (parts,), jnp.float32, least / len(pieces), high / len(pieces))
        gain = gain * jnp.repeat(jnp.exp(draws), extent[axis_at] // parts).reshape((-1,) + (1,) * (len(extent) - 1 - axis_at))
    return gain


def gaussian(key, shape, spread, reach, shards=(), kind=jnp.bfloat16):
    values = jax.random.normal(key, shape, jnp.float32) * spread
    if len(shards) > 0:
        values = level_of(key, shape, shards, -0.22, 0.18) * values
    return jnp.clip(values, min=-reach, max=reach).astype(kind)


def setup_inputs(seed: int = 0) -> dict:
    splits = jax.random.split(jax.random.key(seed), 13)
    queries = gaussian(splits[0], (REQUESTS, TREE, D), 1.0, 3.0, ((0, 4),))
    new_keys = gaussian(splits[1], (REQUESTS, TREE, D), 1.0, 3.0, ((0, 4),))
    new_values = gaussian(splits[2], (REQUESTS, TREE, D), 1.0, 6.0, ((0, 4),))
    cache_keys = gaussian(splits[3], (REQUESTS, CAP, D), 1.0, 3.0, ((0, 4), (1, 32)))
    cache_values = gaussian(splits[4], (REQUESTS, CAP, D), 1.0, 6.0, ((0, 4), (1, 32)))
    lengths = draw_lengths(jax.random.fold_in(splits[12], 71), 0)
    parents = draw_parents(jax.random.fold_in(splits[12], 71), 0)
    tree_tokens = set_ends(jax.random.randint(splits[7], (REQUESTS, TREE), 0, VOCAB), jax.random.fold_in(splits[7], 1), 0, VOCAB - 1).astype(jnp.int32)
    residual = gaussian(splits[8], (REQUESTS, TREE, D), 1.0, 6.0, ((0, 4),))
    out_weight = gaussian(splits[9], (D, D), D ** -0.5, 0.125, ((0, 128),))
    norm_gain = jnp.clip(1.0 + 0.15 * jax.random.normal(splits[10], (D,), jnp.float32), 0.25, 1.75)
    vocab_weight = gaussian(splits[11], (D, VOCAB), (D // 9) ** -0.5, 0.375, ((1, 32),))
    return dict(queries=queries, new_keys=new_keys, new_values=new_values, cache_keys=cache_keys, cache_values=cache_values, lengths=lengths, parents=parents, tree_tokens=tree_tokens, residual=residual, out_weight=out_weight, norm_gain=norm_gain, vocab_weight=vocab_weight)


def ancestor_mask(parents):
    tree = parents.shape[-1]
    idx = jnp.arange(tree, dtype=jnp.int32)
    links = ((idx[None, :, None] == idx[None, None, :]) | (parents[:, :, None] == idx[None, None, :])).astype(jnp.float32)
    for _ in range((tree - 1).bit_length()):
        links = jnp.minimum(jnp.einsum('rij,rjk->rik', links, links, precision=lax.Precision.HIGHEST), 1.0)
    return links > 0.5

def reference(queries, new_keys, new_values, cache_keys, cache_values, lengths, parents, tree_tokens, residual, out_weight, norm_gain, vocab_weight):
    scale = HEAD_DIM ** (-0.5)
    ancestors = ancestor_mask(parents)
    positions = jnp.arange(CAP, dtype=jnp.int32)

    def one_request(items):
        query, nkey, nval, ckey, cval, length, anc = items
        q4 = query.reshape(TREE, HEADS, HEAD_DIM).astype(jnp.float32)
        k4 = ckey.reshape(CAP, HEADS, HEAD_DIM).astype(jnp.float32)
        v4 = cval.reshape(CAP, HEADS, HEAD_DIM).astype(jnp.float32)
        nk4 = nkey.reshape(TREE, HEADS, HEAD_DIM).astype(jnp.float32)
        nv4 = nval.reshape(TREE, HEADS, HEAD_DIM).astype(jnp.float32)
        visible = (positions < length) & ((positions < SINK) | (positions >= length - WINDOW))
        cache_e = jnp.where(visible[None, None, :], jnp.exp(jnp.einsum('ihd,shd->his', q4, k4) * scale), 0.0)
        tree_e = jnp.where(anc[None], jnp.exp(jnp.einsum('ihd,jhd->hij', q4, nk4) * scale), 0.0)
        denom = lax.optimization_barrier(jnp.sum(cache_e, -1)) + lax.optimization_barrier(jnp.sum(tree_e, -1))
        cache_r = lax.optimization_barrier(cache_e.astype(jnp.bfloat16)).astype(jnp.float32)
        tree_r = lax.optimization_barrier(tree_e.astype(jnp.bfloat16)).astype(jnp.float32)
        numer = jnp.einsum('his,shd->ihd', cache_r, v4) + jnp.einsum('hij,jhd->ihd', tree_r, nv4)
        return (numer / jnp.transpose(denom)[:, :, None]).reshape(TREE, D).astype(jnp.bfloat16)
    attended = lax.map(one_request, (queries, new_keys, new_values, cache_keys, cache_values, lengths, ancestors))
    flat = attended.reshape(REQUESTS * TREE, D)
    projected = jnp.dot(flat, out_weight, preferred_element_type=jnp.float32)
    hidden = (residual.reshape(REQUESTS * TREE, D).astype(jnp.float32) + projected).astype(jnp.bfloat16)
    hfloat = hidden.astype(jnp.float32)
    normed = (hfloat * lax.rsqrt(lax.optimization_barrier(jnp.mean(hfloat * hfloat, -1, keepdims=True)) + 1e-06) * norm_gain).astype(jnp.bfloat16)
    normed = normed.reshape(REQUESTS, TREE, D)

    def score_request(items):
        rows, par, toks = items
        logits = jnp.dot(rows, vocab_weight, preferred_element_type=jnp.float32)
        total = lax.optimization_barrier(jnp.sum(jnp.exp(logits), -1))
        return logits[par, toks] - jnp.log(total[par])
    node_logprob = lax.map(score_request, (normed, parents, tree_tokens))
    return (hidden.reshape(REQUESTS, TREE, D), node_logprob)
```

```python
import functools

import jax
import jax.numpy as jnp
from jax import lax
from jax.experimental import pallas as pl
from jax.experimental.pallas import tpu as pltpu
from jax.sharding import Mesh, PartitionSpec as P

HEADS = 16
SINK = 4
BF = jnp.bfloat16
F32 = jnp.float32
NT = (((1,), (1,)), ((), ()))
MB = 1 << 20


def attend_kernel(window, lane_off, info_ref, len_ref, par_ref, q_ref, k_ref, v_ref, nk_ref, nv_ref, out_ref, anc_ref):
    r = pl.program_id(0)
    first = info_ref[1]
    treq = info_ref[2]
    length = len_ref[r]
    tree, width = q_ref.shape[1], q_ref.shape[2]
    slots = k_ref.shape[1]
    heads = width // 128
    scale = 128 ** (-0.5)
    lane = lax.broadcasted_iota(jnp.int32, (tree, 128), 1)
    seen = (first < length) & ((first < SINK) | (first + slots - 1 >= length - window))
    is_tree = r == treq

    def attend(keys_ref, values_ref, mask):
        dens = jnp.zeros((tree, 128), F32)
        for h in range(heads):
            cols = slice(h * 128, (h + 1) * 128)
            s = lax.dot_general(q_ref[0, :, cols], keys_ref[0, :, cols], NT, preferred_element_type=F32)
            e = jnp.where(mask, jnp.exp(s * scale), 0.0)
            den = jnp.sum(e, axis=1, keepdims=True)
            dens = jnp.where((lane == lane_off + h) | (lane == lane_off + heads + h), den, dens)
            o = jnp.dot(e.astype(BF), values_ref[0, :, cols], preferred_element_type=F32)
            out_ref[0, :, cols] = o.astype(BF)
        high = dens.astype(BF).astype(F32)
        part = jnp.where(lane < lane_off + heads, high, dens - high)
        out_ref[0, :, width:] = part.astype(BF)

    @pl.when(jnp.logical_not(seen | is_tree))
    def _():
        out_ref[...] = jnp.zeros_like(out_ref)

    @pl.when(seen)
    def _():
        pos = first + lax.broadcasted_iota(jnp.int32, (tree, slots), 1)
        mask = (pos < length) & ((pos < SINK) | (pos >= length - window))
        attend(k_ref, v_ref, mask)

    @pl.when(is_tree)
    def _():
        node = lax.broadcasted_iota(jnp.int32, (1, tree), 1)
        anc_ref[0:1, :] = jnp.where(node == 0, 1.0, 0.0)

        def body(i, carry):
            up = anc_ref[pl.ds(par_ref[r, i], 1), :]
            anc_ref[pl.ds(i, 1), :] = jnp.where(node == i, 1.0, up)
            return carry

        lax.fori_loop(1, tree, body, 0)
        attend(nk_ref, nv_ref, anc_ref[...] > 0.5)


def attend_half(window, lane_off, info, lengths, parents, q, k, v, nk, nv):
    reqs, tree, width = q.shape
    slots = k.shape[1]
    half = width // 2
    qs = pl.BlockSpec((1, tree, half), lambda r, i, l, p: (r, 0, i[0]))
    ks = pl.BlockSpec((1, slots, half), lambda r, i, l, p: (r, 0, i[0]))
    ns = pl.BlockSpec((1, tree, half), lambda r, i, l, p: (jnp.clip(i[2], 0, reqs - 1), 0, i[0]))
    return pl.pallas_call(
        functools.partial(attend_kernel, window, lane_off),
        out_shape=jax.ShapeDtypeStruct((reqs, tree, half + 128), BF),
        grid_spec=pltpu.PrefetchScalarGridSpec(
            num_scalar_prefetch=3,
            grid=(reqs,),
            in_specs=[qs, ks, ks, ns, ns],
            out_specs=pl.BlockSpec((1, tree, half + 128), lambda r, i, l, p: (r, 0, 0)),
            scratch_shapes=[pltpu.VMEM((tree, tree), F32)],
        ),
        compiler_params=pltpu.CompilerParams(vmem_limit_bytes=48 * MB),
        name="attend",
    )(info, lengths, parents, q, k, v, nk, nv)


def combine_kernel(parts_ref, out_ref):
    width = out_ref.shape[2]
    heads = width // 128
    total = jnp.sum(parts_ref[...].astype(F32), axis=0)
    den = total[:, width:]
    lane = lax.broadcasted_iota(jnp.int32, den.shape, 1)
    for h in range(heads):
        d = jnp.sum(jnp.where((lane % heads == h) & (lane < 4 * heads), den, 0.0), axis=1, keepdims=True)
        cols = slice(h * 128, (h + 1) * 128)
        val = (total[:, cols] / d).astype(BF)
        for c in range(out_ref.shape[0]):
            out_ref[c, :, cols] = val


def combine(parts, copies):
    rows, cols = parts.shape[1], parts.shape[2]
    return pl.pallas_call(
        combine_kernel,
        out_shape=jax.ShapeDtypeStruct((copies, rows, cols - 128), BF),
        compiler_params=pltpu.CompilerParams(vmem_limit_bytes=48 * MB),
        name="combine",
    )(parts)


def project_kernel(info_ref, att_ref, w_ref, res_ref, out_ref):
    nx, nc, rows, half = att_ref.shape
    acc = res_ref[...].astype(F32).reshape(nx * rows, res_ref.shape[2])
    for c in range(nc):
        a = jnp.concatenate([att_ref[x, c] for x in range(nx)], axis=0)
        acc = acc + jnp.dot(a, w_ref[c * half:(c + 1) * half, :], preferred_element_type=F32)
    hid = acc.astype(BF)
    for i in range(out_ref.shape[0]):
        out_ref[i] = hid


def project(info, att, w, residual, copies):
    nx, nc, rows, half = att.shape
    tree = residual.shape[1]
    reqs = nx * rows // tree
    cols = w.shape[1]
    return pl.pallas_call(
        project_kernel,
        out_shape=jax.ShapeDtypeStruct((copies, nx * rows, cols), BF),
        grid_spec=pltpu.PrefetchScalarGridSpec(
            num_scalar_prefetch=1,
            grid=(1,),
            in_specs=[
                pl.BlockSpec(att.shape, lambda g, i: (0, 0, 0, 0)),
                pl.BlockSpec(w.shape, lambda g, i: (0, 0)),
                pl.BlockSpec((reqs, tree, cols), lambda g, i: (i[0], 0, i[1])),
            ],
            out_specs=pl.BlockSpec((copies, nx * rows, cols), lambda g, i: (0, 0, 0)),
        ),
        compiler_params=pltpu.CompilerParams(vmem_limit_bytes=48 * MB),
        name="project",
    )(info, att, w, residual)


def vocab_kernel(tree, chunks, info_ref, mine_ref, theirs_ref, gain_ref, tok_ref, w_ref, hid_ref, stat_ref, x_ref, wbuf_ref, sem):
    copies = []
    for i, (start, size) in enumerate(chunks):
        cp = pltpu.make_async_copy(w_ref.at[:, pl.ds(start, size)], wbuf_ref.at[:, pl.ds(start, size)], sem.at[i])
        cp.start()
        copies.append(cp)
    core = info_ref[0]
    nz, nx, rows, cols = mine_ref.shape
    half = nx * cols
    for z in range(nz):
        rs = slice(z * rows, (z + 1) * rows)
        squares = jnp.zeros((rows, cols), F32)
        for x in range(nx):
            mine, theirs = mine_ref[z, x], theirs_ref[z, x]
            low = jnp.where(core == 0, mine, theirs)
            high = jnp.where(core == 0, theirs, mine)
            hid_ref[rs, x * cols:(x + 1) * cols] = low
            hid_ref[rs, half + x * cols:half + (x + 1) * cols] = high
            squares = squares + low.astype(F32) * low.astype(F32) + high.astype(F32) * high.astype(F32)
        inv = lax.rsqrt(jnp.sum(squares, axis=1, keepdims=True) / (2 * half) + 1e-06)
        for j in range(2 * nx):
            cs = slice(j * cols, (j + 1) * cols)
            x_ref[rs, cs] = (hid_ref[rs, cs].astype(F32) * inv * gain_ref[:, cs]).astype(BF)
    tokens = nz * rows
    reqs = tokens // tree
    sums = jnp.zeros((tokens, 128), F32)
    pick1 = jnp.zeros((tokens, 128), F32)
    pick2 = jnp.zeros((tokens, 128), F32)
    pick0 = [jnp.zeros((8, 128), F32) for _ in range(reqs)]
    lane = lax.broadcasted_iota(jnp.int32, (tokens, 128), 1)
    base = info_ref[1]
    t1 = tok_ref[:, 0:1] - base - lane
    t2 = tok_ref[:, 1:2] - base - lane
    t0 = [tok_ref[r * tree:r * tree + 8, 2:3] - base - lane[:8] for r in range(reqs)]
    for (start, size), cp in zip(chunks, copies):
        cp.wait()
        for at in range(start, start + size, 128):
            step = min(256, start + size - at) if (at - start) % 256 == 0 else 0
            if step == 0:
                continue
            logits = jnp.dot(x_ref[...], wbuf_ref[:, at:at + step], preferred_element_type=F32)
            for o in range(0, step, 128):
                lg = logits[:, o:o + 128]
                sums = sums + jnp.exp(lg)
                pick1 = jnp.where(t1 == at + o, lg, pick1)
                pick2 = jnp.where(t2 == at + o, lg, pick2)
                for r in range(reqs):
                    pick0[r] = jnp.where(t0[r] == at + o, lg[r * tree:r * tree + 8], pick0[r])
    zero = jnp.zeros((tree - 8, 128), F32)
    pick0 = jnp.concatenate([p for r in range(reqs) for p in (pick0[r], zero)], axis=0)
    stats = [jnp.sum(jnp.transpose(a), axis=0, keepdims=True) for a in (sums, pick1, pick2, pick0)]
    stats = jnp.concatenate(stats + [jnp.zeros((4, tokens), F32)], axis=0)
    for i in range(stat_ref.shape[0]):
        stat_ref[i] = stats


def vocab(info, mine, theirs, gain, toks, w, tree, copies):
    nz, nx, rows, cols = mine.shape
    tokens, width, size = nz * rows, 2 * nx * cols, w.shape[1]
    chunks = []
    at = 0
    while at < size:
        step = min(512, size - at)
        chunks.append((at, step))
        at += step
    vm = pl.BlockSpec(memory_space=pltpu.VMEM)
    return pl.pallas_call(
        functools.partial(vocab_kernel, tree, tuple(chunks)),
        out_shape=(
            jax.ShapeDtypeStruct((tokens, width), BF),
            jax.ShapeDtypeStruct((copies, 8, tokens), F32),
        ),
        in_specs=[pl.BlockSpec(memory_space=pltpu.SMEM), vm, vm, vm, vm, pl.BlockSpec(memory_space=pl.ANY)],
        out_specs=(vm, vm),
        scratch_shapes=[
            pltpu.VMEM((tokens, width), BF),
            pltpu.VMEM((width, size), BF),
            pltpu.SemaphoreType.DMA((len(chunks),)),
        ],
        compiler_params=pltpu.CompilerParams(vmem_limit_bytes=56 * MB),
        name="vocab",
    )(info, mine, theirs, gain, toks, w)


def local(
    queries, new_keys, new_values, cache_keys, cache_values, lengths, parents,
    tree_tokens, residual, out_weight, norm_gain, vocab_weight,
):
    reqs, tree, width = queries.shape
    slots = cache_keys.shape[1]
    z, x, core = lax.axis_index("z"), lax.axis_index("x"), lax.axis_index("core")
    nz, nx, nc = lax.axis_size("z"), lax.axis_size("x"), lax.axis_size("core")
    shard = (z * nx + x) * nc + core
    shards = nz * nx * nc
    window = slots * shards // 2
    half = width // nc
    block = half // nx
    tokens = reqs * tree
    swap = [(0, 1), (1, 0)]

    w = out_weight.reshape(-1, nc, nx, block).transpose(2, 1, 0, 3).reshape(nx * nc, -1, block)
    w = lax.all_to_all(w, ("x", "core"), 0, 0).reshape(-1, block)
    w = lax.all_gather(w, ("dp", "z"), axis=0, tiled=True)

    treq = jnp.where(shard < 2 * reqs, shard - reqs, -1)
    args = (lengths, parents, queries, cache_keys, cache_values, new_keys, new_values)
    scal = lambda h: jnp.stack([h, shard * slots, treq]).astype(jnp.int32)
    send = attend_half(window, 0, scal(1 - core), *args)
    got = lax.ppermute(send, "core", swap)
    keep = attend_half(window, 16, scal(core), *args)
    part = keep + got
    part = part.reshape(nz * nx, tokens // (nz * nx), half + 128)
    part = lax.all_to_all(part, ("z", "x"), 0, 0)
    att = combine(part, nx * nc)
    att = lax.all_to_all(att, ("x", "core"), 0, 0).reshape(nx, nc, -1, half)
    info = jnp.stack([z, core * nx + x]).astype(jnp.int32)
    hid = project(info, att, w, residual, nz * nx)
    hid = lax.all_to_all(hid, ("z", "x"), 0, 0).reshape(nz, nx, -1, block)
    other = lax.ppermute(hid, "core", swap)

    base = shard * vocab_weight.shape[1]
    pad = jnp.full((reqs, 2), -1, jnp.int32)
    shifted = jnp.concatenate([tree_tokens, pad], axis=1)
    toks = jnp.stack([shifted[:, 1:tree + 1].reshape(-1), shifted[:, 2:].reshape(-1), jnp.where(jnp.arange(tree) == 0, tree_tokens, -1).reshape(-1)], axis=1)
    info = jnp.stack([core, base]).astype(jnp.int32)
    hidden, stats = vocab(info, hid, other, norm_gain.reshape(1, -1), toks, vocab_weight, tree, shards)
    stats = jnp.sum(lax.all_to_all(stats, ("z", "x", "core"), 0, 0), axis=0)
    total, child1, child2, own = (stats[i].reshape(reqs, tree) for i in range(4))
    logt = jnp.log(total)
    back = lambda a, s: jnp.concatenate([a[:, :s], a[:, :tree - s]], axis=1)
    node = jnp.arange(tree)
    near = parents == node - 1
    first = node == 0
    picked = jnp.where(first, own, jnp.where(near, back(child1, 1), back(child2, 2)))
    logt = jnp.where(first, logt, jnp.where(near, back(logt, 1), back(logt, 2)))
    return hidden.reshape(reqs, tree, width), picked - logt


def solution(mesh):
    sizes = (mesh.shape["dp"], 4, 4, 2)
    grid = Mesh(mesh.devices.reshape(sizes), ("dp", "z", "x", "core"))
    mp = ("z", "x", "core")
    row = P("dp", None, None)
    placed = (
        row, row, row, P("dp", mp, None), P("dp", mp, None), P("dp"), P("dp", None), P("dp", None), row,
        P(("dp",) + mp, None), P(), P(None, mp),
    )
    return jax.shard_map(local, mesh=grid, in_specs=placed, out_specs=(row, P("dp", None)), check_vma=False)
```

```python
import functools

import jax
import jax.numpy as jnp
from jax import lax
from jax.experimental import pallas as pl
from jax.experimental.pallas import tpu as pltpu
from jax.sharding import Mesh, PartitionSpec as P

HEADS = 16
SINK = 4
BF = jnp.bfloat16
F32 = jnp.float32
NT = (((1,), (1,)), ((), ()))
TN = (((0,), (0,)), ((), ()))
CORE, FIRST, TREQ, Z, BLOCK, DP, BASE = range(7)
MB = 1 << 20


def attend_kernel(window, lane_off, info_ref, len_ref, par_ref, q_ref, k_ref, v_ref, nk_ref, nv_ref, out_ref, anc_ref):
    step = pl.program_id(0)
    first = info_ref[FIRST]
    treq = info_ref[TREQ]
    reqs, tree, width = q_ref.shape
    slots = k_ref.shape[1]
    heads = width // 128
    scale = 128 ** (-0.5) * 1.4426950408889634

    def attend(r, keys, values, mask):
        dens = []
        scores = [
            lax.dot_general(keys(h), q_ref[r, :, h * 128:(h + 1) * 128], NT, preferred_element_type=F32)
            for h in range(heads)
        ]
        exps = [jnp.where(mask, jnp.exp2(s * scale), 0.0) for s in scores]
        for h in range(heads):
            dens.append(jnp.sum(exps[h], axis=0, keepdims=True))
            o = lax.dot_general(exps[h].astype(BF), values(h), TN, preferred_element_type=F32)
            out_ref[r, :, h * 128:(h + 1) * 128] = o.astype(BF)
        dens = jnp.concatenate(dens, axis=0)
        high = dens.astype(BF).astype(F32)
        pieces = [high, dens - high, jnp.zeros((128 - lane_off - 2 * heads, tree), F32)]
        if lane_off:
            pieces = [jnp.zeros((lane_off, tree), F32)] + pieces
        out_ref[r, :, width:] = jnp.transpose(jnp.concatenate(pieces, axis=0)).astype(BF)

    @pl.when(treq < 0)
    def _():
        pos = first + lax.broadcasted_iota(jnp.int32, (slots, tree), 0)
        for r in range(reqs):
            length = len_ref[step * reqs + r]
            mask = (pos < length) & ((pos < SINK) | (pos >= length - window))
            attend(
                r, lambda h: k_ref[r, :, h * 128:(h + 1) * 128], lambda h: v_ref[r, :, h * 128:(h + 1) * 128], mask
            )

    @pl.when(treq >= 0)
    def _():
        out_ref[...] = jnp.zeros_like(out_ref)

        @pl.when(treq // reqs == step)
        def _():
            node = lax.broadcasted_iota(jnp.int32, (1, 128), 1)
            anc_ref[...] = jnp.zeros_like(anc_ref)
            anc_ref[0:1, :] = jnp.where(node == 0, 1.0, 0.0)

            def body(i, carry):
                up = anc_ref[pl.ds(par_ref[treq, i], 1), :]
                anc_ref[pl.ds(i, 1), :] = jnp.where(node == i, 1.0, up)
                return carry

            lax.fori_loop(1, tree, body, 0)
            mask = jnp.transpose(anc_ref[...])[:tree, :tree] > 0.5
            attend(
                lax.rem(treq, reqs), lambda h: nk_ref[0, :, h * 128:(h + 1) * 128],
                lambda h: nv_ref[0, :, h * 128:(h + 1) * 128], mask,
            )


def attend_half(window, mine, info, lengths, parents, q, k, v, nk, nv):
    reqs, tree, width = q.shape
    slots = k.shape[1]
    half = width // 2
    group = reqs // 2
    hidx = (lambda i: i[CORE]) if mine else (lambda i: 1 - i[CORE])
    qs = pl.BlockSpec((group, tree, half), lambda r, i, l, p: (r, 0, hidx(i)))
    ks = pl.BlockSpec((group, slots, half), lambda r, i, l, p: (r, 0, hidx(i)))
    ns = pl.BlockSpec((1, tree, half), lambda r, i, l, p: (jnp.clip(i[TREQ], 0, reqs - 1), 0, hidx(i)))
    q, k, v, nk, nv = (pltpu.with_memory_space_constraint(a, pltpu.HBM) for a in (q, k, v, nk, nv))
    return pl.pallas_call(
        functools.partial(attend_kernel, window, 16 if mine else 0),
        out_shape=jax.ShapeDtypeStruct((reqs, tree, half + 128), BF),
        grid_spec=pltpu.PrefetchScalarGridSpec(
            num_scalar_prefetch=3,
            grid=(reqs // group,),
            in_specs=[qs, ks, ks, ns, ns],
            out_specs=pl.BlockSpec((group, tree, half + 128), lambda r, i, l, p: (r, 0, 0)),
            scratch_shapes=[pltpu.VMEM((128, 128), F32)],
        ),
        compiler_params=pltpu.CompilerParams(vmem_limit_bytes=48 * MB),
        name="attend_mine" if mine else "attend_theirs",
    )(info, lengths, parents, q, k, v, nk, nv)


def combine_kernel(parts_ref, out_ref):
    heads = out_ref.shape[1]
    width = heads * 128
    total = jnp.sum(parts_ref[...].astype(F32), axis=0)
    den = total[:, width:]
    lane = lax.broadcasted_iota(jnp.int32, den.shape, 1)
    for h in range(heads):
        d = jnp.sum(jnp.where((lane % heads == h) & (lane < 4 * heads), den, 0.0), axis=1, keepdims=True)
        val = (total[:, h * 128:(h + 1) * 128] / d).astype(BF)
        for c in range(out_ref.shape[0]):
            out_ref[c, h] = val


def combine(parts, copies):
    rows, cols = parts.shape[1], parts.shape[2]
    return pl.pallas_call(
        combine_kernel,
        out_shape=jax.ShapeDtypeStruct((copies, cols // 128 - 1, rows, 128), BF),
        compiler_params=pltpu.CompilerParams(vmem_limit_bytes=48 * MB),
        name="combine",
    )(parts)


def project_kernel(info_ref, att_ref, *refs):
    w_refs, res_ref, out_ref = refs[:-2], refs[-2], refs[-1]
    nx, heads, rows, _ = att_ref.shape
    ny, nz = len(w_refs), w_refs[0].shape[0]
    y, z = info_ref[DP], info_ref[Z]
    acc = res_ref[...].astype(F32).reshape(nx * rows, res_ref.shape[2])
    for i in range(ny):
        for j in range(nz):
            h = lax.rem(y + ny - i, ny) * nz + lax.rem(z + nz - j, nz)
            a = jnp.concatenate([att_ref[x, h] for x in range(nx)], axis=0)
            acc = acc + jnp.dot(a, w_refs[i][j], preferred_element_type=F32)
    hid = acc.astype(BF)
    for i in range(out_ref.shape[0]):
        out_ref[i] = hid


def project(info, att, ws, residual, copies):
    nx, heads, rows, _ = att.shape
    tree = residual.shape[1]
    reqs = nx * rows // tree
    cols = ws[0].shape[2]
    return pl.pallas_call(
        project_kernel,
        out_shape=jax.ShapeDtypeStruct((copies, nx * rows, cols), BF),
        grid_spec=pltpu.PrefetchScalarGridSpec(
            num_scalar_prefetch=1,
            grid=(1,),
            in_specs=[pl.BlockSpec(att.shape, lambda g, i: (0, 0, 0, 0))]
            + [pl.BlockSpec(w.shape, lambda g, i: (0, 0, 0)) for w in ws]
            + [pl.BlockSpec((reqs, tree, cols), lambda g, i: (i[Z], 0, i[BLOCK]))],
            out_specs=pl.BlockSpec((copies, nx * rows, cols), lambda g, i: (0, 0, 0)),
        ),
        compiler_params=pltpu.CompilerParams(vmem_limit_bytes=48 * MB),
        name="project",
    )(info, att, *ws, pltpu.with_memory_space_constraint(residual, pltpu.HBM))


def shift_lanes(a, n):
    return jnp.concatenate([a[:, -n:], a[:, :-n]], axis=1)


def vocab_kernel(tree, chunks, info_ref, mine_ref, theirs_ref, gain_ref, tok_ref, par_ref, w_ref, hid_ref, stat_ref, x_ref, wbuf_ref, sem):
    copies = []
    for i, (start, size) in enumerate(chunks):
        cp = pltpu.make_async_copy(w_ref.at[:, pl.ds(start, size)], wbuf_ref.at[:, pl.ds(start, size)], sem.at[i])
        cp.start()
        copies.append(cp)
    core = info_ref[CORE]
    nz, nx, rows, cols = mine_ref.shape
    half = nx * cols
    for z in range(nz):
        rs = slice(z * rows, (z + 1) * rows)
        squares = jnp.zeros((rows, cols), F32)
        for x in range(nx):
            mine, theirs = mine_ref[z, x], theirs_ref[z, x]
            low = jnp.where(core == 0, mine, theirs)
            high = jnp.where(core == 0, theirs, mine)
            hid_ref[rs, x * cols:(x + 1) * cols] = low
            hid_ref[rs, half + x * cols:half + (x + 1) * cols] = high
            squares = squares + low.astype(F32) * low.astype(F32) + high.astype(F32) * high.astype(F32)
        inv = lax.rsqrt(jnp.sum(squares, axis=1, keepdims=True) / (2 * half) + 1e-06)
        for j in range(2 * nx):
            cs = slice(j * cols, (j + 1) * cols)
            x_ref[rs, cs] = (hid_ref[rs, cs].astype(F32) * inv * gain_ref[:, cs]).astype(BF)
    tokens = nz * rows
    reqs = tokens // tree
    sums = jnp.zeros((tokens, 128), F32)
    pick1 = jnp.zeros((tokens, 128), F32)
    pick2 = jnp.zeros((tokens, 128), F32)
    pick0 = [jnp.zeros((8, 128), F32) for _ in range(reqs)]
    lane = lax.broadcasted_iota(jnp.int32, (tokens, 128), 1)
    base = info_ref[BASE]
    tok = jnp.concatenate([tok_ref[...].astype(F32), jnp.full((reqs, 128 - tree), -1.0, F32)], axis=1)
    tok = jnp.transpose(tok)
    column = lambda n: jnp.concatenate([tok[n:n + tree, r:r + 1] for r in range(reqs)], axis=0).astype(jnp.int32)
    t1 = column(1) - base - lane
    t2 = column(2) - base - lane
    node = lax.broadcasted_iota(jnp.int32, (8, 128), 0)
    t0 = [jnp.where(node == 0, tok[0:8, r:r + 1].astype(jnp.int32) - base - lane[:8], -1) for r in range(reqs)]
    for (start, size), cp in zip(chunks, copies):
        cp.wait()
        for at in range(start, start + size, 256):
            step = min(256, start + size - at)
            logits = jnp.dot(x_ref[...], wbuf_ref[:, at:at + step], preferred_element_type=F32)
            for o in range(0, step, 128):
                lg = logits[:, o:o + 128]
                sums = sums + jnp.exp(lg)
                pick1 = jnp.where(t1 == at + o, lg, pick1)
                pick2 = jnp.where(t2 == at + o, lg, pick2)
                for r in range(reqs):
                    pick0[r] = jnp.where(t0[r] == at + o, lg[r * tree:r * tree + 8], pick0[r])
    zero = jnp.zeros((tree - 8, 128), F32)
    pick0 = jnp.concatenate([p for r in range(reqs) for p in (pick0[r], zero)], axis=0)
    total, pick1, pick2, pick0 = (
        jnp.sum(jnp.transpose(a), axis=0, keepdims=True) for a in (sums, pick1, pick2, pick0)
    )
    at_node = lax.broadcasted_iota(jnp.int32, (1, tokens), 1) % tree
    near = par_ref[...] == at_node - 1
    root = at_node == 0
    pick = jnp.where(root, pick0, jnp.where(near, shift_lanes(pick1, 1), shift_lanes(pick2, 2)))
    total = jnp.where(root, total, jnp.where(near, shift_lanes(total, 1), shift_lanes(total, 2)))
    groups = tokens // 128
    stats = [a[:, g * 128:(g + 1) * 128] for a in (total, pick) for g in range(groups)]
    stats = jnp.concatenate(stats + [jnp.zeros((8 - 2 * groups, 128), F32)], axis=0)
    for i in range(stat_ref.shape[0]):
        stat_ref[i] = stats


def vocab(info, mine, theirs, gain, toks, parents, w, copies):
    tree = toks.shape[1]
    nz, nx, rows, cols = mine.shape
    tokens, width, size = nz * rows, 2 * nx * cols, w.shape[1]
    chunks = []
    at = 0
    while at < size:
        step = min(512, size - at)
        chunks.append((at, step))
        at += step
    vm = pl.BlockSpec(memory_space=pltpu.VMEM)
    return pl.pallas_call(
        functools.partial(vocab_kernel, tree, tuple(chunks)),
        out_shape=(
            jax.ShapeDtypeStruct((tokens, width), BF),
            jax.ShapeDtypeStruct((copies, 8, 128), F32),
        ),
        in_specs=[pl.BlockSpec(memory_space=pltpu.SMEM), vm, vm, vm, vm, vm, pl.BlockSpec(memory_space=pl.ANY)],
        out_specs=(vm, vm),
        scratch_shapes=[
            pltpu.VMEM((tokens, width), BF),
            pltpu.VMEM((width, size), BF),
            pltpu.SemaphoreType.DMA((len(chunks),)),
        ],
        compiler_params=pltpu.CompilerParams(vmem_limit_bytes=56 * MB),
        name="vocab",
    )(info, mine, theirs, gain, toks, parents.reshape(1, -1), w)


def shifted(a, axis, step):
    n = lax.axis_size(axis)
    return lax.ppermute(a, axis, [(i, (i + step) % n) for i in range(n)])


def local(
    queries, new_keys, new_values, cache_keys, cache_values, lengths, parents,
    tree_tokens, residual, out_weight, norm_gain, vocab_weight,
):
    reqs, tree, width = queries.shape
    slots = cache_keys.shape[1]
    y, z, x, core = (lax.axis_index(a) for a in ("dp", "z", "x", "core"))
    ny, nz, nx, nc = (lax.axis_size(a) for a in ("dp", "z", "x", "core"))
    shard = (z * nx + x) * nc + core
    shards = nz * nx * nc
    window = slots * shards // 2
    half = width // nc
    block = half // nx
    tokens = reqs * tree
    swap = [(0, 1), (1, 0)]
    treq = jnp.where((shard >= reqs) & (shard < 2 * reqs), shard - reqs, -1)
    info = jnp.stack([core, shard * slots, treq, z, core * nx + x, y, shard * vocab_weight.shape[1]]).astype(jnp.int32)

    w = out_weight.reshape(-1, nc, nx, block).transpose(2, 1, 0, 3).reshape(nx * nc, -1, block)
    w = lax.all_to_all(w, ("x", "core"), 0, 0).reshape(-1, block)
    w = jnp.stack([w] + [shifted(w, "z", s) for s in range(1, nz)])
    ws = [w] + [shifted(w, "dp", s) for s in range(1, ny)]

    args = (lengths, parents, queries, cache_keys, cache_values, new_keys, new_values)
    send = attend_half(window, False, info, *args)
    got = lax.ppermute(send, "core", swap)
    keep = attend_half(window, True, info, *args)
    part = (keep + got).reshape(nz * nx, tokens // (nz * nx), half + 128)
    part = lax.all_to_all(part, ("z", "x"), 0, 0)
    att = combine(part, nx * nc)
    att = lax.all_to_all(att, ("x", "core"), 0, 0).reshape(nx, HEADS, -1, 128)
    hid = project(info, att, ws, residual, nz * nx)
    hid = lax.all_to_all(hid, ("z", "x"), 0, 0).reshape(nz, nx, -1, block)
    other = lax.ppermute(hid, "core", swap)
    hidden, stats = vocab(info, hid, other, norm_gain.reshape(1, -1), tree_tokens, parents, vocab_weight, shards)
    stats = jnp.sum(lax.all_to_all(stats, ("z", "x", "core"), 0, 0), axis=0)
    rows = tokens // 128
    logprob = stats[rows:2 * rows] - jnp.log(stats[:rows])
    return hidden.reshape(reqs, tree, width), logprob.reshape(reqs, tree)


def solution(mesh):
    sizes = (mesh.shape["dp"], 4, 4, 2)
    grid = Mesh(mesh.devices.reshape(sizes), ("dp", "z", "x", "core"))
    mp = ("z", "x", "core")
    row = P("dp", None, None)
    placed = (
        row, row, row, P("dp", mp, None), P("dp", mp, None), P("dp"), P("dp", None), P("dp", None), row,
        P(("dp",) + mp, None), P(), P(None, mp),
    )
    return jax.shard_map(local, mesh=grid, in_specs=placed, out_specs=(row, P("dp", None)), check_vma=False)
```

```python
import functools

import jax
import jax.numpy as jnp
from jax import lax
from jax.experimental import pallas as pl
from jax.experimental.pallas import tpu as pltpu
from jax.sharding import Mesh, PartitionSpec as P

HEADS = 16
SINK = 4
BF = jnp.bfloat16
F32 = jnp.float32
NT = (((1,), (1,)), ((), ()))
TN = (((0,), (0,)), ((), ()))
CORE, FIRST, TREQ, Z, X, BLOCK, DP, BASE = range(8)
MB = 1 << 20


def attend_kernel(window, lane_off, info_ref, len_ref, par_ref, q_ref, k_ref, v_ref, nk_ref, nv_ref, *refs):
    step = pl.program_id(0)
    if len(refs) == 4:
        w_ref, out_ref, spread_ref, anc_ref = refs
        nz, nx, nc, _, block = spread_ref.shape

        @pl.when(step == 0)
        def _():
            for c in range(nc):
                for x in range(nx):
                    at = (c * nx + x) * block
                    for z in range(nz):
                        spread_ref[z, x, c] = w_ref[:, at:at + block]
    else:
        out_ref, anc_ref = refs
    first = info_ref[FIRST]
    treq = info_ref[TREQ]
    reqs, tree, width = q_ref.shape
    slots = k_ref.shape[1]
    heads = width // 128
    scale = 128 ** (-0.5) * 1.4426950408889634

    def attend(r, keys, values, mask):
        dens = []
        scores = [
            lax.dot_general(keys(h), q_ref[r, :, h * 128:(h + 1) * 128], NT, preferred_element_type=F32)
            for h in range(heads)
        ]
        exps = [jnp.where(mask, jnp.exp2(s * scale), 0.0) for s in scores]
        for h in range(heads):
            dens.append(jnp.sum(exps[h], axis=0, keepdims=True))
            o = lax.dot_general(exps[h].astype(BF), values(h), TN, preferred_element_type=F32)
            out_ref[r, :, h * 128:(h + 1) * 128] = o.astype(BF)
        dens = jnp.concatenate(dens, axis=0)
        high = dens.astype(BF).astype(F32)
        pieces = [high, dens - high, jnp.zeros((128 - lane_off - 2 * heads, tree), F32)]
        if lane_off:
            pieces = [jnp.zeros((lane_off, tree), F32)] + pieces
        out_ref[r, :, width:] = jnp.transpose(jnp.concatenate(pieces, axis=0)).astype(BF)

    @pl.when(treq < 0)
    def _():
        pos = first + lax.broadcasted_iota(jnp.int32, (slots, tree), 0)
        for r in range(reqs):
            length = len_ref[step * reqs + r]
            mask = (pos < length) & ((pos < SINK) | (pos >= length - window))
            attend(
                r, lambda h: k_ref[r, :, h * 128:(h + 1) * 128], lambda h: v_ref[r, :, h * 128:(h + 1) * 128], mask
            )

    @pl.when(treq >= 0)
    def _():
        out_ref[...] = jnp.zeros_like(out_ref)

        @pl.when(treq // reqs == step)
        def _():
            node = lax.broadcasted_iota(jnp.int32, (1, 128), 1)
            anc_ref[...] = jnp.zeros_like(anc_ref)
            anc_ref[0:1, :] = jnp.where(node == 0, 1.0, 0.0)

            def body(i, carry):
                up = anc_ref[pl.ds(par_ref[treq, i], 1), :]
                anc_ref[pl.ds(i, 1), :] = jnp.where(node == i, 1.0, up)
                return carry

            lax.fori_loop(1, tree, body, 0)
            mask = jnp.transpose(anc_ref[...])[:tree, :tree] > 0.5
            attend(
                lax.rem(treq, reqs), lambda h: nk_ref[0, :, h * 128:(h + 1) * 128],
                lambda h: nv_ref[0, :, h * 128:(h + 1) * 128], mask,
            )


def attend_half(window, mine, info, lengths, parents, q, k, v, nk, nv, w=None, spread=None):
    reqs, tree, width = q.shape
    slots = k.shape[1]
    half = width // 2
    group = reqs // 2
    hidx = (lambda i: i[CORE]) if mine else (lambda i: 1 - i[CORE])
    qs = pl.BlockSpec((group, tree, half), lambda r, i, l, p: (r, 0, hidx(i)))
    ks = pl.BlockSpec((group, slots, half), lambda r, i, l, p: (r, 0, hidx(i)))
    ns = pl.BlockSpec((1, tree, half), lambda r, i, l, p: (jnp.clip(i[TREQ], 0, reqs - 1), 0, hidx(i)))
    lengths, parents, q, k, v, nk, nv = (
        pltpu.with_memory_space_constraint(a, pltpu.HBM) for a in (lengths, parents, q, k, v, nk, nv)
    )
    in_specs = [qs, ks, ks, ns, ns]
    out_specs = [pl.BlockSpec((group, tree, half + 128), lambda r, i, l, p: (r, 0, 0))]
    out_shape = [jax.ShapeDtypeStruct((reqs, tree, half + 128), BF)]
    extra = ()
    if w is not None:
        extra = (pltpu.with_memory_space_constraint(w, pltpu.HBM),)
        in_specs.append(pl.BlockSpec(w.shape, lambda r, i, l, p: (0, 0)))
        out_specs.append(pl.BlockSpec(spread, lambda r, i, l, p: (0, 0, 0, 0, 0)))
        out_shape.append(jax.ShapeDtypeStruct(spread, w.dtype))
    return pl.pallas_call(
        functools.partial(attend_kernel, window, 16 if mine else 0),
        out_shape=out_shape,
        grid_spec=pltpu.PrefetchScalarGridSpec(
            num_scalar_prefetch=3,
            grid=(reqs // group,),
            in_specs=in_specs,
            out_specs=out_specs,
            scratch_shapes=[pltpu.VMEM((128, 128), F32)],
        ),
        compiler_params=pltpu.CompilerParams(vmem_limit_bytes=16 * MB),
        name="attend_mine" if mine else "attend_theirs",
    )(info, lengths, parents, q, k, v, nk, nv, *extra)


def combine_kernel(parts_ref, out_ref):
    width = out_ref.shape[1]
    heads = width // 128
    total = jnp.sum(parts_ref[...].astype(F32), axis=0)
    den = total[:, width:]
    lane = lax.broadcasted_iota(jnp.int32, den.shape, 1)
    for h in range(heads):
        d = jnp.sum(jnp.where((lane % heads == h) & (lane < 4 * heads), den, 0.0), axis=1, keepdims=True)
        cols = slice(h * 128, (h + 1) * 128)
        out_ref[:, cols] = (total[:, cols] / d).astype(BF)


def combine(parts):
    rows, cols = parts.shape[1], parts.shape[2]
    return pl.pallas_call(
        combine_kernel,
        out_shape=jax.ShapeDtypeStruct((rows, cols - 128), BF),
        compiler_params=pltpu.CompilerParams(vmem_limit_bytes=16 * MB),
        name="combine",
    )(parts)


def project_kernel(nx, info_ref, *refs):
    own, other = refs[:nx], refs[nx:2 * nx]
    ws, (res_ref, _, out_ref) = refs[2 * nx:-3], refs[-3:]
    core, x, y = info_ref[CORE], info_ref[X], info_ref[DP]
    rows, half = own[0].shape
    ny, deep = len(ws), ws[0].shape[0]
    mine = jnp.concatenate([own[s][...] for s in range(nx)], axis=0)
    theirs = jnp.concatenate([other[s][...] for s in range(nx)], axis=0)
    acc = None
    for s in range(ny):
        at = lax.rem(y + ny - s, ny)
        a = jnp.where(core == at // 2, mine, theirs)
        a = jnp.where(at % 2 == 0, a[:, :deep], a[:, deep:])
        part = jnp.dot(a, ws[s][...], preferred_element_type=F32)
        acc = part if acc is None else acc + part
    for s in range(nx):
        at = lax.rem(x + nx - s, nx)
        hid = (res_ref[at].astype(F32) + acc[s * rows:(s + 1) * rows]).astype(BF)
        for i in range(out_ref.shape[0]):
            out_ref[i, at] = hid


def project(info, own, other, ws, residual, after, copies):
    nx = len(own)
    rows, half = own[0].shape
    cols = ws[0].shape[1]
    part = pl.BlockSpec((rows, half), lambda g, i: (0, 0))
    residual = pltpu.with_memory_space_constraint(residual.reshape(-1, rows, residual.shape[2]), pltpu.HBM)
    return pl.pallas_call(
        functools.partial(project_kernel, nx),
        out_shape=jax.ShapeDtypeStruct((copies, nx, rows, cols), BF),
        grid_spec=pltpu.PrefetchScalarGridSpec(
            num_scalar_prefetch=1,
            grid=(1,),
            in_specs=[part] * (2 * nx)
            + [pl.BlockSpec(w.shape, lambda g, i: (0, 0)) for w in ws]
            + [pl.BlockSpec((nx, rows, cols), lambda g, i: (i[Z], 0, i[BLOCK]))]
            + [pl.BlockSpec(memory_space=pl.ANY)],
            out_specs=pl.BlockSpec((copies, nx, rows, cols), lambda g, i: (0, 0, 0, 0)),
        ),
        compiler_params=pltpu.CompilerParams(vmem_limit_bytes=16 * MB),
        name="project",
    )(info, *own, *other, *ws, residual, after)


def vocab_kernel(info_ref, mine_ref, theirs_ref, gain_ref, tok_ref, par_ref, w_ref, hid_out, stat_ref, hid_ref, x_ref, sem):
    core = info_ref[CORE]
    nz, nx, rows, cols = mine_ref.shape
    half = nx * cols
    for z in range(nz):
        rs = slice(z * rows, (z + 1) * rows)
        squares = jnp.zeros((rows, cols), F32)
        for x in range(nx):
            mine, theirs = mine_ref[z, x], theirs_ref[z, x]
            low = jnp.where(core == 0, mine, theirs)
            high = jnp.where(core == 0, theirs, mine)
            hid_ref[rs, x * cols:(x + 1) * cols] = low
            hid_ref[rs, half + x * cols:half + (x + 1) * cols] = high
            squares = squares + low.astype(F32) * low.astype(F32) + high.astype(F32) * high.astype(F32)
        inv = lax.rsqrt(jnp.sum(squares, axis=1, keepdims=True) / (2 * half) + 1e-06)
        for j in range(2 * nx):
            cs = slice(j * cols, (j + 1) * cols)
            x_ref[rs, cs] = (hid_ref[rs, cs].astype(F32) * inv * gain_ref[:, cs]).astype(BF)
    copy = pltpu.make_async_copy(hid_ref, hid_out, sem)
    copy.start()
    tokens = nz * rows
    reqs, tree = tok_ref.shape
    size = w_ref.shape[1]
    sums = jnp.zeros((tokens, 128), F32)
    pick1 = jnp.zeros((tokens, 128), F32)
    pick2 = jnp.zeros((tokens, 128), F32)
    pick0 = [jnp.zeros((8, 128), F32) for _ in range(reqs)]
    lane = lax.broadcasted_iota(jnp.int32, (tokens, 128), 1)
    base = info_ref[BASE]
    tok = jnp.concatenate([tok_ref[...].astype(F32), jnp.full((reqs, 128 - tree), -1.0, F32)], axis=1)
    tok = jnp.transpose(tok)
    column = lambda n: jnp.concatenate([tok[n:n + tree, r:r + 1] for r in range(reqs)], axis=0).astype(jnp.int32)
    t1 = column(1) - base - lane
    t2 = column(2) - base - lane
    node = lax.broadcasted_iota(jnp.int32, (8, 128), 0)
    t0 = [jnp.where(node == 0, tok[0:8, r:r + 1].astype(jnp.int32) - base - lane[:8], -1) for r in range(reqs)]
    for at in range(0, size, 256):
        step = min(256, size - at)
        logits = jnp.dot(x_ref[...], w_ref[:, at:at + step], preferred_element_type=F32)
        for o in range(0, step, 128):
            lg = logits[:, o:o + 128]
            sums = sums + jnp.exp(lg)
            pick1 = jnp.where(t1 == at + o, lg, pick1)
            pick2 = jnp.where(t2 == at + o, lg, pick2)
            for r in range(reqs):
                pick0[r] = jnp.where(t0[r] == at + o, lg[r * tree:r * tree + 8], pick0[r])
    zero = jnp.zeros((tree - 8, 128), F32)
    pick0 = jnp.concatenate([p for r in range(reqs) for p in (pick0[r], zero)], axis=0)

    def by_request(a):
        a = jnp.sum(jnp.transpose(a), axis=0, keepdims=True)
        return jnp.concatenate([a[:, r * tree:(r + 1) * tree] for r in range(reqs)], axis=0)

    def later(a, n):
        return jnp.concatenate([a[:, :n], a[:, :tree - n]], axis=1)

    total, pick1, pick2, pick0 = (by_request(a) for a in (sums, pick1, pick2, pick0))
    at_node = lax.broadcasted_iota(jnp.int32, (reqs, tree), 1)
    near = par_ref[...] == at_node - 1
    root = at_node == 0
    pick = jnp.where(root, pick0, jnp.where(near, later(pick1, 1), later(pick2, 2)))
    total = jnp.where(root, total, jnp.where(near, later(total, 1), later(total, 2)))
    gap = jnp.zeros((reqs, 64 - tree), F32)
    stats = jnp.concatenate([total, gap, pick, gap], axis=1)
    for i in range(stat_ref.shape[0]):
        stat_ref[i] = stats
    copy.wait()


def vocab(info, mine, theirs, gain, toks, parents, w, copies):
    nz, nx, rows, cols = mine.shape
    tokens, width = nz * rows, 2 * nx * cols
    vm = pl.BlockSpec(memory_space=pltpu.VMEM)
    return pl.pallas_call(
        vocab_kernel,
        out_shape=(
            jax.ShapeDtypeStruct((tokens, width), BF),
            jax.ShapeDtypeStruct((copies, toks.shape[0], 128), F32),
        ),
        in_specs=[pl.BlockSpec(memory_space=pltpu.SMEM), vm, vm, vm, vm, vm, vm],
        out_specs=(pl.BlockSpec(memory_space=pl.ANY), vm),
        scratch_shapes=[pltpu.VMEM((tokens, width), BF), pltpu.VMEM((tokens, width), BF), pltpu.SemaphoreType.DMA],
        compiler_params=pltpu.CompilerParams(vmem_limit_bytes=24 * MB),
        name="vocab",
    )(info, mine, theirs, gain, toks, parents, w)


def fetch_kernel(w_ref, after_ref, out_ref, sem):
    copy = pltpu.make_async_copy(w_ref, out_ref, sem)
    copy.start()
    copy.wait()


def fetch(w, after):
    hbm = pl.BlockSpec(memory_space=pl.ANY)
    return pl.pallas_call(
        fetch_kernel,
        out_shape=jax.ShapeDtypeStruct(w.shape, w.dtype),
        in_specs=[hbm, hbm],
        out_specs=pl.BlockSpec(memory_space=pltpu.VMEM),
        scratch_shapes=[pltpu.SemaphoreType.DMA],
        compiler_params=pltpu.CompilerParams(vmem_limit_bytes=2 * MB),
        name="fetch",
    )(pltpu.with_memory_space_constraint(w, pltpu.HBM), after)


def shifted(a, axis, step):
    n = lax.axis_size(axis)
    return lax.ppermute(a, axis, [(i, (i + step) % n) for i in range(n)])


def local(
    queries, new_keys, new_values, cache_keys, cache_values, lengths, parents,
    tree_tokens, residual, out_weight, norm_gain, vocab_weight,
):
    reqs, tree, width = queries.shape
    slots = cache_keys.shape[1]
    y, z, x, core = (lax.axis_index(a) for a in ("dp", "z", "x", "core"))
    ny, nz, nx, nc = (lax.axis_size(a) for a in ("dp", "z", "x", "core"))
    shard = (z * nx + x) * nc + core
    shards = nz * nx * nc
    window = slots * shards // 2
    half = width // nc
    block = half // nx
    tokens = reqs * tree
    swap = [(0, 1), (1, 0)]
    treq = jnp.where((shard >= reqs) & (shard < 2 * reqs), shard - reqs, -1)
    info = jnp.stack([core, shard * slots, treq, z, x, core * nx + x, y, shard * vocab_weight.shape[1]]).astype(jnp.int32)

    args = (lengths, parents, queries, cache_keys, cache_values, new_keys, new_values)
    send, w = attend_half(window, False, info, *args, out_weight, (nz, nx, nc, out_weight.shape[0], block))
    got = lax.ppermute(send, "core", swap)
    w = lax.all_to_all(w.reshape(shards, -1, block), ("z", "x", "core"), 0, 0).reshape(-1, block)
    ws = [w] + [shifted(w, "dp", s) for s in range(1, ny)]
    (keep,) = attend_half(window, True, info, *args)
    part = (keep + got).reshape(nz * nx, tokens // (nz * nx), half + 128)
    part = lax.all_to_all(part, ("z", "x"), 0, 0)
    att = combine(part)
    own = [att] + [shifted(att, "x", s) for s in range(1, nx)]
    other = [lax.ppermute(a, "core", swap) for a in own]
    scorer = fetch(vocab_weight, att)
    hid = project(info, own, other, ws, residual, scorer, nz * nx).reshape(nz * nx, -1, block)
    hid = lax.all_to_all(hid, ("z", "x"), 0, 0).reshape(nz, nx, -1, block)
    other = lax.ppermute(hid, "core", swap)
    hidden, stats = vocab(info, hid, other, norm_gain.reshape(1, -1), tree_tokens, parents, scorer, shards)
    stats = jnp.sum(lax.all_to_all(stats, ("z", "x", "core"), 0, 0), axis=0)
    logprob = stats[:, 64:64 + tree] - jnp.log(stats[:, :tree])
    return hidden.reshape(reqs, tree, width), logprob


def solution(mesh):
    sizes = (mesh.shape["dp"], 4, 4, 2)
    grid = Mesh(mesh.devices.reshape(sizes), ("dp", "z", "x", "core"))
    mp = ("z", "x", "core")
    row = P("dp", None, None)
    placed = (
        row, row, row, P("dp", mp, None), P("dp", mp, None), P("dp"), P("dp", None), P("dp", None), row,
        P(("dp",) + mp, None), P(), P(None, mp),
    )
    return jax.shard_map(local, mesh=grid, in_specs=placed, out_specs=(row, P("dp", None)), check_vma=False)
```

```python
import functools

import jax
import jax.numpy as jnp
from jax import lax
from jax.experimental import pallas as pl
from jax.experimental.pallas import tpu as pltpu
from jax.sharding import Mesh, PartitionSpec as P

HEADS = 16
SINK = 4
BF = jnp.bfloat16
F32 = jnp.float32
NT = (((1,), (1,)), ((), ()))
TN = (((0,), (0,)), ((), ()))
CORE, FIRST, TREQ, Z, X, BLOCK, DP, BASE = range(8)
MB = 1 << 20


def attend_kernel(window, lane_off, info_ref, len_ref, par_ref, q_ref, k_ref, v_ref, nk_ref, nv_ref, *refs):
    step = pl.program_id(0)
    if len(refs) == 4:
        w_ref, out_ref, spread_ref, anc_ref = refs
        nz, nx, nc, _, block = spread_ref.shape

        @pl.when(step == 0)
        def _():
            for c in range(nc):
                for x in range(nx):
                    at = (c * nx + x) * block
                    for z in range(nz):
                        spread_ref[z, x, c] = w_ref[:, at:at + block]
    else:
        out_ref, anc_ref = refs
    first = info_ref[FIRST]
    treq = info_ref[TREQ]
    reqs, tree, width = q_ref.shape
    slots = k_ref.shape[1]
    heads = width // 128
    scale = 128 ** (-0.5) * 1.4426950408889634

    def attend(r, keys, values, mask):
        dens = []
        scores = [
            lax.dot_general(keys(h), q_ref[r, :, h * 128:(h + 1) * 128], NT, preferred_element_type=F32)
            for h in range(heads)
        ]
        exps = [jnp.where(mask, jnp.exp2(s * scale), 0.0) for s in scores]
        for h in range(heads):
            dens.append(jnp.sum(exps[h], axis=0, keepdims=True))
            o = lax.dot_general(exps[h].astype(BF), values(h), TN, preferred_element_type=F32)
            out_ref[r, :, h * 128:(h + 1) * 128] = o.astype(BF)
        dens = jnp.concatenate(dens, axis=0)
        high = dens.astype(BF).astype(F32)
        pieces = [high, dens - high, jnp.zeros((128 - lane_off - 2 * heads, tree), F32)]
        if lane_off:
            pieces = [jnp.zeros((lane_off, tree), F32)] + pieces
        out_ref[r, :, width:] = jnp.transpose(jnp.concatenate(pieces, axis=0)).astype(BF)

    @pl.when(treq < 0)
    def _():
        pos = first + lax.broadcasted_iota(jnp.int32, (slots, tree), 0)
        for r in range(reqs):
            length = len_ref[step * reqs + r]
            mask = (pos < length) & ((pos < SINK) | (pos >= length - window))
            attend(
                r, lambda h: k_ref[r, :, h * 128:(h + 1) * 128], lambda h: v_ref[r, :, h * 128:(h + 1) * 128], mask
            )

    @pl.when(treq >= 0)
    def _():
        out_ref[...] = jnp.zeros_like(out_ref)

        @pl.when(treq // reqs == step)
        def _():
            node = lax.broadcasted_iota(jnp.int32, (1, 128), 1)
            anc_ref[...] = jnp.zeros_like(anc_ref)
            anc_ref[0:1, :] = jnp.where(node == 0, 1.0, 0.0)

            def body(i, carry):
                up = anc_ref[pl.ds(par_ref[treq, i], 1), :]
                anc_ref[pl.ds(i, 1), :] = jnp.where(node == i, 1.0, up)
                return carry

            lax.fori_loop(1, tree, body, 0)
            mask = jnp.transpose(anc_ref[...])[:tree, :tree] > 0.5
            attend(
                lax.rem(treq, reqs), lambda h: nk_ref[0, :, h * 128:(h + 1) * 128],
                lambda h: nv_ref[0, :, h * 128:(h + 1) * 128], mask,
            )


def attend_half(window, mine, info, lengths, parents, q, k, v, nk, nv, w=None, spread=None):
    reqs, tree, width = q.shape
    slots = k.shape[1]
    half = width // 2
    group = reqs // 2
    hidx = (lambda i: i[CORE]) if mine else (lambda i: 1 - i[CORE])
    qs = pl.BlockSpec((group, tree, half), lambda r, i, l, p: (r, 0, hidx(i)))
    ks = pl.BlockSpec((group, slots, half), lambda r, i, l, p: (r, 0, hidx(i)))
    ns = pl.BlockSpec((1, tree, half), lambda r, i, l, p: (jnp.clip(i[TREQ], 0, reqs - 1), 0, hidx(i)))
    lengths, parents, q, k, v, nk, nv = (
        pltpu.with_memory_space_constraint(a, pltpu.HBM) for a in (lengths, parents, q, k, v, nk, nv)
    )
    in_specs = [qs, ks, ks, ns, ns]
    out_specs = [pl.BlockSpec((group, tree, half + 128), lambda r, i, l, p: (r, 0, 0))]
    out_shape = [jax.ShapeDtypeStruct((reqs, tree, half + 128), BF)]
    extra = ()
    if w is not None:
        extra = (pltpu.with_memory_space_constraint(w, pltpu.HBM),)
        in_specs.append(pl.BlockSpec(w.shape, lambda r, i, l, p: (0, 0)))
        out_specs.append(pl.BlockSpec(spread, lambda r, i, l, p: (0, 0, 0, 0, 0)))
        out_shape.append(jax.ShapeDtypeStruct(spread, w.dtype))
    return pl.pallas_call(
        functools.partial(attend_kernel, window, 16 if mine else 0),
        out_shape=out_shape,
        grid_spec=pltpu.PrefetchScalarGridSpec(
            num_scalar_prefetch=3,
            grid=(reqs // group,),
            in_specs=in_specs,
            out_specs=out_specs,
            scratch_shapes=[pltpu.VMEM((128, 128), F32)],
        ),
        compiler_params=pltpu.CompilerParams(vmem_limit_bytes=16 * MB),
        name="attend_mine" if mine else "attend_theirs",
    )(info, lengths, parents, q, k, v, nk, nv, *extra)


def combine_kernel(parts_ref, out_ref):
    width = out_ref.shape[1]
    heads = width // 128
    total = jnp.sum(parts_ref[...].astype(F32), axis=0)
    den = total[:, width:]
    lane = lax.broadcasted_iota(jnp.int32, den.shape, 1)
    for h in range(heads):
        d = jnp.sum(jnp.where((lane % heads == h) & (lane < 4 * heads), den, 0.0), axis=1, keepdims=True)
        cols = slice(h * 128, (h + 1) * 128)
        out_ref[:, cols] = (total[:, cols] / d).astype(BF)


def combine(parts):
    rows, cols = parts.shape[1], parts.shape[2]
    return pl.pallas_call(
        combine_kernel,
        out_shape=jax.ShapeDtypeStruct((rows, cols - 128), BF),
        compiler_params=pltpu.CompilerParams(vmem_limit_bytes=16 * MB),
        name="combine",
    )(parts)


def project_kernel(nx, info_ref, *refs):
    own, other = refs[:nx], refs[nx:2 * nx]
    ws, (res_ref, out_ref) = refs[2 * nx:-2], refs[-2:]
    core, x, y = info_ref[CORE], info_ref[X], info_ref[DP]
    rows, half = own[0].shape
    ny, deep = len(ws), ws[0].shape[0]
    mine = jnp.concatenate([own[s][...] for s in range(nx)], axis=0)
    theirs = jnp.concatenate([other[s][...] for s in range(nx)], axis=0)
    acc = None
    for s in range(ny):
        at = lax.rem(y + ny - s, ny)
        a = jnp.where(core == at // 2, mine, theirs)
        a = jnp.where(at % 2 == 0, a[:, :deep], a[:, deep:])
        part = jnp.dot(a, ws[s][...], preferred_element_type=F32)
        acc = part if acc is None else acc + part
    for s in range(nx):
        at = lax.rem(x + nx - s, nx)
        hid = (res_ref[at].astype(F32) + acc[s * rows:(s + 1) * rows]).astype(BF)
        for i in range(out_ref.shape[0]):
            out_ref[i, at] = hid


def project(info, own, other, ws, residual, copies):
    nx = len(own)
    rows, half = own[0].shape
    cols = ws[0].shape[1]
    part = pl.BlockSpec((rows, half), lambda g, i: (0, 0))
    residual = pltpu.with_memory_space_constraint(residual.reshape(-1, rows, residual.shape[2]), pltpu.HBM)
    return pl.pallas_call(
        functools.partial(project_kernel, nx),
        out_shape=jax.ShapeDtypeStruct((copies, nx, rows, cols), BF),
        grid_spec=pltpu.PrefetchScalarGridSpec(
            num_scalar_prefetch=1,
            grid=(1,),
            in_specs=[part] * (2 * nx)
            + [pl.BlockSpec(w.shape, lambda g, i: (0, 0)) for w in ws]
            + [pl.BlockSpec((nx, rows, cols), lambda g, i: (i[Z], 0, i[BLOCK]))],
            out_specs=pl.BlockSpec((copies, nx, rows, cols), lambda g, i: (0, 0, 0, 0)),
        ),
        compiler_params=pltpu.CompilerParams(vmem_limit_bytes=16 * MB),
        name="project",
    )(info, *own, *other, *ws, residual)


def vocab_kernel(
    info_ref, mine_ref, theirs_ref, gain_ref, tok_ref, par_ref, w_ref, more_ref, hid_out, stat_ref, hid_ref, x_ref, rest_ref, sem
):
    lead, others = w_ref.shape[1], rest_ref.shape[1]
    load = pltpu.make_async_copy(more_ref.at[:, pl.ds(lead, others)], rest_ref, sem.at[1])
    load.start()
    core = info_ref[CORE]
    nz, nx, rows, cols = mine_ref.shape
    half = nx * cols
    for z in range(nz):
        rs = slice(z * rows, (z + 1) * rows)
        squares = jnp.zeros((rows, cols), F32)
        for x in range(nx):
            mine, theirs = mine_ref[z, x], theirs_ref[z, x]
            low = jnp.where(core == 0, mine, theirs)
            high = jnp.where(core == 0, theirs, mine)
            hid_ref[rs, x * cols:(x + 1) * cols] = low
            hid_ref[rs, half + x * cols:half + (x + 1) * cols] = high
            squares = squares + low.astype(F32) * low.astype(F32) + high.astype(F32) * high.astype(F32)
        inv = lax.rsqrt(jnp.sum(squares, axis=1, keepdims=True) / (2 * half) + 1e-06)
        for j in range(2 * nx):
            cs = slice(j * cols, (j + 1) * cols)
            x_ref[rs, cs] = (hid_ref[rs, cs].astype(F32) * inv * gain_ref[:, cs]).astype(BF)
    copy = pltpu.make_async_copy(hid_ref, hid_out, sem.at[0])
    copy.start()
    tokens = nz * rows
    reqs, tree = tok_ref.shape
    sums = jnp.zeros((tokens, 128), F32)
    pick1 = jnp.zeros((tokens, 128), F32)
    pick2 = jnp.zeros((tokens, 128), F32)
    pick0 = [jnp.zeros((8, 128), F32) for _ in range(reqs)]
    lane = lax.broadcasted_iota(jnp.int32, (tokens, 128), 1)
    base = info_ref[BASE]
    tok = jnp.concatenate([tok_ref[...].astype(F32), jnp.full((reqs, 128 - tree), -1.0, F32)], axis=1)
    tok = jnp.transpose(tok)
    column = lambda n: jnp.concatenate([tok[n:n + tree, r:r + 1] for r in range(reqs)], axis=0).astype(jnp.int32)
    t1 = column(1) - base - lane
    t2 = column(2) - base - lane
    node = lax.broadcasted_iota(jnp.int32, (8, 128), 0)
    t0 = [jnp.where(node == 0, tok[0:8, r:r + 1].astype(jnp.int32) - base - lane[:8], -1) for r in range(reqs)]
    parts = [(w_ref, at, min(256, lead - at), at) for at in range(0, lead, 256)]
    parts += [(rest_ref, at, min(256, others - at), lead + at) for at in range(0, others, 256)]
    for ref, start, step, at in parts:
        if at == lead:
            load.wait()
        logits = jnp.dot(x_ref[...], ref[:, start:start + step], preferred_element_type=F32)
        for o in range(0, step, 128):
            lg = logits[:, o:o + 128]
            sums = sums + jnp.exp(lg)
            pick1 = jnp.where(t1 == at + o, lg, pick1)
            pick2 = jnp.where(t2 == at + o, lg, pick2)
            for r in range(reqs):
                pick0[r] = jnp.where(t0[r] == at + o, lg[r * tree:r * tree + 8], pick0[r])
    zero = jnp.zeros((tree - 8, 128), F32)
    pick0 = jnp.concatenate([p for r in range(reqs) for p in (pick0[r], zero)], axis=0)

    def by_request(a):
        a = jnp.sum(jnp.transpose(a), axis=0, keepdims=True)
        return jnp.concatenate([a[:, r * tree:(r + 1) * tree] for r in range(reqs)], axis=0)

    def later(a, n):
        return jnp.concatenate([a[:, :n], a[:, :tree - n]], axis=1)

    total, pick1, pick2, pick0 = (by_request(a) for a in (sums, pick1, pick2, pick0))
    at_node = lax.broadcasted_iota(jnp.int32, (reqs, tree), 1)
    near = par_ref[...] == at_node - 1
    root = at_node == 0
    pick = jnp.where(root, pick0, jnp.where(near, later(pick1, 1), later(pick2, 2)))
    total = jnp.where(root, total, jnp.where(near, later(total, 1), later(total, 2)))
    gap = jnp.zeros((reqs, 64 - tree), F32)
    stats = jnp.concatenate([total, gap, pick, gap], axis=1)
    for i in range(stat_ref.shape[0]):
        stat_ref[i] = stats
    copy.wait()


def vocab(info, mine, theirs, gain, toks, parents, lead, w, copies):
    nz, nx, rows, cols = mine.shape
    tokens, width = nz * rows, 2 * nx * cols
    vm = pl.BlockSpec(memory_space=pltpu.VMEM)
    return pl.pallas_call(
        vocab_kernel,
        out_shape=(
            jax.ShapeDtypeStruct((tokens, width), BF),
            jax.ShapeDtypeStruct((copies, toks.shape[0], 128), F32),
        ),
        in_specs=[pl.BlockSpec(memory_space=pltpu.SMEM), vm, vm, vm, vm, vm, vm, pl.BlockSpec(memory_space=pl.ANY)],
        out_specs=(pl.BlockSpec(memory_space=pl.ANY), vm),
        scratch_shapes=[
            pltpu.VMEM((tokens, width), BF),
            pltpu.VMEM((tokens, width), BF),
            pltpu.VMEM((width, w.shape[1] - lead.shape[1]), BF),
            pltpu.SemaphoreType.DMA((2,)),
        ],
        compiler_params=pltpu.CompilerParams(vmem_limit_bytes=24 * MB),
        name="vocab",
    )(info, mine, theirs, gain, toks, parents, lead, pltpu.with_memory_space_constraint(w, pltpu.HBM))


def fetch_kernel(w_ref, after_ref, out_ref, sem):
    copy = pltpu.make_async_copy(w_ref.at[:, pl.ds(0, out_ref.shape[1])], out_ref, sem)
    copy.start()
    copy.wait()


def fetch(w, after, cols):
    hbm = pl.BlockSpec(memory_space=pl.ANY)
    return pl.pallas_call(
        fetch_kernel,
        out_shape=jax.ShapeDtypeStruct((w.shape[0], cols), w.dtype),
        in_specs=[hbm, hbm],
        out_specs=pl.BlockSpec(memory_space=pltpu.VMEM),
        scratch_shapes=[pltpu.SemaphoreType.DMA],
        compiler_params=pltpu.CompilerParams(vmem_limit_bytes=2 * MB),
        name="fetch",
    )(pltpu.with_memory_space_constraint(w, pltpu.HBM), after)


def shifted(a, axis, step):
    n = lax.axis_size(axis)
    return lax.ppermute(a, axis, [(i, (i + step) % n) for i in range(n)])


def local(
    queries, new_keys, new_values, cache_keys, cache_values, lengths, parents,
    tree_tokens, residual, out_weight, norm_gain, vocab_weight,
):
    reqs, tree, width = queries.shape
    slots = cache_keys.shape[1]
    y, z, x, core = (lax.axis_index(a) for a in ("dp", "z", "x", "core"))
    ny, nz, nx, nc = (lax.axis_size(a) for a in ("dp", "z", "x", "core"))
    shard = (z * nx + x) * nc + core
    shards = nz * nx * nc
    window = slots * shards // 2
    half = width // nc
    block = half // nx
    tokens = reqs * tree
    swap = [(0, 1), (1, 0)]
    treq = jnp.where((shard >= reqs) & (shard < 2 * reqs), shard - reqs, -1)
    info = jnp.stack([core, shard * slots, treq, z, x, core * nx + x, y, shard * vocab_weight.shape[1]]).astype(jnp.int32)

    args = (lengths, parents, queries, cache_keys, cache_values, new_keys, new_values)
    send, w = attend_half(window, False, info, *args, out_weight, (nz, nx, nc, out_weight.shape[0], block))
    got = lax.ppermute(send, "core", swap)
    w = lax.all_to_all(w.reshape(shards, -1, block), ("z", "x", "core"), 0, 0).reshape(-1, block)
    ws = [w] + [shifted(w, "dp", s) for s in range(1, ny)]
    (keep,) = attend_half(window, True, info, *args)
    part = (keep + got).reshape(nz * nx, tokens // (nz * nx), half + 128)
    part = lax.all_to_all(part, ("z", "x"), 0, 0)
    att = combine(part)
    own = [att] + [shifted(att, "x", s) for s in range(1, nx)]
    other = [lax.ppermute(a, "core", swap) for a in own]
    hid = project(info, own, other, ws, residual, nz * nx).reshape(nz * nx, -1, block)
    hid = lax.all_to_all(hid, ("z", "x"), 0, 0).reshape(nz, nx, -1, block)
    other = lax.ppermute(hid, "core", swap)
    scorer = fetch(vocab_weight, hid, 1024)
    hidden, stats = vocab(info, hid, other, norm_gain.reshape(1, -1), tree_tokens, parents, scorer, vocab_weight, shards)
    stats = jnp.sum(lax.all_to_all(stats, ("z", "x", "core"), 0, 0), axis=0)
    logprob = stats[:, 64:64 + tree] - jnp.log(stats[:, :tree])
    return hidden.reshape(reqs, tree, width), logprob


def solution(mesh):
    sizes = (mesh.shape["dp"], 4, 4, 2)
    grid = Mesh(mesh.devices.reshape(sizes), ("dp", "z", "x", "core"))
    mp = ("z", "x", "core")
    row = P("dp", None, None)
    placed = (
        row, row, row, P("dp", mp, None), P("dp", mp, None), P("dp"), P("dp", None), P("dp", None), row,
        P(("dp",) + mp, None), P(), P(None, mp),
    )
    return jax.shard_map(local, mesh=grid, in_specs=placed, out_specs=(row, P("dp", None)), check_vma=False)
```

```python
import functools

import jax
import jax.numpy as jnp
from jax import lax
from jax.experimental import pallas as pl
from jax.experimental.pallas import tpu as pltpu
from jax.sharding import Mesh, PartitionSpec as P

HEADS = 16
SINK = 4
BF = jnp.bfloat16
F32 = jnp.float32
NT = (((1,), (1,)), ((), ()))
TN = (((0,), (0,)), ((), ()))
CORE, FIRST, TREQ, Z, X, BLOCK, DP, BASE = range(8)
MB = 1 << 20


def attend_kernel(window, add, info_ref, len_ref, par_ref, q_ref, k_ref, v_ref, nk_ref, nv_ref, *refs):
    step = pl.program_id(0)
    if add:
        got_ref, out_ref, anc_ref = refs
    else:
        w_ref, out_ref, spread_ref, anc_ref = refs
        nz, nx, nc, _, block = spread_ref.shape

        @pl.when(step == 0)
        def _():
            for c in range(nc):
                for x in range(nx):
                    at = (c * nx + x) * block
                    for z in range(nz):
                        spread_ref[z, x, c] = w_ref[:, at:at + block]

    first = info_ref[FIRST]
    treq = info_ref[TREQ]
    reqs, tree, width = q_ref.shape
    slots = k_ref.shape[1]
    heads = width // 128
    part = tree // 2
    scale = 128 ** (-0.5) * 1.4426950408889634
    zero = jnp.zeros((tree, 128), BF)
    pairs = [slice(p * 256, (p + 1) * 256) for p in range(heads // 2)]

    def score(r, keys):
        out = []
        for cols in pairs:
            q = q_ref[r, :, cols]
            q = jnp.concatenate(
                [jnp.concatenate([q[:, :128], zero], axis=1), jnp.concatenate([zero, q[:, 128:]], axis=1)], axis=0
            )
            out.append(lax.dot_general(keys(cols), q, NT, preferred_element_type=F32))
        return out

    def weigh(scores, mask):
        exps = [jnp.where(mask, jnp.exp2(s * scale), 0.0) for s in scores]
        dens = [jnp.sum(e, axis=0, keepdims=True) for e in exps]
        dens = [d[:, t * tree:(t + 1) * tree] for d in dens for t in range(2)]
        return [e.astype(BF) for e in exps], jnp.concatenate(dens, axis=0)

    def finish(r, exps, dens, values):
        for p, cols in enumerate(pairs):
            o = lax.dot_general(exps[p], values(cols), TN, preferred_element_type=F32)
            for h, val in ((2 * p, o[:tree, :128]), (2 * p + 1, o[tree:, 128:])):
                for t in range(2):
                    rows = slice(h * part, (h + 1) * part)
                    half = val[t * part:(t + 1) * part]
                    if add:
                        half = half + got_ref[2 * r + t, rows].astype(F32)
                    out_ref[2 * r + t, rows] = half.astype(BF)
        gap = jnp.zeros((heads, 64 - part), F32)
        for t in range(2):
            den = dens[:, t * part:(t + 1) * part]
            if add:
                got = got_ref[2 * r + t, heads * part:].astype(F32)
                den = den + got[:, :part] + got[:, 64:64 + part]
            high = den.astype(BF).astype(F32)
            out_ref[2 * r + t, heads * part:] = jnp.concatenate([high, gap, den - high, gap], axis=1).astype(BF)

    @pl.when(treq < 0)
    def _():
        pos = first + lax.broadcasted_iota(jnp.int32, (slots, 2 * tree), 0)
        scores = [score(r, lambda cols: k_ref[r, :, cols]) for r in range(reqs)]
        weights = []
        for r in range(reqs):
            length = len_ref[step * reqs + r]
            mask = (pos < length) & ((pos < SINK) | (pos >= length - window))
            weights.append(weigh(scores[r], mask))
        for r in range(reqs):
            finish(r, *weights[r], lambda cols: v_ref[r, :, cols])

    @pl.when(treq >= 0)
    def _():
        out_ref[...] = got_ref[...] if add else jnp.zeros_like(out_ref)

        @pl.when(treq // reqs == step)
        def _():
            node = lax.broadcasted_iota(jnp.int32, (1, 128), 1)
            anc_ref[...] = jnp.zeros_like(anc_ref)
            anc_ref[0:1, :] = jnp.where(node == 0, 1.0, 0.0)

            def body(i, carry):
                up = anc_ref[pl.ds(par_ref[treq, i], 1), :]
                anc_ref[pl.ds(i, 1), :] = jnp.where(node == i, 1.0, up)
                return carry

            lax.fori_loop(1, tree, body, 0)
            mask = jnp.transpose(anc_ref[...])[:tree, :tree]
            mask = jnp.concatenate([mask, mask], axis=1) > 0.5
            r = lax.rem(treq, reqs)
            weights = weigh(score(r, lambda cols: nk_ref[0, :, cols]), mask)
            finish(r, *weights, lambda cols: nv_ref[0, :, cols])


def attend_half(window, info, lengths, parents, q, k, v, nk, nv, got=None, w=None, spread=None):
    reqs, tree, width = q.shape
    slots = k.shape[1]
    half = width // 2
    group = reqs // 2
    add = got is not None
    hidx = (lambda i: i[CORE]) if add else (lambda i: 1 - i[CORE])
    qs = pl.BlockSpec((group, tree, half), lambda r, i, l, p: (r, 0, hidx(i)))
    ks = pl.BlockSpec((group, slots, half), lambda r, i, l, p: (r, 0, hidx(i)))
    ns = pl.BlockSpec((1, tree, half), lambda r, i, l, p: (jnp.clip(i[TREQ], 0, reqs - 1), 0, hidx(i)))
    lengths, parents, q, k, v, nk, nv = (
        pltpu.with_memory_space_constraint(a, pltpu.HBM) for a in (lengths, parents, q, k, v, nk, nv)
    )
    rows = half // 128 * (tree // 2) + half // 128
    sums = pl.BlockSpec((2 * group, rows, 128), lambda r, i, l, p: (r, 0, 0))
    in_specs = [qs, ks, ks, ns, ns]
    out_specs = [sums]
    out_shape = [jax.ShapeDtypeStruct((2 * reqs, rows, 128), BF)]
    if add:
        extra = (got,)
        in_specs.append(sums)
    else:
        extra = (pltpu.with_memory_space_constraint(w, pltpu.HBM),)
        in_specs.append(pl.BlockSpec(w.shape, lambda r, i, l, p: (0, 0)))
        out_specs.append(pl.BlockSpec(spread, lambda r, i, l, p: (0, 0, 0, 0, 0)))
        out_shape.append(jax.ShapeDtypeStruct(spread, w.dtype))
    return pl.pallas_call(
        functools.partial(attend_kernel, window, add),
        out_shape=out_shape,
        grid_spec=pltpu.PrefetchScalarGridSpec(
            num_scalar_prefetch=3,
            grid=(reqs // group,),
            in_specs=in_specs,
            out_specs=out_specs,
            scratch_shapes=[pltpu.VMEM((128, 128), F32)],
        ),
        compiler_params=pltpu.CompilerParams(vmem_limit_bytes=24 * MB),
        name="attend_mine" if add else "attend_theirs",
    )(info, lengths, parents, q, k, v, nk, nv, *extra)


def combine_kernel(parts_ref, out_ref):
    rows, width = out_ref.shape
    heads = width // 128
    total = jnp.sum(parts_ref[...].astype(F32), axis=0)
    den = total[heads * rows:]
    den = jnp.concatenate([den[:, :rows] + den[:, 64:64 + rows], jnp.ones((heads, 128 - rows), F32)], axis=1)
    den = jnp.transpose(jnp.concatenate([den, jnp.ones((128 - heads, 128), F32)], axis=0))
    for h in range(heads):
        val = total[h * rows:(h + 1) * rows] / den[:rows, h:h + 1]
        out_ref[:, h * 128:(h + 1) * 128] = val.astype(BF)


def combine(parts, rows, width):
    return pl.pallas_call(
        combine_kernel,
        out_shape=jax.ShapeDtypeStruct((rows, width), BF),
        compiler_params=pltpu.CompilerParams(vmem_limit_bytes=16 * MB),
        name="combine",
    )(parts)


def project_kernel(nx, info_ref, *refs):
    own, other = refs[:nx], refs[nx:2 * nx]
    ws, (res_ref, out_ref) = refs[2 * nx:-2], refs[-2:]
    core, x, y = info_ref[CORE], info_ref[X], info_ref[DP]
    rows, half = own[0].shape
    ny, deep = len(ws), ws[0].shape[0]
    mine = jnp.concatenate([own[s][...] for s in range(nx)], axis=0)
    theirs = jnp.concatenate([other[s][...] for s in range(nx)], axis=0)
    acc = None
    for s in range(ny):
        at = lax.rem(y + ny - s, ny)
        a = jnp.where(core == at // 2, mine, theirs)
        a = jnp.where(at % 2 == 0, a[:, :deep], a[:, deep:])
        part = jnp.dot(a, ws[s][...], preferred_element_type=F32)
        acc = part if acc is None else acc + part
    for s in range(nx):
        at = lax.rem(x + nx - s, nx)
        hid = (res_ref[at].astype(F32) + acc[s * rows:(s + 1) * rows]).astype(BF)
        for i in range(out_ref.shape[0]):
            out_ref[i, at] = hid


def project(info, own, other, ws, residual, copies):
    nx = len(own)
    rows, half = own[0].shape
    cols = ws[0].shape[1]
    part = pl.BlockSpec((rows, half), lambda g, i: (0, 0))
    residual = pltpu.with_memory_space_constraint(residual.reshape(-1, rows, residual.shape[2]), pltpu.HBM)
    return pl.pallas_call(
        functools.partial(project_kernel, nx),
        out_shape=jax.ShapeDtypeStruct((copies, nx, rows, cols), BF),
        grid_spec=pltpu.PrefetchScalarGridSpec(
            num_scalar_prefetch=1,
            grid=(1,),
            in_specs=[part] * (2 * nx)
            + [pl.BlockSpec(w.shape, lambda g, i: (0, 0)) for w in ws]
            + [pl.BlockSpec((nx, rows, cols), lambda g, i: (i[Z], 0, i[BLOCK]))],
            out_specs=pl.BlockSpec((copies, nx, rows, cols), lambda g, i: (0, 0, 0, 0)),
        ),
        compiler_params=pltpu.CompilerParams(vmem_limit_bytes=16 * MB),
        name="project",
    )(info, *own, *other, *ws, residual)


def vocab_kernel(
    info_ref, mine_ref, theirs_ref, gain_ref, tok_ref, par_ref, w_ref, more_ref, hid_out, stat_ref, hid_ref, x_ref, rest_ref, sem
):
    lead, others = w_ref.shape[1], rest_ref.shape[1]
    load = pltpu.make_async_copy(more_ref.at[:, pl.ds(lead, others)], rest_ref, sem.at[1])
    load.start()
    core = info_ref[CORE]
    nz, nx, rows, cols = mine_ref.shape
    half = nx * cols
    for z in range(nz):
        rs = slice(z * rows, (z + 1) * rows)
        squares = jnp.zeros((rows, cols), F32)
        for x in range(nx):
            mine, theirs = mine_ref[z, x], theirs_ref[z, x]
            low = jnp.where(core == 0, mine, theirs)
            high = jnp.where(core == 0, theirs, mine)
            hid_ref[rs, x * cols:(x + 1) * cols] = low
            hid_ref[rs, half + x * cols:half + (x + 1) * cols] = high
            squares = squares + low.astype(F32) * low.astype(F32) + high.astype(F32) * high.astype(F32)
        inv = lax.rsqrt(jnp.sum(squares, axis=1, keepdims=True) / (2 * half) + 1e-06)
        for j in range(2 * nx):
            cs = slice(j * cols, (j + 1) * cols)
            x_ref[rs, cs] = (hid_ref[rs, cs].astype(F32) * inv * gain_ref[:, cs]).astype(BF)
    copy = pltpu.make_async_copy(hid_ref, hid_out, sem.at[0])
    copy.start()
    tokens = nz * rows
    reqs, tree = tok_ref.shape
    sums = jnp.zeros((tokens, 128), F32)
    pick1 = jnp.zeros((tokens, 128), F32)
    pick2 = jnp.zeros((tokens, 128), F32)
    pick0 = [jnp.zeros((8, 128), F32) for _ in range(reqs)]
    lane = lax.broadcasted_iota(jnp.int32, (tokens, 128), 1)
    base = info_ref[BASE]
    tok = jnp.concatenate([tok_ref[...].astype(F32), jnp.full((reqs, 128 - tree), -1.0, F32)], axis=1)
    tok = jnp.transpose(tok)
    column = lambda n: jnp.concatenate([tok[n:n + tree, r:r + 1] for r in range(reqs)], axis=0).astype(jnp.int32)
    t1 = column(1) - base - lane
    t2 = column(2) - base - lane
    node = lax.broadcasted_iota(jnp.int32, (8, 128), 0)
    t0 = [jnp.where(node == 0, tok[0:8, r:r + 1].astype(jnp.int32) - base - lane[:8], -1) for r in range(reqs)]
    parts = [(w_ref, at, min(256, lead - at), at) for at in range(0, lead, 256)]
    parts += [(rest_ref, at, min(256, others - at), lead + at) for at in range(0, others, 256)]
    for ref, start, step, at in parts:
        if at == lead:
            load.wait()
        logits = jnp.dot(x_ref[...], ref[:, start:start + step], preferred_element_type=F32)
        for o in range(0, step, 128):
            lg = logits[:, o:o + 128]
            sums = sums + jnp.exp(lg)
            pick1 = jnp.where(t1 == at + o, lg, pick1)
            pick2 = jnp.where(t2 == at + o, lg, pick2)
            for r in range(reqs):
                pick0[r] = jnp.where(t0[r] == at + o, lg[r * tree:r * tree + 8], pick0[r])
    zero = jnp.zeros((tree - 8, 128), F32)
    pick0 = jnp.concatenate([p for r in range(reqs) for p in (pick0[r], zero)], axis=0)

    def by_request(a):
        a = jnp.sum(jnp.transpose(a), axis=0, keepdims=True)
        return jnp.concatenate([a[:, r * tree:(r + 1) * tree] for r in range(reqs)], axis=0)

    def later(a, n):
        return jnp.concatenate([a[:, :n], a[:, :tree - n]], axis=1)

    total, pick1, pick2, pick0 = (by_request(a) for a in (sums, pick1, pick2, pick0))
    at_node = lax.broadcasted_iota(jnp.int32, (reqs, tree), 1)
    near = par_ref[...] == at_node - 1
    root = at_node == 0
    pick = jnp.where(root, pick0, jnp.where(near, later(pick1, 1), later(pick2, 2)))
    total = jnp.where(root, total, jnp.where(near, later(total, 1), later(total, 2)))
    gap = jnp.zeros((reqs, 64 - tree), F32)
    stats = jnp.concatenate([total, gap, pick, gap], axis=1)
    for i in range(stat_ref.shape[0]):
        stat_ref[i] = stats
    copy.wait()


def vocab(info, mine, theirs, gain, toks, parents, lead, w, copies):
    nz, nx, rows, cols = mine.shape
    tokens, width = nz * rows, 2 * nx * cols
    vm = pl.BlockSpec(memory_space=pltpu.VMEM)
    return pl.pallas_call(
        vocab_kernel,
        out_shape=(
            jax.ShapeDtypeStruct((tokens, width), BF),
            jax.ShapeDtypeStruct((copies, toks.shape[0], 128), F32),
        ),
        in_specs=[pl.BlockSpec(memory_space=pltpu.SMEM), vm, vm, vm, vm, vm, vm, pl.BlockSpec(memory_space=pl.ANY)],
        out_specs=(pl.BlockSpec(memory_space=pl.ANY), vm),
        scratch_shapes=[
            pltpu.VMEM((tokens, width), BF),
            pltpu.VMEM((tokens, width), BF),
            pltpu.VMEM((width, w.shape[1] - lead.shape[1]), BF),
            pltpu.SemaphoreType.DMA((2,)),
        ],
        compiler_params=pltpu.CompilerParams(vmem_limit_bytes=24 * MB),
        name="vocab",
    )(info, mine, theirs, gain, toks, parents, lead, pltpu.with_memory_space_constraint(w, pltpu.HBM))


def fetch_kernel(w_ref, after_ref, out_ref, sem):
    copy = pltpu.make_async_copy(w_ref.at[:, pl.ds(0, out_ref.shape[1])], out_ref, sem)
    copy.start()
    copy.wait()


def fetch(w, after, cols):
    hbm = pl.BlockSpec(memory_space=pl.ANY)
    return pl.pallas_call(
        fetch_kernel,
        out_shape=jax.ShapeDtypeStruct((w.shape[0], cols), w.dtype),
        in_specs=[hbm, hbm],
        out_specs=pl.BlockSpec(memory_space=pltpu.VMEM),
        scratch_shapes=[pltpu.SemaphoreType.DMA],
        compiler_params=pltpu.CompilerParams(vmem_limit_bytes=2 * MB),
        name="fetch",
    )(pltpu.with_memory_space_constraint(w, pltpu.HBM), after)


def shifted(a, axis, step):
    n = lax.axis_size(axis)
    return lax.ppermute(a, axis, [(i, (i + step) % n) for i in range(n)])


def local(
    queries, new_keys, new_values, cache_keys, cache_values, lengths, parents,
    tree_tokens, residual, out_weight, norm_gain, vocab_weight,
):
    reqs, tree, width = queries.shape
    slots = cache_keys.shape[1]
    y, z, x, core = (lax.axis_index(a) for a in ("dp", "z", "x", "core"))
    ny, nz, nx, nc = (lax.axis_size(a) for a in ("dp", "z", "x", "core"))
    shard = (z * nx + x) * nc + core
    shards = nz * nx * nc
    window = slots * shards // 2
    half = width // nc
    block = half // nx
    tokens = reqs * tree
    swap = [(0, 1), (1, 0)]
    treq = jnp.where((shard >= reqs) & (shard < 2 * reqs), shard - reqs, -1)
    info = jnp.stack([core, shard * slots, treq, z, x, core * nx + x, y, shard * vocab_weight.shape[1]]).astype(jnp.int32)

    args = (lengths, parents, queries, cache_keys, cache_values, new_keys, new_values)
    spread = (nz, nx, nc, out_weight.shape[0], block)
    send, w = attend_half(window, info, *args, w=out_weight, spread=spread)
    got = lax.ppermute(send, "core", swap)
    w = lax.all_to_all(w.reshape(shards, -1, block), ("z", "x", "core"), 0, 0).reshape(-1, block)
    ws = [w] + [shifted(w, "dp", s) for s in range(1, ny)]
    (part,) = attend_half(window, info, *args, got=got)
    part = lax.all_to_all(part, ("z", "x"), 0, 0)
    att = combine(part, tokens // (nz * nx), half)
    own = [att] + [shifted(att, "x", s) for s in range(1, nx)]
    other = [lax.ppermute(a, "core", swap) for a in own]
    hid = project(info, own, other, ws, residual, nz * nx).reshape(nz * nx, -1, block)
    hid = lax.all_to_all(hid, ("z", "x"), 0, 0).reshape(nz, nx, -1, block)
    other = lax.ppermute(hid, "core", swap)
    scorer = fetch(vocab_weight, hid, 1024)
    hidden, stats = vocab(info, hid, other, norm_gain.reshape(1, -1), tree_tokens, parents, scorer, vocab_weight, shards)
    stats = jnp.sum(lax.all_to_all(stats, ("z", "x", "core"), 0, 0), axis=0)
    logprob = stats[:, 64:64 + tree] - jnp.log(stats[:, :tree])
    return hidden.reshape(reqs, tree, width), logprob


def solution(mesh):
    sizes = (mesh.shape["dp"], 4, 4, 2)
    grid = Mesh(mesh.devices.reshape(sizes), ("dp", "z", "x", "core"))
    mp = ("z", "x", "core")
    row = P("dp", None, None)
    placed = (
        row, row, row, P("dp", mp, None), P("dp", mp, None), P("dp"), P("dp", None), P("dp", None), row,
        P(("dp",) + mp, None), P(), P(None, mp),
    )
    return jax.shard_map(local, mesh=grid, in_specs=placed, out_specs=(row, P("dp", None)), check_vma=False)
```

```python
import functools

import jax
import jax.numpy as jnp
from jax import lax
from jax.experimental import pallas as pl
from jax.experimental.pallas import tpu as pltpu
from jax.sharding import Mesh, PartitionSpec as P

HEADS = 16
SINK = 4
BF = jnp.bfloat16
F32 = jnp.float32
NT = (((1,), (1,)), ((), ()))
TN = (((0,), (0,)), ((), ()))
CORE, FIRST, TREQ, Z, X, BLOCK, DP, BASE = range(8)
MB = 1 << 20


def attend_kernel(window, add, info_ref, len_ref, par_ref, q_ref, k_ref, v_ref, nk_ref, nv_ref, *refs):
    step = pl.program_id(0)
    if add:
        got_ref, out_ref, anc_ref = refs
    else:
        w_ref, out_ref, spread_ref, anc_ref = refs
        nz, nx, _, _, block = spread_ref.shape

        @pl.when(step == 0)
        def _():
            for x in range(nx):
                a = w_ref[:, x * block:(x + 1) * block]
                b = w_ref[:, (nx + x) * block:(nx + x + 1) * block]
                low = info_ref[CORE] == 0
                for z in range(nz):
                    spread_ref[z, x, 0] = jnp.where(low, a, b)
                    spread_ref[z, x, 1] = jnp.where(low, b, a)

    first = info_ref[FIRST]
    treq = info_ref[TREQ]
    reqs, tree, width = q_ref.shape
    slots = k_ref.shape[1]
    heads = width // 128
    part = tree // 2
    scale = 128 ** (-0.5) * 1.4426950408889634
    zero = jnp.zeros((tree, 128), BF)
    pairs = [slice(p * 256, (p + 1) * 256) for p in range(heads // 2)]

    def score(r, keys):
        out = []
        for cols in pairs:
            q = q_ref[r, :, cols]
            q = jnp.concatenate(
                [jnp.concatenate([q[:, :128], zero], axis=1), jnp.concatenate([zero, q[:, 128:]], axis=1)], axis=0
            )
            out.append(lax.dot_general(keys(cols), q, NT, preferred_element_type=F32))
        return out

    def weigh(scores, mask):
        exps = [jnp.where(mask, jnp.exp2(s * scale), 0.0) for s in scores]
        dens = [jnp.sum(e, axis=0, keepdims=True) for e in exps]
        dens = [d[:, t * tree:(t + 1) * tree] for d in dens for t in range(2)]
        return [e.astype(BF) for e in exps], jnp.concatenate(dens, axis=0)

    def finish(r, exps, dens, values):
        for p, cols in enumerate(pairs):
            o = lax.dot_general(exps[p], values(cols), TN, preferred_element_type=F32)
            for h, val in ((2 * p, o[:tree, :128]), (2 * p + 1, o[tree:, 128:])):
                for t in range(2):
                    rows = slice(h * part, (h + 1) * part)
                    half = val[t * part:(t + 1) * part]
                    if add:
                        half = half + got_ref[2 * r + t, rows].astype(F32)
                    out_ref[2 * r + t, rows] = half.astype(BF)
        gap = jnp.zeros((heads, 64 - part), F32)
        for t in range(2):
            den = dens[:, t * part:(t + 1) * part]
            if add:
                got = got_ref[2 * r + t, heads * part:].astype(F32)
                den = den + got[:, :part] + got[:, 64:64 + part]
            high = den.astype(BF).astype(F32)
            out_ref[2 * r + t, heads * part:] = jnp.concatenate([high, gap, den - high, gap], axis=1).astype(BF)

    @pl.when(treq < 0)
    def _():
        pos = first + lax.broadcasted_iota(jnp.int32, (slots, 2 * tree), 0)
        scores = [score(r, lambda cols: k_ref[r, :, cols]) for r in range(reqs)]
        weights = []
        for r in range(reqs):
            length = len_ref[step * reqs + r]
            mask = (pos < length) & ((pos < SINK) | (pos >= length - window))
            weights.append(weigh(scores[r], mask))
        for r in range(reqs):
            finish(r, *weights[r], lambda cols: v_ref[r, :, cols])

    @pl.when(treq >= 0)
    def _():
        out_ref[...] = got_ref[...] if add else jnp.zeros_like(out_ref)

        @pl.when(treq // reqs == step)
        def _():
            node = lax.broadcasted_iota(jnp.int32, (1, 128), 1)
            anc_ref[...] = jnp.zeros_like(anc_ref)
            anc_ref[0:1, :] = jnp.where(node == 0, 1.0, 0.0)

            def body(i, carry):
                up = anc_ref[pl.ds(par_ref[treq, i], 1), :]
                anc_ref[pl.ds(i, 1), :] = jnp.where(node == i, 1.0, up)
                return carry

            lax.fori_loop(1, tree, body, 0)
            mask = jnp.transpose(anc_ref[...])[:tree, :tree]
            mask = jnp.concatenate([mask, mask], axis=1) > 0.5
            r = lax.rem(treq, reqs)
            weights = weigh(score(r, lambda cols: nk_ref[0, :, cols]), mask)
            finish(r, *weights, lambda cols: nv_ref[0, :, cols])


def attend_half(window, info, lengths, parents, q, k, v, nk, nv, got=None, w=None, spread=None):
    reqs, tree, width = q.shape
    slots = k.shape[1]
    half = width // 2
    group = reqs // 2
    add = got is not None
    hidx = (lambda i: i[CORE]) if add else (lambda i: 1 - i[CORE])
    qs = pl.BlockSpec((group, tree, half), lambda r, i, l, p: (r, 0, hidx(i)))
    ks = pl.BlockSpec((group, slots, half), lambda r, i, l, p: (r, 0, hidx(i)))
    ns = pl.BlockSpec((1, tree, half), lambda r, i, l, p: (jnp.clip(i[TREQ], 0, reqs - 1), 0, hidx(i)))
    lengths, parents, q, k, v, nk, nv = (
        pltpu.with_memory_space_constraint(a, pltpu.HBM) for a in (lengths, parents, q, k, v, nk, nv)
    )
    rows = half // 128 * (tree // 2) + half // 128
    sums = pl.BlockSpec((2 * group, rows, 128), lambda r, i, l, p: (r, 0, 0))
    in_specs = [qs, ks, ks, ns, ns]
    out_specs = [sums]
    out_shape = [jax.ShapeDtypeStruct((2 * reqs, rows, 128), BF)]
    if add:
        extra = (got,)
        in_specs.append(sums)
    else:
        extra = (pltpu.with_memory_space_constraint(w, pltpu.HBM),)
        in_specs.append(pl.BlockSpec(w.shape, lambda r, i, l, p: (0, 0)))
        out_specs.append(pl.BlockSpec(spread, lambda r, i, l, p: (0, 0, 0, 0, 0)))
        out_shape.append(jax.ShapeDtypeStruct(spread, w.dtype))
    return pl.pallas_call(
        functools.partial(attend_kernel, window, add),
        out_shape=out_shape,
        grid_spec=pltpu.PrefetchScalarGridSpec(
            num_scalar_prefetch=3,
            grid=(reqs // group,),
            in_specs=in_specs,
            out_specs=out_specs,
            scratch_shapes=[pltpu.VMEM((128, 128), F32)],
        ),
        compiler_params=pltpu.CompilerParams(vmem_limit_bytes=24 * MB),
        name="attend_mine" if add else "attend_theirs",
    )(info, lengths, parents, q, k, v, nk, nv, *extra)


def combine_kernel(parts_ref, out_ref):
    rows, width = out_ref.shape
    heads = width // 128
    total = jnp.sum(parts_ref[...].astype(F32), axis=0)
    den = total[heads * rows:]
    den = jnp.concatenate([den[:, :rows] + den[:, 64:64 + rows], jnp.ones((heads, 128 - rows), F32)], axis=1)
    den = jnp.transpose(jnp.concatenate([den, jnp.ones((128 - heads, 128), F32)], axis=0))
    for h in range(heads):
        val = total[h * rows:(h + 1) * rows] / den[:rows, h:h + 1]
        out_ref[:, h * 128:(h + 1) * 128] = val.astype(BF)


def combine(parts, rows, width):
    return pl.pallas_call(
        combine_kernel,
        out_shape=jax.ShapeDtypeStruct((rows, width), BF),
        compiler_params=pltpu.CompilerParams(vmem_limit_bytes=16 * MB),
        name="combine",
    )(parts)


def project_kernel(nx, info_ref, *refs):
    own, other = refs[:nx], refs[nx:2 * nx]
    ws, (res_ref, out_ref) = refs[2 * nx:-2], refs[-2:]
    core, x, y = info_ref[CORE], info_ref[X], info_ref[DP]
    rows, half = own[0].shape
    ny, deep = len(ws), 2 * ws[0].shape[1]
    run = out_ref.shape[0]
    run = deep // (2 * run)
    mine = jnp.concatenate([own[s][...] for s in range(nx)], axis=0)
    theirs = jnp.concatenate([other[s][...] for s in range(nx)], axis=0)
    acc = None
    for s in range(ny):
        at = lax.rem(y + ny - s, ny)
        a = jnp.where(core == at // 2, mine, theirs)
        a = jnp.where(at % 2 == 0, a[:, :deep], a[:, deep:])
        even = jnp.where(core == 0, ws[s][0], ws[s][1])
        odd = jnp.where(core == 0, ws[s][1], ws[s][0])
        w = [b[i:i + run] for i in range(0, deep // 2, run) for b in (even, odd)]
        part = jnp.dot(a, jnp.concatenate(w, axis=0), preferred_element_type=F32)
        acc = part if acc is None else acc + part
    for s in range(nx):
        at = lax.rem(x + nx - s, nx)
        hid = (res_ref[at].astype(F32) + acc[s * rows:(s + 1) * rows]).astype(BF)
        for i in range(out_ref.shape[0]):
            out_ref[i, at] = hid


def project(info, own, other, ws, residual, copies):
    nx = len(own)
    rows, half = own[0].shape
    cols = ws[0].shape[2]
    part = pl.BlockSpec((rows, half), lambda g, i: (0, 0))
    residual = pltpu.with_memory_space_constraint(residual.reshape(-1, rows, residual.shape[2]), pltpu.HBM)
    return pl.pallas_call(
        functools.partial(project_kernel, nx),
        out_shape=jax.ShapeDtypeStruct((copies, nx, rows, cols), BF),
        grid_spec=pltpu.PrefetchScalarGridSpec(
            num_scalar_prefetch=1,
            grid=(1,),
            in_specs=[part] * (2 * nx)
            + [pl.BlockSpec(w.shape, lambda g, i: (0, 0, 0)) for w in ws]
            + [pl.BlockSpec((nx, rows, cols), lambda g, i: (i[Z], 0, i[BLOCK]))],
            out_specs=pl.BlockSpec((copies, nx, rows, cols), lambda g, i: (0, 0, 0, 0)),
        ),
        compiler_params=pltpu.CompilerParams(vmem_limit_bytes=16 * MB),
        name="project",
    )(info, *own, *other, *ws, residual)


def vocab_kernel(
    info_ref, mine_ref, theirs_ref, gain_ref, tok_ref, par_ref, w_ref, more_ref, hid_out, stat_ref, hid_ref, x_ref, rest_ref, sem
):
    lead, others = w_ref.shape[1], rest_ref.shape[1]
    load = pltpu.make_async_copy(more_ref.at[:, pl.ds(lead, others)], rest_ref, sem.at[1])
    load.start()
    core = info_ref[CORE]
    nz, nx, rows, cols = mine_ref.shape
    half = nx * cols
    for z in range(nz):
        rs = slice(z * rows, (z + 1) * rows)
        squares = jnp.zeros((rows, cols), F32)
        for x in range(nx):
            mine, theirs = mine_ref[z, x], theirs_ref[z, x]
            low = jnp.where(core == 0, mine, theirs)
            high = jnp.where(core == 0, theirs, mine)
            hid_ref[rs, x * cols:(x + 1) * cols] = low
            hid_ref[rs, half + x * cols:half + (x + 1) * cols] = high
            squares = squares + low.astype(F32) * low.astype(F32) + high.astype(F32) * high.astype(F32)
        inv = lax.rsqrt(jnp.sum(squares, axis=1, keepdims=True) / (2 * half) + 1e-06)
        for j in range(2 * nx):
            cs = slice(j * cols, (j + 1) * cols)
            x_ref[rs, cs] = (hid_ref[rs, cs].astype(F32) * inv * gain_ref[:, cs]).astype(BF)
    copy = pltpu.make_async_copy(hid_ref, hid_out, sem.at[0])
    copy.start()
    tokens = nz * rows
    reqs, tree = tok_ref.shape
    sums = jnp.zeros((tokens, 128), F32)
    pick1 = jnp.zeros((tokens, 128), F32)
    pick2 = jnp.zeros((tokens, 128), F32)
    pick0 = [jnp.zeros((8, 128), F32) for _ in range(reqs)]
    lane = lax.broadcasted_iota(jnp.int32, (tokens, 128), 1)
    base = info_ref[BASE]
    tok = jnp.concatenate([tok_ref[...].astype(F32), jnp.full((reqs, 128 - tree), -1.0, F32)], axis=1)
    tok = jnp.transpose(tok)
    column = lambda n: jnp.concatenate([tok[n:n + tree, r:r + 1] for r in range(reqs)], axis=0).astype(jnp.int32)
    t1 = column(1) - base - lane
    t2 = column(2) - base - lane
    node = lax.broadcasted_iota(jnp.int32, (8, 128), 0)
    t0 = [jnp.where(node == 0, tok[0:8, r:r + 1].astype(jnp.int32) - base - lane[:8], -1) for r in range(reqs)]
    parts = [(w_ref, at, min(256, lead - at), at) for at in range(0, lead, 256)]
    parts += [(rest_ref, at, min(256, others - at), lead + at) for at in range(0, others, 256)]
    for ref, start, step, at in parts:
        if at == lead:
            load.wait()
        logits = jnp.dot(x_ref[...], ref[:, start:start + step], preferred_element_type=F32)
        for o in range(0, step, 128):
            lg = logits[:, o:o + 128]
            sums = sums + jnp.exp(lg)
            pick1 = jnp.where(t1 == at + o, lg, pick1)
            pick2 = jnp.where(t2 == at + o, lg, pick2)
            for r in range(reqs):
                pick0[r] = jnp.where(t0[r] == at + o, lg[r * tree:r * tree + 8], pick0[r])
    zero = jnp.zeros((tree - 8, 128), F32)
    pick0 = jnp.concatenate([p for r in range(reqs) for p in (pick0[r], zero)], axis=0)

    def by_request(a):
        a = jnp.sum(jnp.transpose(a), axis=0, keepdims=True)
        return jnp.concatenate([a[:, r * tree:(r + 1) * tree] for r in range(reqs)], axis=0)

    def later(a, n):
        return jnp.concatenate([a[:, :n], a[:, :tree - n]], axis=1)

    total, pick1, pick2, pick0 = (by_request(a) for a in (sums, pick1, pick2, pick0))
    at_node = lax.broadcasted_iota(jnp.int32, (reqs, tree), 1)
    near = par_ref[...] == at_node - 1
    root = at_node == 0
    pick = jnp.where(root, pick0, jnp.where(near, later(pick1, 1), later(pick2, 2)))
    total = jnp.where(root, total, jnp.where(near, later(total, 1), later(total, 2)))
    gap = jnp.zeros((reqs, 64 - tree), F32)
    stats = jnp.concatenate([total, gap, pick, gap], axis=1)
    for i in range(stat_ref.shape[0]):
        stat_ref[i] = stats
    copy.wait()


def vocab(info, mine, theirs, gain, toks, parents, lead, w, copies):
    nz, nx, rows, cols = mine.shape
    tokens, width = nz * rows, 2 * nx * cols
    vm = pl.BlockSpec(memory_space=pltpu.VMEM)
    return pl.pallas_call(
        vocab_kernel,
        out_shape=(
            jax.ShapeDtypeStruct((tokens, width), BF),
            jax.ShapeDtypeStruct((copies, toks.shape[0], 128), F32),
        ),
        in_specs=[pl.BlockSpec(memory_space=pltpu.SMEM), vm, vm, vm, vm, vm, vm, pl.BlockSpec(memory_space=pl.ANY)],
        out_specs=(pl.BlockSpec(memory_space=pl.ANY), vm),
        scratch_shapes=[
            pltpu.VMEM((tokens, width), BF),
            pltpu.VMEM((tokens, width), BF),
            pltpu.VMEM((width, w.shape[1] - lead.shape[1]), BF),
            pltpu.SemaphoreType.DMA((2,)),
        ],
        compiler_params=pltpu.CompilerParams(vmem_limit_bytes=24 * MB),
        name="vocab",
    )(info, mine, theirs, gain, toks, parents, lead, pltpu.with_memory_space_constraint(w, pltpu.HBM))


def fetch_kernel(w_ref, after_ref, out_ref, sem):
    copy = pltpu.make_async_copy(w_ref.at[:, pl.ds(0, out_ref.shape[1])], out_ref, sem)
    copy.start()
    copy.wait()


def fetch(w, after, cols):
    hbm = pl.BlockSpec(memory_space=pl.ANY)
    return pl.pallas_call(
        fetch_kernel,
        out_shape=jax.ShapeDtypeStruct((w.shape[0], cols), w.dtype),
        in_specs=[hbm, hbm],
        out_specs=pl.BlockSpec(memory_space=pltpu.VMEM),
        scratch_shapes=[pltpu.SemaphoreType.DMA],
        compiler_params=pltpu.CompilerParams(vmem_limit_bytes=2 * MB),
        name="fetch",
    )(pltpu.with_memory_space_constraint(w, pltpu.HBM), after)


def shifted(a, axis, step):
    n = lax.axis_size(axis)
    return lax.ppermute(a, axis, [(i, (i + step) % n) for i in range(n)])


def local(
    queries, new_keys, new_values, cache_keys, cache_values, lengths, parents,
    tree_tokens, residual, out_weight, norm_gain, vocab_weight,
):
    reqs, tree, width = queries.shape
    slots = cache_keys.shape[1]
    y, z, x, core = (lax.axis_index(a) for a in ("dp", "z", "x", "core"))
    ny, nz, nx, nc = (lax.axis_size(a) for a in ("dp", "z", "x", "core"))
    shard = (z * nx + x) * nc + core
    shards = nz * nx * nc
    window = slots * shards // 2
    half = width // nc
    block = half // nx
    tokens = reqs * tree
    swap = [(0, 1), (1, 0)]
    treq = jnp.where((shard >= reqs) & (shard < 2 * reqs), shard - reqs, -1)
    info = jnp.stack([core, shard * slots, treq, z, x, core * nx + x, y, shard * vocab_weight.shape[1]]).astype(jnp.int32)

    args = (lengths, parents, queries, cache_keys, cache_values, new_keys, new_values)
    spread = (nz, nx, nc, out_weight.shape[0], block)
    send, w = attend_half(window, info, *args, w=out_weight, spread=spread)
    got = lax.ppermute(send, "core", swap)
    w = lax.all_to_all(w.reshape((nz * nx,) + w.shape[2:]), ("z", "x"), 0, 0)
    w = jnp.stack([w[:, 0].reshape(-1, block), lax.ppermute(w[:, 1].reshape(-1, block), "core", swap)])
    ws = [w] + [shifted(w, "dp", s) for s in range(1, ny)]
    (part,) = attend_half(window, info, *args, got=got)
    part = lax.all_to_all(part, ("z", "x"), 0, 0)
    att = combine(part, tokens // (nz * nx), half)
    own = [att] + [shifted(att, "x", s) for s in range(1, nx)]
    other = [lax.ppermute(a, "core", swap) for a in own]
    hid = project(info, own, other, ws, residual, nz * nx).reshape(nz * nx, -1, block)
    hid = lax.all_to_all(hid, ("z", "x"), 0, 0).reshape(nz, nx, -1, block)
    other = lax.ppermute(hid, "core", swap)
    scorer = fetch(vocab_weight, hid, 1536)
    hidden, stats = vocab(info, hid, other, norm_gain.reshape(1, -1), tree_tokens, parents, scorer, vocab_weight, shards)
    stats = jnp.sum(lax.all_to_all(stats, ("z", "x", "core"), 0, 0), axis=0)
    logprob = stats[:, 64:64 + tree] - jnp.log(stats[:, :tree])
    return hidden.reshape(reqs, tree, width), logprob


def solution(mesh):
    sizes = (mesh.shape["dp"], 4, 4, 2)
    grid = Mesh(mesh.devices.reshape(sizes), ("dp", "z", "x", "core"))
    mp = ("z", "x", "core")
    row = P("dp", None, None)
    placed = (
        row, row, row, P("dp", mp, None), P("dp", mp, None), P("dp"), P("dp", None), P("dp", None), row,
        P(("dp",) + mp, None), P(), P(None, mp),
    )
    return jax.shard_map(local, mesh=grid, in_specs=placed, out_specs=(row, P("dp", None)), check_vma=False)
```

```python
import functools

import jax
import jax.numpy as jnp
from jax import lax
from jax.experimental import pallas as pl
from jax.experimental.pallas import tpu as pltpu
from jax.sharding import Mesh, PartitionSpec as P

HEADS = 16
SINK = 4
BF = jnp.bfloat16
F32 = jnp.float32
NT = (((1,), (1,)), ((), ()))
TN = (((0,), (0,)), ((), ()))
CORE, FIRST, TREQ, Z, X, BLOCK, DP, BASE = range(8)
MB = 1 << 20


def attend_kernel(window, add, info_ref, len_ref, par_ref, q_ref, k_ref, v_ref, nk_ref, nv_ref, *refs):
    step = pl.program_id(0)
    if add:
        got_ref, out_ref, anc_ref = refs
    else:
        w_ref, out_ref, spread_ref, anc_ref = refs
        nz, nx, _, _, block = spread_ref.shape

        @pl.when(step == 0)
        def _():
            for x in range(nx):
                a = w_ref[:, x * block:(x + 1) * block]
                b = w_ref[:, (nx + x) * block:(nx + x + 1) * block]
                low = info_ref[CORE] == 0
                for z in range(nz):
                    spread_ref[z, x, 0] = jnp.where(low, a, b)
                    spread_ref[z, x, 1] = jnp.where(low, b, a)

    first = info_ref[FIRST]
    treq = info_ref[TREQ]
    reqs, tree, width = q_ref.shape
    slots = k_ref.shape[1]
    heads = width // 128
    part = tree // 2
    scale = 128 ** (-0.5) * 1.4426950408889634
    zero = jnp.zeros((tree, 128), BF)
    pairs = [slice(p * 256, (p + 1) * 256) for p in range(heads // 2)]

    def score(r, keys):
        out = []
        for cols in pairs:
            q = q_ref[r, :, cols]
            q = jnp.concatenate(
                [jnp.concatenate([q[:, :128], zero], axis=1), jnp.concatenate([zero, q[:, 128:]], axis=1)], axis=0
            )
            out.append(lax.dot_general(keys(cols), q, NT, preferred_element_type=F32))
        return out

    def weigh(scores, mask):
        exps = [jnp.where(mask, jnp.exp2(s * scale), 0.0) for s in scores]
        dens = [jnp.sum(e, axis=0, keepdims=True) for e in exps]
        dens = [d[:, t * tree:(t + 1) * tree] for d in dens for t in range(2)]
        return [e.astype(BF) for e in exps], jnp.concatenate(dens, axis=0)

    def finish(r, exps, dens, values):
        for p, cols in enumerate(pairs):
            o = lax.dot_general(exps[p], values(cols), TN, preferred_element_type=F32)
            for h, val in ((2 * p, o[:tree, :128]), (2 * p + 1, o[tree:, 128:])):
                for t in range(2):
                    rows = slice(h * part, (h + 1) * part)
                    half = val[t * part:(t + 1) * part]
                    if add:
                        half = half + got_ref[2 * r + t, rows].astype(F32)
                    out_ref[2 * r + t, rows] = half.astype(BF)
        gap = jnp.zeros((heads, 64 - part), F32)
        for t in range(2):
            den = dens[:, t * part:(t + 1) * part]
            if add:
                got = got_ref[2 * r + t, heads * part:].astype(F32)
                den = den + got[:, :part] + got[:, 64:64 + part]
            high = den.astype(BF).astype(F32)
            out_ref[2 * r + t, heads * part:] = jnp.concatenate([high, gap, den - high, gap], axis=1).astype(BF)

    @pl.when(treq < 0)
    def _():
        pos = first + lax.broadcasted_iota(jnp.int32, (slots, 2 * tree), 0)
        scores = [score(r, lambda cols: k_ref[r, :, cols]) for r in range(reqs)]
        weights = []
        for r in range(reqs):
            length = len_ref[step * reqs + r]
            mask = (pos < length) & ((pos < SINK) | (pos >= length - window))
            weights.append(weigh(scores[r], mask))
        for r in range(reqs):
            finish(r, *weights[r], lambda cols: v_ref[r, :, cols])

    @pl.when(treq >= 0)
    def _():
        out_ref[...] = got_ref[...] if add else jnp.zeros_like(out_ref)

        @pl.when(treq // reqs == step)
        def _():
            node = lax.broadcasted_iota(jnp.int32, (1, 128), 1)
            anc_ref[...] = jnp.zeros_like(anc_ref)
            anc_ref[0:1, :] = jnp.where(node == 0, 1.0, 0.0)

            def body(i, carry):
                up = anc_ref[pl.ds(par_ref[treq, i], 1), :]
                anc_ref[pl.ds(i, 1), :] = jnp.where(node == i, 1.0, up)
                return carry

            lax.fori_loop(1, tree, body, 0)
            mask = jnp.transpose(anc_ref[...])[:tree, :tree]
            mask = jnp.concatenate([mask, mask], axis=1) > 0.5
            r = lax.rem(treq, reqs)
            weights = weigh(score(r, lambda cols: nk_ref[0, :, cols]), mask)
            finish(r, *weights, lambda cols: nv_ref[0, :, cols])


def attend_half(window, info, lengths, parents, q, k, v, nk, nv, got=None, w=None, spread=None):
    reqs, tree, width = q.shape
    slots = k.shape[1]
    half = width // 2
    group = reqs // 2
    add = got is not None
    hidx = (lambda i: i[CORE]) if add else (lambda i: 1 - i[CORE])
    qs = pl.BlockSpec((group, tree, half), lambda r, i, l, p: (r, 0, hidx(i)))
    ks = pl.BlockSpec((group, slots, half), lambda r, i, l, p: (r, 0, hidx(i)))
    ns = pl.BlockSpec((1, tree, half), lambda r, i, l, p: (jnp.clip(i[TREQ], 0, reqs - 1), 0, hidx(i)))
    lengths, parents, q, k, v, nk, nv = (
        pltpu.with_memory_space_constraint(a, pltpu.HBM) for a in (lengths, parents, q, k, v, nk, nv)
    )
    rows = half // 128 * (tree // 2) + half // 128
    sums = pl.BlockSpec((2 * group, rows, 128), lambda r, i, l, p: (r, 0, 0))
    in_specs = [qs, ks, ks, ns, ns]
    out_specs = [sums]
    out_shape = [jax.ShapeDtypeStruct((2 * reqs, rows, 128), BF)]
    if add:
        extra = (got,)
        in_specs.append(sums)
    else:
        extra = (pltpu.with_memory_space_constraint(w, pltpu.HBM),)
        in_specs.append(pl.BlockSpec(w.shape, lambda r, i, l, p: (0, 0)))
        out_specs.append(pl.BlockSpec(spread, lambda r, i, l, p: (0, 0, 0, 0, 0)))
        out_shape.append(jax.ShapeDtypeStruct(spread, w.dtype))
    return pl.pallas_call(
        functools.partial(attend_kernel, window, add),
        out_shape=out_shape,
        grid_spec=pltpu.PrefetchScalarGridSpec(
            num_scalar_prefetch=3,
            grid=(reqs // group,),
            in_specs=in_specs,
            out_specs=out_specs,
            scratch_shapes=[pltpu.VMEM((128, 128), F32)],
        ),
        compiler_params=pltpu.CompilerParams(vmem_limit_bytes=24 * MB),
        name="attend_mine" if add else "attend_theirs",
    )(info, lengths, parents, q, k, v, nk, nv, *extra)


def combine_kernel(parts_ref, out_ref):
    rows, width = out_ref.shape
    heads = width // 128
    total = jnp.sum(parts_ref[...].astype(F32), axis=0)
    den = total[heads * rows:]
    den = jnp.concatenate([den[:, :rows] + den[:, 64:64 + rows], jnp.ones((heads, 128 - rows), F32)], axis=1)
    den = jnp.transpose(jnp.concatenate([den, jnp.ones((128 - heads, 128), F32)], axis=0))
    for h in range(heads):
        val = total[h * rows:(h + 1) * rows] / den[:rows, h:h + 1]
        out_ref[:, h * 128:(h + 1) * 128] = val.astype(BF)


def combine(parts, rows, width):
    return pl.pallas_call(
        combine_kernel,
        out_shape=jax.ShapeDtypeStruct((rows, width), BF),
        compiler_params=pltpu.CompilerParams(vmem_limit_bytes=16 * MB),
        name="combine",
    )(parts)


def pile_kernel(n, *refs):
    for i in range(n):
        refs[-1][i] = refs[i][...]


def pile(arrays, after):
    shape = (len(arrays),) + arrays[0].shape
    vm = pl.BlockSpec(memory_space=pltpu.VMEM)
    return pl.pallas_call(
        functools.partial(pile_kernel, len(arrays)),
        out_shape=jax.ShapeDtypeStruct(shape, arrays[0].dtype),
        in_specs=[vm] * len(arrays) + [pl.BlockSpec(memory_space=pl.ANY)] * len(after),
        out_specs=vm,
        compiler_params=pltpu.CompilerParams(vmem_limit_bytes=2 * MB),
        name="pile",
    )(*arrays, *after)


def project_kernel(info_ref, own, other, *refs):
    ws, (res_ref, out_ref) = refs[:-2], refs[-2:]
    core, x, y = info_ref[CORE], info_ref[X], info_ref[DP]
    nx, rows, half = own.shape
    ny, deep = len(ws), 2 * ws[0].shape[1]
    run = out_ref.shape[0]
    run = deep // (2 * run)
    mine = jnp.concatenate([own[s] for s in range(nx)], axis=0)
    theirs = jnp.concatenate([other[s] for s in range(nx)], axis=0)
    acc = None
    for s in range(ny):
        at = lax.rem(y + ny - s, ny)
        a = jnp.where(core == at // 2, mine, theirs)
        a = jnp.where(at % 2 == 0, a[:, :deep], a[:, deep:])
        even = jnp.where(core == 0, ws[s][0], ws[s][1])
        odd = jnp.where(core == 0, ws[s][1], ws[s][0])
        w = [b[i:i + run] for i in range(0, deep // 2, run) for b in (even, odd)]
        part = jnp.dot(a, jnp.concatenate(w, axis=0), preferred_element_type=F32)
        acc = part if acc is None else acc + part
    for s in range(nx):
        at = lax.rem(x + nx - s, nx)
        hid = (res_ref[at].astype(F32) + acc[s * rows:(s + 1) * rows]).astype(BF)
        for i in range(out_ref.shape[0]):
            out_ref[i, at] = hid


def project(info, own, other, ws, residual, copies):
    nx, rows, half = own.shape
    cols = ws[0].shape[2]
    part = pl.BlockSpec((nx, rows, half), lambda g, i: (0, 0, 0))
    residual = pltpu.with_memory_space_constraint(residual.reshape(-1, rows, residual.shape[2]), pltpu.HBM)
    return pl.pallas_call(
        project_kernel,
        out_shape=jax.ShapeDtypeStruct((copies, nx, rows, cols), BF),
        grid_spec=pltpu.PrefetchScalarGridSpec(
            num_scalar_prefetch=1,
            grid=(1,),
            in_specs=[part, part]
            + [pl.BlockSpec(w.shape, lambda g, i: (0, 0, 0)) for w in ws]
            + [pl.BlockSpec((nx, rows, cols), lambda g, i: (i[Z], 0, i[BLOCK]))],
            out_specs=pl.BlockSpec((copies, nx, rows, cols), lambda g, i: (0, 0, 0, 0)),
        ),
        compiler_params=pltpu.CompilerParams(vmem_limit_bytes=16 * MB),
        name="project",
    )(info, own, other, *ws, residual)


def vocab_kernel(
    info_ref, mine_ref, theirs_ref, gain_ref, tok_ref, par_ref, w_ref, more_ref, hid_out, stat_ref, hid_ref, x_ref, rest_ref, sem
):
    lead, others = w_ref.shape[1], rest_ref.shape[1]
    load = pltpu.make_async_copy(more_ref.at[:, pl.ds(lead, others)], rest_ref, sem.at[1])
    load.start()
    core = info_ref[CORE]
    nz, nx, rows, cols = mine_ref.shape
    half = nx * cols
    for z in range(nz):
        rs = slice(z * rows, (z + 1) * rows)
        squares = jnp.zeros((rows, cols), F32)
        for x in range(nx):
            mine, theirs = mine_ref[z, x], theirs_ref[z, x]
            low = jnp.where(core == 0, mine, theirs)
            high = jnp.where(core == 0, theirs, mine)
            hid_ref[rs, x * cols:(x + 1) * cols] = low
            hid_ref[rs, half + x * cols:half + (x + 1) * cols] = high
            squares = squares + low.astype(F32) * low.astype(F32) + high.astype(F32) * high.astype(F32)
        inv = lax.rsqrt(jnp.sum(squares, axis=1, keepdims=True) / (2 * half) + 1e-06)
        for j in range(2 * nx):
            cs = slice(j * cols, (j + 1) * cols)
            x_ref[rs, cs] = (hid_ref[rs, cs].astype(F32) * inv * gain_ref[:, cs]).astype(BF)
    copy = pltpu.make_async_copy(hid_ref, hid_out, sem.at[0])
    copy.start()
    tokens = nz * rows
    reqs, tree = tok_ref.shape
    sums = jnp.zeros((tokens, 128), F32)
    pick1 = jnp.zeros((tokens, 128), F32)
    pick2 = jnp.zeros((tokens, 128), F32)
    pick0 = [jnp.zeros((8, 128), F32) for _ in range(reqs)]
    lane = lax.broadcasted_iota(jnp.int32, (tokens, 128), 1)
    base = info_ref[BASE]
    tok = jnp.concatenate([tok_ref[...].astype(F32), jnp.full((reqs, 128 - tree), -1.0, F32)], axis=1)
    tok = jnp.transpose(tok)
    column = lambda n: jnp.concatenate([tok[n:n + tree, r:r + 1] for r in range(reqs)], axis=0).astype(jnp.int32)
    t1 = column(1) - base - lane
    t2 = column(2) - base - lane
    node = lax.broadcasted_iota(jnp.int32, (8, 128), 0)
    t0 = [jnp.where(node == 0, tok[0:8, r:r + 1].astype(jnp.int32) - base - lane[:8], -1) for r in range(reqs)]
    parts = [(w_ref, at, min(256, lead - at), at) for at in range(0, lead, 256)]
    parts += [(rest_ref, at, min(256, others - at), lead + at) for at in range(0, others, 256)]
    for ref, start, step, at in parts:
        if at == lead:
            load.wait()
        logits = jnp.dot(x_ref[...], ref[:, start:start + step], preferred_element_type=F32)
        for o in range(0, step, 128):
            lg = logits[:, o:o + 128]
            sums = sums + jnp.exp(lg)
            pick1 = jnp.where(t1 == at + o, lg, pick1)
            pick2 = jnp.where(t2 == at + o, lg, pick2)
            for r in range(reqs):
                pick0[r] = jnp.where(t0[r] == at + o, lg[r * tree:r * tree + 8], pick0[r])
    zero = jnp.zeros((tree - 8, 128), F32)
    pick0 = jnp.concatenate([p for r in range(reqs) for p in (pick0[r], zero)], axis=0)

    def by_request(a):
        a = jnp.sum(jnp.transpose(a), axis=0, keepdims=True)
        return jnp.concatenate([a[:, r * tree:(r + 1) * tree] for r in range(reqs)], axis=0)

    def later(a, n):
        return jnp.concatenate([a[:, :n], a[:, :tree - n]], axis=1)

    total, pick1, pick2, pick0 = (by_request(a) for a in (sums, pick1, pick2, pick0))
    at_node = lax.broadcasted_iota(jnp.int32, (reqs, tree), 1)
    near = par_ref[...] == at_node - 1
    root = at_node == 0
    pick = jnp.where(root, pick0, jnp.where(near, later(pick1, 1), later(pick2, 2)))
    total = jnp.where(root, total, jnp.where(near, later(total, 1), later(total, 2)))
    gap = jnp.zeros((reqs, 64 - tree), F32)
    stats = jnp.concatenate([total, gap, pick, gap], axis=1)
    for i in range(stat_ref.shape[0]):
        stat_ref[i] = stats
    copy.wait()


def vocab(info, mine, theirs, gain, toks, parents, lead, w, copies):
    nz, nx, rows, cols = mine.shape
    tokens, width = nz * rows, 2 * nx * cols
    vm = pl.BlockSpec(memory_space=pltpu.VMEM)
    return pl.pallas_call(
        vocab_kernel,
        out_shape=(
            jax.ShapeDtypeStruct((tokens, width), BF),
            jax.ShapeDtypeStruct((copies, toks.shape[0], 128), F32),
        ),
        in_specs=[pl.BlockSpec(memory_space=pltpu.SMEM), vm, vm, vm, vm, vm, vm, pl.BlockSpec(memory_space=pl.ANY)],
        out_specs=(pl.BlockSpec(memory_space=pl.ANY), vm),
        scratch_shapes=[
            pltpu.VMEM((tokens, width), BF),
            pltpu.VMEM((tokens, width), BF),
            pltpu.VMEM((width, w.shape[1] - lead.shape[1]), BF),
            pltpu.SemaphoreType.DMA((2,)),
        ],
        compiler_params=pltpu.CompilerParams(vmem_limit_bytes=24 * MB),
        name="vocab",
    )(info, mine, theirs, gain, toks, parents, lead, pltpu.with_memory_space_constraint(w, pltpu.HBM))


def fetch_kernel(w_ref, after_ref, out_ref, sem):
    copy = pltpu.make_async_copy(w_ref.at[:, pl.ds(0, out_ref.shape[1])], out_ref, sem)
    copy.start()
    copy.wait()


def fetch(w, after, cols):
    hbm = pl.BlockSpec(memory_space=pl.ANY)
    return pl.pallas_call(
        fetch_kernel,
        out_shape=jax.ShapeDtypeStruct((w.shape[0], cols), w.dtype),
        in_specs=[hbm, hbm],
        out_specs=pl.BlockSpec(memory_space=pltpu.VMEM),
        scratch_shapes=[pltpu.SemaphoreType.DMA],
        compiler_params=pltpu.CompilerParams(vmem_limit_bytes=2 * MB),
        name="fetch",
    )(pltpu.with_memory_space_constraint(w, pltpu.HBM), after)


def shifted(a, axis, step):
    n = lax.axis_size(axis)
    return lax.ppermute(a, axis, [(i, (i + step) % n) for i in range(n)])


def local(
    queries, new_keys, new_values, cache_keys, cache_values, lengths, parents,
    tree_tokens, residual, out_weight, norm_gain, vocab_weight,
):
    reqs, tree, width = queries.shape
    slots = cache_keys.shape[1]
    y, z, x, core = (lax.axis_index(a) for a in ("dp", "z", "x", "core"))
    ny, nz, nx, nc = (lax.axis_size(a) for a in ("dp", "z", "x", "core"))
    shard = (z * nx + x) * nc + core
    shards = nz * nx * nc
    window = slots * shards // 2
    half = width // nc
    block = half // nx
    tokens = reqs * tree
    swap = [(0, 1), (1, 0)]
    treq = jnp.where((shard >= reqs) & (shard < 2 * reqs), shard - reqs, -1)
    info = jnp.stack([core, shard * slots, treq, z, x, core * nx + x, y, shard * vocab_weight.shape[1]]).astype(jnp.int32)

    args = (lengths, parents, queries, cache_keys, cache_values, new_keys, new_values)
    spread = (nz, nx, nc, out_weight.shape[0], block)
    send, w = attend_half(window, info, *args, w=out_weight, spread=spread)
    got = lax.ppermute(send, "core", swap)
    w = lax.all_to_all(w.reshape((nz * nx,) + w.shape[2:]), ("z", "x"), 0, 0)
    w = jnp.stack([w[:, 0].reshape(-1, block), lax.ppermute(w[:, 1].reshape(-1, block), "core", swap)])
    ws = [w] + [shifted(w, "dp", s) for s in range(1, ny)]
    (part,) = attend_half(window, info, *args, got=got)
    part = lax.all_to_all(part, ("z", "x"), 0, 0)
    att = combine(part, tokens // (nz * nx), half)
    own = pile([att] + [shifted(att, "x", s) for s in range(1, nx)], ws)
    other = lax.ppermute(own, "core", swap)
    hid = project(info, own, other, ws, residual, nz * nx).reshape(nz * nx, -1, block)
    hid = lax.all_to_all(hid, ("z", "x"), 0, 0).reshape(nz, nx, -1, block)
    other = lax.ppermute(hid, "core", swap)
    scorer = fetch(vocab_weight, hid, 1536)
    hidden, stats = vocab(info, hid, other, norm_gain.reshape(1, -1), tree_tokens, parents, scorer, vocab_weight, shards)
    stats = jnp.sum(lax.all_to_all(stats, ("z", "x", "core"), 0, 0), axis=0)
    logprob = stats[:, 64:64 + tree] - jnp.log(stats[:, :tree])
    return hidden.reshape(reqs, tree, width), logprob


def solution(mesh):
    sizes = (mesh.shape["dp"], 4, 4, 2)
    grid = Mesh(mesh.devices.reshape(sizes), ("dp", "z", "x", "core"))
    mp = ("z", "x", "core")
    row = P("dp", None, None)
    placed = (
        row, row, row, P("dp", mp, None), P("dp", mp, None), P("dp"), P("dp", None), P("dp", None), row,
        P(("dp",) + mp, None), P(), P(None, mp),
    )
    return jax.shard_map(local, mesh=grid, in_specs=placed, out_specs=(row, P("dp", None)), check_vma=False)
```

```python
import functools

import jax
import jax.numpy as jnp
from jax import lax
from jax.experimental import pallas as pl
from jax.experimental.pallas import tpu as pltpu
from jax.sharding import Mesh, PartitionSpec as P

HEADS = 16
SINK = 4
BF = jnp.bfloat16
F32 = jnp.float32
NT = (((1,), (1,)), ((), ()))
TN = (((0,), (0,)), ((), ()))
CORE, FIRST, TREQ, Z, X, BLOCK, DP, BASE = range(8)
MB = 1 << 20


def attend_kernel(window, add, info_ref, len_ref, par_ref, q_ref, k_ref, v_ref, nk_ref, nv_ref, *refs):
    step = pl.program_id(0)
    if add:
        got_ref, out_ref, anc_ref = refs
    else:
        w_ref, out_ref, spread_ref, anc_ref = refs
        nz, nx, nc, _, block = spread_ref.shape

        @pl.when(step == 0)
        def _():
            for c in range(nc):
                for x in range(nx):
                    at = (c * nx + x) * block
                    for z in range(nz):
                        spread_ref[z, x, c] = w_ref[:, at:at + block]

    first = info_ref[FIRST]
    treq = info_ref[TREQ]
    reqs, tree, width = q_ref.shape
    slots = k_ref.shape[1]
    heads = width // 128
    part = tree // 2
    scale = 128 ** (-0.5) * 1.4426950408889634
    zero = jnp.zeros((tree, 128), BF)
    pairs = [slice(p * 256, (p + 1) * 256) for p in range(heads // 2)]

    def score(r, keys):
        out = []
        for cols in pairs:
            q = q_ref[r, :, cols]
            q = jnp.concatenate(
                [jnp.concatenate([q[:, :128], zero], axis=1), jnp.concatenate([zero, q[:, 128:]], axis=1)], axis=0
            )
            out.append(lax.dot_general(keys(cols), q, NT, preferred_element_type=F32))
        return out

    def weigh(scores, mask):
        exps = [jnp.where(mask, jnp.exp2(s * scale), 0.0) for s in scores]
        dens = [jnp.sum(e, axis=0, keepdims=True) for e in exps]
        dens = [d[:, t * tree:(t + 1) * tree] for d in dens for t in range(2)]
        return [e.astype(BF) for e in exps], jnp.concatenate(dens, axis=0)

    def finish(r, exps, dens, values):
        for p, cols in enumerate(pairs):
            o = lax.dot_general(exps[p], values(cols), TN, preferred_element_type=F32)
            for h, val in ((2 * p, o[:tree, :128]), (2 * p + 1, o[tree:, 128:])):
                for t in range(2):
                    rows = slice(h * part, (h + 1) * part)
                    half = val[t * part:(t + 1) * part]
                    if add:
                        half = half + got_ref[2 * r + t, rows].astype(F32)
                    out_ref[2 * r + t, rows] = half.astype(BF)
        gap = jnp.zeros((heads, 64 - part), F32)
        for t in range(2):
            den = dens[:, t * part:(t + 1) * part]
            if add:
                got = got_ref[2 * r + t, heads * part:].astype(F32)
                den = den + got[:, :part] + got[:, 64:64 + part]
            high = den.astype(BF).astype(F32)
            out_ref[2 * r + t, heads * part:] = jnp.concatenate([high, gap, den - high, gap], axis=1).astype(BF)

    @pl.when(treq < 0)
    def _():
        pos = first + lax.broadcasted_iota(jnp.int32, (slots, 2 * tree), 0)
        scores = [score(r, lambda cols: k_ref[r, :, cols]) for r in range(reqs)]
        weights = []
        for r in range(reqs):
            length = len_ref[step * reqs + r]
            mask = (pos < length) & ((pos < SINK) | (pos >= length - window))
            weights.append(weigh(scores[r], mask))
        for r in range(reqs):
            finish(r, *weights[r], lambda cols: v_ref[r, :, cols])

    @pl.when(treq >= 0)
    def _():
        out_ref[...] = got_ref[...] if add else jnp.zeros_like(out_ref)

        @pl.when(treq // reqs == step)
        def _():
            node = lax.broadcasted_iota(jnp.int32, (1, 128), 1)
            anc_ref[...] = jnp.zeros_like(anc_ref)
            anc_ref[0:1, :] = jnp.where(node == 0, 1.0, 0.0)

            def body(i, carry):
                up = anc_ref[pl.ds(par_ref[treq, i], 1), :]
                anc_ref[pl.ds(i, 1), :] = jnp.where(node == i, 1.0, up)
                return carry

            lax.fori_loop(1, tree, body, 0)
            mask = jnp.transpose(anc_ref[...])[:tree, :tree]
            mask = jnp.concatenate([mask, mask], axis=1) > 0.5
            r = lax.rem(treq, reqs)
            weights = weigh(score(r, lambda cols: nk_ref[0, :, cols]), mask)
            finish(r, *weights, lambda cols: nv_ref[0, :, cols])


def attend_half(window, info, lengths, parents, q, k, v, nk, nv, got=None, w=None, spread=None):
    reqs, tree, width = q.shape
    slots = k.shape[1]
    half = width // 2
    group = reqs // 2
    add = got is not None
    hidx = (lambda i: i[CORE]) if add else (lambda i: 1 - i[CORE])
    qs = pl.BlockSpec((group, tree, half), lambda r, i, l, p: (r, 0, hidx(i)))
    ks = pl.BlockSpec((group, slots, half), lambda r, i, l, p: (r, 0, hidx(i)))
    ns = pl.BlockSpec((1, tree, half), lambda r, i, l, p: (jnp.clip(i[TREQ], 0, reqs - 1), 0, hidx(i)))
    lengths, parents, q, k, v, nk, nv = (
        pltpu.with_memory_space_constraint(a, pltpu.HBM) for a in (lengths, parents, q, k, v, nk, nv)
    )
    rows = half // 128 * (tree // 2) + half // 128
    sums = pl.BlockSpec((2 * group, rows, 128), lambda r, i, l, p: (r, 0, 0))
    in_specs = [qs, ks, ks, ns, ns]
    out_specs = [sums]
    out_shape = [jax.ShapeDtypeStruct((2 * reqs, rows, 128), BF)]
    if add:
        extra = (got,)
        in_specs.append(sums)
    else:
        extra = (pltpu.with_memory_space_constraint(w, pltpu.HBM),)
        in_specs.append(pl.BlockSpec(w.shape, lambda r, i, l, p: (0, 0)))
        out_specs.append(pl.BlockSpec(spread, lambda r, i, l, p: (0, 0, 0, 0, 0)))
        out_shape.append(jax.ShapeDtypeStruct(spread, w.dtype))
    return pl.pallas_call(
        functools.partial(attend_kernel, window, add),
        out_shape=out_shape,
        grid_spec=pltpu.PrefetchScalarGridSpec(
            num_scalar_prefetch=3,
            grid=(reqs // group,),
            in_specs=in_specs,
            out_specs=out_specs,
            scratch_shapes=[pltpu.VMEM((128, 128), F32)],
        ),
        compiler_params=pltpu.CompilerParams(vmem_limit_bytes=24 * MB),
        name="attend_mine" if add else "attend_theirs",
    )(info, lengths, parents, q, k, v, nk, nv, *extra)


def combine_kernel(parts_ref, out_ref):
    rows, width = out_ref.shape
    heads = width // 128
    total = jnp.sum(parts_ref[...].astype(F32), axis=0)
    den = total[heads * rows:]
    den = jnp.concatenate([den[:, :rows] + den[:, 64:64 + rows], jnp.ones((heads, 128 - rows), F32)], axis=1)
    den = jnp.transpose(jnp.concatenate([den, jnp.ones((128 - heads, 128), F32)], axis=0))
    for h in range(heads):
        val = total[h * rows:(h + 1) * rows] / den[:rows, h:h + 1]
        out_ref[:, h * 128:(h + 1) * 128] = val.astype(BF)


def combine(parts, rows, width):
    return pl.pallas_call(
        combine_kernel,
        out_shape=jax.ShapeDtypeStruct((rows, width), BF),
        compiler_params=pltpu.CompilerParams(vmem_limit_bytes=16 * MB),
        name="combine",
    )(parts)


def pile_kernel(n, *refs):
    for i in range(n):
        refs[-1][i] = refs[i][...]


def pile(arrays, after):
    shape = (len(arrays),) + arrays[0].shape
    vm = pl.BlockSpec(memory_space=pltpu.VMEM)
    return pl.pallas_call(
        functools.partial(pile_kernel, len(arrays)),
        out_shape=jax.ShapeDtypeStruct(shape, arrays[0].dtype),
        in_specs=[vm] * len(arrays) + [pl.BlockSpec(memory_space=pl.ANY)] * len(after),
        out_specs=vm,
        compiler_params=pltpu.CompilerParams(vmem_limit_bytes=2 * MB),
        name="pile",
    )(*arrays, *after)


def project_kernel(info_ref, own, other, *refs):
    ws, (res_ref, out_ref) = refs[:-2], refs[-2:]
    core, x, y = info_ref[CORE], info_ref[X], info_ref[DP]
    nx, rows, half = own.shape
    ny, deep = len(ws), ws[0].shape[0]
    mine = jnp.concatenate([own[s] for s in range(nx)], axis=0)
    theirs = jnp.concatenate([other[s] for s in range(nx)], axis=0)
    acc = None
    for s in range(ny):
        at = lax.rem(y + ny - s, ny)
        a = jnp.where(core == at // 2, mine, theirs)
        a = jnp.where(at % 2 == 0, a[:, :deep], a[:, deep:])
        part = jnp.dot(a, ws[s][...], preferred_element_type=F32)
        acc = part if acc is None else acc + part
    for s in range(nx):
        at = lax.rem(x + nx - s, nx)
        hid = (res_ref[at].astype(F32) + acc[s * rows:(s + 1) * rows]).astype(BF)
        for i in range(out_ref.shape[0]):
            out_ref[i, at] = hid


def project(info, own, other, ws, residual, copies):
    nx, rows, half = own.shape
    cols = ws[0].shape[1]
    part = pl.BlockSpec((nx, rows, half), lambda g, i: (0, 0, 0))
    residual = pltpu.with_memory_space_constraint(residual.reshape(-1, rows, residual.shape[2]), pltpu.HBM)
    return pl.pallas_call(
        project_kernel,
        out_shape=jax.ShapeDtypeStruct((copies, nx, rows, cols), BF),
        grid_spec=pltpu.PrefetchScalarGridSpec(
            num_scalar_prefetch=1,
            grid=(1,),
            in_specs=[part, part]
            + [pl.BlockSpec(w.shape, lambda g, i: (0, 0)) for w in ws]
            + [pl.BlockSpec((nx, rows, cols), lambda g, i: (i[Z], 0, i[BLOCK]))],
            out_specs=pl.BlockSpec((copies, nx, rows, cols), lambda g, i: (0, 0, 0, 0)),
        ),
        compiler_params=pltpu.CompilerParams(vmem_limit_bytes=16 * MB),
        name="project",
    )(info, own, other, *ws, residual)


def vocab_kernel(
    info_ref, mine_ref, theirs_ref, gain_ref, tok_ref, par_ref, w_ref, more_ref, hid_out, stat_ref, hid_ref, x_ref, rest_ref, sem
):
    lead, others = w_ref.shape[1], rest_ref.shape[1]
    load = pltpu.make_async_copy(more_ref.at[:, pl.ds(lead, others)], rest_ref, sem.at[1])
    load.start()
    core = info_ref[CORE]
    nz, nx, rows, cols = mine_ref.shape
    half = nx * cols
    for z in range(nz):
        rs = slice(z * rows, (z + 1) * rows)
        squares = jnp.zeros((rows, cols), F32)
        for x in range(nx):
            mine, theirs = mine_ref[z, x], theirs_ref[z, x]
            low = jnp.where(core == 0, mine, theirs)
            high = jnp.where(core == 0, theirs, mine)
            hid_ref[rs, x * cols:(x + 1) * cols] = low
            hid_ref[rs, half + x * cols:half + (x + 1) * cols] = high
            squares = squares + low.astype(F32) * low.astype(F32) + high.astype(F32) * high.astype(F32)
        inv = lax.rsqrt(jnp.sum(squares, axis=1, keepdims=True) / (2 * half) + 1e-06)
        for j in range(2 * nx):
            cs = slice(j * cols, (j + 1) * cols)
            x_ref[rs, cs] = (hid_ref[rs, cs].astype(F32) * inv * gain_ref[:, cs]).astype(BF)
    copy = pltpu.make_async_copy(hid_ref, hid_out, sem.at[0])
    copy.start()
    tokens = nz * rows
    reqs, tree = tok_ref.shape
    sums = jnp.zeros((tokens, 128), F32)
    pick1 = jnp.zeros((tokens, 128), F32)
    pick2 = jnp.zeros((tokens, 128), F32)
    pick0 = [jnp.zeros((8, 128), F32) for _ in range(reqs)]
    lane = lax.broadcasted_iota(jnp.int32, (tokens, 128), 1)
    base = info_ref[BASE]
    tok = jnp.concatenate([tok_ref[...].astype(F32), jnp.full((reqs, 128 - tree), -1.0, F32)], axis=1)
    tok = jnp.transpose(tok)
    column = lambda n: jnp.concatenate([tok[n:n + tree, r:r + 1] for r in range(reqs)], axis=0).astype(jnp.int32)
    t1 = column(1) - base - lane
    t2 = column(2) - base - lane
    node = lax.broadcasted_iota(jnp.int32, (8, 128), 0)
    t0 = [jnp.where(node == 0, tok[0:8, r:r + 1].astype(jnp.int32) - base - lane[:8], -1) for r in range(reqs)]
    parts = [(w_ref, at, min(256, lead - at), at) for at in range(0, lead, 256)]
    parts += [(rest_ref, at, min(256, others - at), lead + at) for at in range(0, others, 256)]
    for ref, start, step, at in parts:
        if at == lead:
            load.wait()
        logits = jnp.dot(x_ref[...], ref[:, start:start + step], preferred_element_type=F32)
        for o in range(0, step, 128):
            lg = logits[:, o:o + 128]
            sums = sums + jnp.exp(lg)
            pick1 = jnp.where(t1 == at + o, lg, pick1)
            pick2 = jnp.where(t2 == at + o, lg, pick2)
            for r in range(reqs):
                pick0[r] = jnp.where(t0[r] == at + o, lg[r * tree:r * tree + 8], pick0[r])
    zero = jnp.zeros((tree - 8, 128), F32)
    pick0 = jnp.concatenate([p for r in range(reqs) for p in (pick0[r], zero)], axis=0)

    def by_request(a):
        a = jnp.sum(jnp.transpose(a), axis=0, keepdims=True)
        return jnp.concatenate([a[:, r * tree:(r + 1) * tree] for r in range(reqs)], axis=0)

    def later(a, n):
        return jnp.concatenate([a[:, :n], a[:, :tree - n]], axis=1)

    total, pick1, pick2, pick0 = (by_request(a) for a in (sums, pick1, pick2, pick0))
    at_node = lax.broadcasted_iota(jnp.int32, (reqs, tree), 1)
    near = par_ref[...] == at_node - 1
    root = at_node == 0
    pick = jnp.where(root, pick0, jnp.where(near, later(pick1, 1), later(pick2, 2)))
    total = jnp.where(root, total, jnp.where(near, later(total, 1), later(total, 2)))
    gap = jnp.zeros((reqs, 64 - tree), F32)
    stats = jnp.concatenate([total, gap, pick, gap], axis=1)
    for i in range(stat_ref.shape[0]):
        stat_ref[i] = stats
    copy.wait()


def vocab(info, mine, theirs, gain, toks, parents, lead, w, copies):
    nz, nx, rows, cols = mine.shape
    tokens, width = nz * rows, 2 * nx * cols
    vm = pl.BlockSpec(memory_space=pltpu.VMEM)
    return pl.pallas_call(
        vocab_kernel,
        out_shape=(
            jax.ShapeDtypeStruct((tokens, width), BF),
            jax.ShapeDtypeStruct((copies, toks.shape[0], 128), F32),
        ),
        in_specs=[pl.BlockSpec(memory_space=pltpu.SMEM), vm, vm, vm, vm, vm, vm, pl.BlockSpec(memory_space=pl.ANY)],
        out_specs=(pl.BlockSpec(memory_space=pl.ANY), vm),
        scratch_shapes=[
            pltpu.VMEM((tokens, width), BF),
            pltpu.VMEM((tokens, width), BF),
            pltpu.VMEM((width, w.shape[1] - lead.shape[1]), BF),
            pltpu.SemaphoreType.DMA((2,)),
        ],
        compiler_params=pltpu.CompilerParams(vmem_limit_bytes=24 * MB),
        name="vocab",
    )(info, mine, theirs, gain, toks, parents, lead, pltpu.with_memory_space_constraint(w, pltpu.HBM))


def fetch_kernel(w_ref, after_ref, out_ref, sem):
    copy = pltpu.make_async_copy(w_ref.at[:, pl.ds(0, out_ref.shape[1])], out_ref, sem)
    copy.start()
    copy.wait()


def fetch(w, after, cols):
    hbm = pl.BlockSpec(memory_space=pl.ANY)
    return pl.pallas_call(
        fetch_kernel,
        out_shape=jax.ShapeDtypeStruct((w.shape[0], cols), w.dtype),
        in_specs=[hbm, hbm],
        out_specs=pl.BlockSpec(memory_space=pltpu.VMEM),
        scratch_shapes=[pltpu.SemaphoreType.DMA],
        compiler_params=pltpu.CompilerParams(vmem_limit_bytes=2 * MB),
        name="fetch",
    )(pltpu.with_memory_space_constraint(w, pltpu.HBM), after)


def shifted(a, axis, step):
    n = lax.axis_size(axis)
    return lax.ppermute(a, axis, [(i, (i + step) % n) for i in range(n)])


def local(
    queries, new_keys, new_values, cache_keys, cache_values, lengths, parents,
    tree_tokens, residual, out_weight, norm_gain, vocab_weight,
):
    reqs, tree, width = queries.shape
    slots = cache_keys.shape[1]
    y, z, x, core = (lax.axis_index(a) for a in ("dp", "z", "x", "core"))
    ny, nz, nx, nc = (lax.axis_size(a) for a in ("dp", "z", "x", "core"))
    shard = (z * nx + x) * nc + core
    shards = nz * nx * nc
    window = slots * shards // 2
    half = width // nc
    block = half // nx
    tokens = reqs * tree
    swap = [(0, 1), (1, 0)]
    treq = jnp.where((shard >= reqs) & (shard < 2 * reqs), shard - reqs, -1)
    info = jnp.stack([core, shard * slots, treq, z, x, core * nx + x, y, shard * vocab_weight.shape[1]]).astype(jnp.int32)

    args = (lengths, parents, queries, cache_keys, cache_values, new_keys, new_values)
    spread = (nz, nx, nc, out_weight.shape[0], block)
    send, w = attend_half(window, info, *args, w=out_weight, spread=spread)
    got = lax.ppermute(send, "core", swap)
    w = lax.all_to_all(w.reshape(shards, -1, block), ("z", "x", "core"), 0, 0).reshape(-1, block)
    ws = [w] + [shifted(w, "dp", s) for s in range(1, ny)]
    (part,) = attend_half(window, info, *args, got=got)
    part = lax.all_to_all(part, ("z", "x"), 0, 0)
    att = combine(part, tokens // (nz * nx), half)
    own = pile([att] + [shifted(att, "x", s) for s in range(1, nx)], ws)
    other = lax.ppermute(own, "core", swap)
    hid = project(info, own, other, ws, residual, nz * nx).reshape(nz * nx, -1, block)
    hid = lax.all_to_all(hid, ("z", "x"), 0, 0).reshape(nz, nx, -1, block)
    other = lax.ppermute(hid, "core", swap)
    scorer = fetch(vocab_weight, hid, 1536)
    hidden, stats = vocab(info, hid, other, norm_gain.reshape(1, -1), tree_tokens, parents, scorer, vocab_weight, shards)
    stats = jnp.sum(lax.all_to_all(stats, ("z", "x", "core"), 0, 0), axis=0)
    logprob = stats[:, 64:64 + tree] - jnp.log(stats[:, :tree])
    return hidden.reshape(reqs, tree, width), logprob


def solution(mesh):
    sizes = (mesh.shape["dp"], 4, 4, 2)
    grid = Mesh(mesh.devices.reshape(sizes), ("dp", "z", "x", "core"))
    mp = ("z", "x", "core")
    row = P("dp", None, None)
    placed = (
        row, row, row, P("dp", mp, None), P("dp", mp, None), P("dp"), P("dp", None), P("dp", None), row,
        P(("dp",) + mp, None), P(), P(None, mp),
    )
    return jax.shard_map(local, mesh=grid, in_specs=placed, out_specs=(row, P("dp", None)), check_vma=False)
```

```python
import functools

import jax
import jax.numpy as jnp
from jax import lax
from jax.experimental import pallas as pl
from jax.experimental.pallas import tpu as pltpu
from jax.sharding import Mesh, PartitionSpec as P

HEADS = 16
SINK = 4
BF = jnp.bfloat16
F32 = jnp.float32
NT = (((1,), (1,)), ((), ()))
TN = (((0,), (0,)), ((), ()))
CORE, FIRST, TREQ, Z, X, BLOCK, DP, BASE = range(8)
MB = 1 << 20


def attend_kernel(window, add, info_ref, len_ref, par_ref, q_ref, k_ref, v_ref, nk_ref, nv_ref, *refs):
    step = pl.program_id(0)
    if add:
        got_ref, out_ref, anc_ref, new_ref, sem = refs
    else:
        w_ref, out_ref, spread_hbm, anc_ref, new_ref, sem, spread_ref, spread_sem = refs
        nz, nx, nc, _, block = spread_ref.shape
        leave = pltpu.make_async_copy(spread_ref, spread_hbm, spread_sem)

        @pl.when(step == 0)
        def _():
            for c in range(nc):
                for x in range(nx):
                    at = (c * nx + x) * block
                    for z in range(nz):
                        spread_ref[z, x, c] = w_ref[:, at:at + block]
            leave.start()

    first = info_ref[FIRST]
    treq = info_ref[TREQ]
    reqs, tree, width = q_ref.shape
    slots = k_ref.shape[1]
    heads = width // 128
    part = tree // 2
    scale = 128 ** (-0.5) * 1.4426950408889634
    zero = jnp.zeros((tree, 128), BF)
    pairs = [slice(p * 256, (p + 1) * 256) for p in range(heads // 2)]

    def score(r, keys):
        out = []
        for cols in pairs:
            q = q_ref[r, :, cols]
            q = jnp.concatenate(
                [jnp.concatenate([q[:, :128], zero], axis=1), jnp.concatenate([zero, q[:, 128:]], axis=1)], axis=0
            )
            out.append(lax.dot_general(keys(cols), q, NT, preferred_element_type=F32))
        return out

    def weigh(scores, mask):
        exps = [jnp.where(mask, jnp.exp2(s * scale), 0.0) for s in scores]
        dens = [jnp.sum(e, axis=0, keepdims=True) for e in exps]
        dens = [d[:, t * tree:(t + 1) * tree] for d in dens for t in range(2)]
        return [e.astype(BF) for e in exps], jnp.concatenate(dens, axis=0)

    def finish(r, exps, dens, values):
        for p, cols in enumerate(pairs):
            o = lax.dot_general(exps[p], values(cols), TN, preferred_element_type=F32)
            for h, val in ((2 * p, o[:tree, :128]), (2 * p + 1, o[tree:, 128:])):
                for t in range(2):
                    rows = slice(h * part, (h + 1) * part)
                    half = val[t * part:(t + 1) * part]
                    if add:
                        half = half + got_ref[2 * r + t, rows].astype(F32)
                    out_ref[2 * r + t, rows] = half.astype(BF)
        gap = jnp.zeros((heads, 64 - part), F32)
        for t in range(2):
            den = dens[:, t * part:(t + 1) * part]
            if add:
                got = got_ref[2 * r + t, heads * part:].astype(F32)
                den = den + got[:, :part] + got[:, 64:64 + part]
            high = den.astype(BF).astype(F32)
            out_ref[2 * r + t, heads * part:] = jnp.concatenate([high, gap, den - high, gap], axis=1).astype(BF)

    @pl.when(treq < 0)
    def _():
        pos = first + lax.broadcasted_iota(jnp.int32, (slots, 2 * tree), 0)
        scores = [score(r, lambda cols: k_ref[r, :, cols]) for r in range(reqs)]
        weights = []
        for r in range(reqs):
            length = len_ref[step * reqs + r]
            mask = (pos < length) & ((pos < SINK) | (pos >= length - window))
            weights.append(weigh(scores[r], mask))
        for r in range(reqs):
            finish(r, *weights[r], lambda cols: v_ref[r, :, cols])

    @pl.when(treq >= 0)
    def _():
        out_ref[...] = got_ref[...] if add else jnp.zeros_like(out_ref)

        @pl.when(treq // reqs == step)
        def _():
            half = info_ref[CORE] if add else 1 - info_ref[CORE]
            at = pl.ds(pl.multiple_of(half * width, 128), width)
            copies = [
                pltpu.make_async_copy(ref.at[treq, :, at], new_ref.at[i], sem.at[i])
                for i, ref in enumerate((nk_ref, nv_ref))
            ]
            for copy in copies:
                copy.start()
            node = lax.broadcasted_iota(jnp.int32, (1, 128), 1)
            anc_ref[...] = jnp.zeros_like(anc_ref)
            anc_ref[0:1, :] = jnp.where(node == 0, 1.0, 0.0)

            def body(i, carry):
                up = anc_ref[pl.ds(par_ref[treq, i], 1), :]
                anc_ref[pl.ds(i, 1), :] = jnp.where(node == i, 1.0, up)
                return carry

            lax.fori_loop(1, tree, body, 0)
            mask = jnp.transpose(anc_ref[...])[:tree, :tree]
            mask = jnp.concatenate([mask, mask], axis=1) > 0.5
            r = lax.rem(treq, reqs)
            for copy in copies:
                copy.wait()
            weights = weigh(score(r, lambda cols: new_ref[0, :, cols]), mask)
            finish(r, *weights, lambda cols: new_ref[1, :, cols])

    if not add:

        @pl.when(step == pl.num_programs(0) - 1)
        def _():
            leave.wait()


def attend_half(window, info, lengths, parents, q, k, v, nk, nv, got=None, w=None, spread=None):
    reqs, tree, width = q.shape
    slots = k.shape[1]
    half = width // 2
    group = reqs // 2
    add = got is not None
    hidx = (lambda i: i[CORE]) if add else (lambda i: 1 - i[CORE])
    qs = pl.BlockSpec((group, tree, half), lambda r, i, l, p: (r, 0, hidx(i)))
    ks = pl.BlockSpec((group, slots, half), lambda r, i, l, p: (r, 0, hidx(i)))
    ns = pl.BlockSpec(memory_space=pl.ANY)
    lengths, parents, q, k, v, nk, nv = (
        pltpu.with_memory_space_constraint(a, pltpu.HBM) for a in (lengths, parents, q, k, v, nk, nv)
    )
    rows = half // 128 * (tree // 2) + half // 128
    sums = pl.BlockSpec((2 * group, rows, 128), lambda r, i, l, p: (r, 0, 0))
    in_specs = [qs, ks, ks, ns, ns]
    out_specs = [sums]
    out_shape = [jax.ShapeDtypeStruct((2 * reqs, rows, 128), BF)]
    scratch = [pltpu.VMEM((128, 128), F32), pltpu.VMEM((2, tree, half), BF), pltpu.SemaphoreType.DMA((2,))]
    if add:
        extra = (got,)
        in_specs.append(sums)
    else:
        extra = (pltpu.with_memory_space_constraint(w, pltpu.HBM),)
        in_specs.append(pl.BlockSpec(w.shape, lambda r, i, l, p: (0, 0)))
        out_specs.append(pl.BlockSpec(memory_space=pl.ANY))
        scratch += [pltpu.VMEM(spread, w.dtype), pltpu.SemaphoreType.DMA]
        out_shape.append(jax.ShapeDtypeStruct(spread, w.dtype))
    return pl.pallas_call(
        functools.partial(attend_kernel, window, add),
        out_shape=out_shape,
        grid_spec=pltpu.PrefetchScalarGridSpec(
            num_scalar_prefetch=3,
            grid=(reqs // group,),
            in_specs=in_specs,
            out_specs=out_specs,
            scratch_shapes=scratch,
        ),
        compiler_params=pltpu.CompilerParams(vmem_limit_bytes=24 * MB),
        name="attend_mine" if add else "attend_theirs",
    )(info, lengths, parents, q, k, v, nk, nv, *extra)


def combine_kernel(parts_ref, out_ref):
    rows, width = out_ref.shape
    heads = width // 128
    total = jnp.sum(parts_ref[...].astype(F32), axis=0)
    den = total[heads * rows:]
    den = jnp.concatenate([den[:, :rows] + den[:, 64:64 + rows], jnp.ones((heads, 128 - rows), F32)], axis=1)
    den = jnp.transpose(jnp.concatenate([den, jnp.ones((128 - heads, 128), F32)], axis=0))
    for h in range(heads):
        val = total[h * rows:(h + 1) * rows] / den[:rows, h:h + 1]
        out_ref[:, h * 128:(h + 1) * 128] = val.astype(BF)


def combine(parts, rows, width):
    return pl.pallas_call(
        combine_kernel,
        out_shape=jax.ShapeDtypeStruct((rows, width), BF),
        compiler_params=pltpu.CompilerParams(vmem_limit_bytes=16 * MB),
        name="combine",
    )(parts)


def pile_kernel(n, *refs):
    for i in range(n):
        refs[-1][i] = refs[i][...]


def pile(arrays, after):
    shape = (len(arrays),) + arrays[0].shape
    vm = pl.BlockSpec(memory_space=pltpu.VMEM)
    return pl.pallas_call(
        functools.partial(pile_kernel, len(arrays)),
        out_shape=jax.ShapeDtypeStruct(shape, arrays[0].dtype),
        in_specs=[vm] * len(arrays) + [pl.BlockSpec(memory_space=pl.ANY)] * len(after),
        out_specs=vm,
        compiler_params=pltpu.CompilerParams(vmem_limit_bytes=2 * MB),
        name="pile",
    )(*arrays, *after)


def project_kernel(info_ref, own, other, *refs):
    ws, (res_ref, out_ref) = refs[:-2], refs[-2:]
    core, x, y = info_ref[CORE], info_ref[X], info_ref[DP]
    nx, rows, half = own.shape
    ny, deep = len(ws), ws[0].shape[0]
    mine = jnp.concatenate([own[s] for s in range(nx)], axis=0)
    theirs = jnp.concatenate([other[s] for s in range(nx)], axis=0)
    acc = None
    for s in range(ny):
        at = lax.rem(y + ny - s, ny)
        a = jnp.where(core == at // 2, mine, theirs)
        a = jnp.where(at % 2 == 0, a[:, :deep], a[:, deep:])
        part = jnp.dot(a, ws[s][...], preferred_element_type=F32)
        acc = part if acc is None else acc + part
    for s in range(nx):
        at = lax.rem(x + nx - s, nx)
        hid = (res_ref[at].astype(F32) + acc[s * rows:(s + 1) * rows]).astype(BF)
        for i in range(out_ref.shape[0]):
            out_ref[i, at] = hid


def project(info, own, other, ws, residual, copies):
    nx, rows, half = own.shape
    cols = ws[0].shape[1]
    part = pl.BlockSpec((nx, rows, half), lambda g, i: (0, 0, 0))
    residual = pltpu.with_memory_space_constraint(residual.reshape(-1, rows, residual.shape[2]), pltpu.HBM)
    return pl.pallas_call(
        project_kernel,
        out_shape=jax.ShapeDtypeStruct((copies, nx, rows, cols), BF),
        grid_spec=pltpu.PrefetchScalarGridSpec(
            num_scalar_prefetch=1,
            grid=(1,),
            in_specs=[part, part]
            + [pl.BlockSpec(w.shape, lambda g, i: (0, 0)) for w in ws]
            + [pl.BlockSpec((nx, rows, cols), lambda g, i: (i[Z], 0, i[BLOCK]))],
            out_specs=pl.BlockSpec((copies, nx, rows, cols), lambda g, i: (0, 0, 0, 0)),
        ),
        compiler_params=pltpu.CompilerParams(vmem_limit_bytes=16 * MB),
        name="project",
    )(info, own, other, *ws, residual)


def vocab_kernel(
    info_ref, mine_ref, theirs_ref, gain_ref, tok_ref, par_ref, w_ref, more_ref, hid_out, stat_ref, hid_ref, x_ref, rest_ref, sem
):
    lead, others = w_ref.shape[1], rest_ref.shape[1]
    load = pltpu.make_async_copy(more_ref.at[:, pl.ds(lead, others)], rest_ref, sem.at[1])
    load.start()
    core = info_ref[CORE]
    nz, nx, rows, cols = mine_ref.shape
    half = nx * cols
    for z in range(nz):
        rs = slice(z * rows, (z + 1) * rows)
        squares = jnp.zeros((rows, cols), F32)
        for x in range(nx):
            mine, theirs = mine_ref[z, x], theirs_ref[z, x]
            low = jnp.where(core == 0, mine, theirs)
            high = jnp.where(core == 0, theirs, mine)
            hid_ref[rs, x * cols:(x + 1) * cols] = low
            hid_ref[rs, half + x * cols:half + (x + 1) * cols] = high
            squares = squares + low.astype(F32) * low.astype(F32) + high.astype(F32) * high.astype(F32)
        inv = lax.rsqrt(jnp.sum(squares, axis=1, keepdims=True) / (2 * half) + 1e-06)
        for j in range(2 * nx):
            cs = slice(j * cols, (j + 1) * cols)
            x_ref[rs, cs] = (hid_ref[rs, cs].astype(F32) * inv * gain_ref[:, cs]).astype(BF)
    copy = pltpu.make_async_copy(hid_ref, hid_out, sem.at[0])
    copy.start()
    tokens = nz * rows
    reqs, tree = tok_ref.shape
    sums = jnp.zeros((tokens, 128), F32)
    pick1 = jnp.zeros((tokens, 128), F32)
    pick2 = jnp.zeros((tokens, 128), F32)
    pick0 = [jnp.zeros((8, 128), F32) for _ in range(reqs)]
    lane = lax.broadcasted_iota(jnp.int32, (tokens, 128), 1)
    base = info_ref[BASE]
    tok = jnp.concatenate([tok_ref[...].astype(F32), jnp.full((reqs, 128 - tree), -1.0, F32)], axis=1)
    tok = jnp.transpose(tok)
    column = lambda n: jnp.concatenate([tok[n:n + tree, r:r + 1] for r in range(reqs)], axis=0).astype(jnp.int32)
    t1 = column(1) - base - lane
    t2 = column(2) - base - lane
    node = lax.broadcasted_iota(jnp.int32, (8, 128), 0)
    t0 = [jnp.where(node == 0, tok[0:8, r:r + 1].astype(jnp.int32) - base - lane[:8], -1) for r in range(reqs)]
    parts = [(w_ref, at, min(256, lead - at), at) for at in range(0, lead, 256)]
    parts += [(rest_ref, at, min(256, others - at), lead + at) for at in range(0, others, 256)]
    for ref, start, step, at in parts:
        if at == lead:
            load.wait()
        logits = jnp.dot(x_ref[...], ref[:, start:start + step], preferred_element_type=F32)
        for o in range(0, step, 128):
            lg = logits[:, o:o + 128]
            sums = sums + jnp.exp(lg)
            pick1 = jnp.where(t1 == at + o, lg, pick1)
            pick2 = jnp.where(t2 == at + o, lg, pick2)
            for r in range(reqs):
                pick0[r] = jnp.where(t0[r] == at + o, lg[r * tree:r * tree + 8], pick0[r])
    zero = jnp.zeros((tree - 8, 128), F32)
    pick0 = jnp.concatenate([p for r in range(reqs) for p in (pick0[r], zero)], axis=0)

    def by_request(a):
        a = jnp.sum(jnp.transpose(a), axis=0, keepdims=True)
        return jnp.concatenate([a[:, r * tree:(r + 1) * tree] for r in range(reqs)], axis=0)

    def later(a, n):
        return jnp.concatenate([a[:, :n], a[:, :tree - n]], axis=1)

    total, pick1, pick2, pick0 = (by_request(a) for a in (sums, pick1, pick2, pick0))
    at_node = lax.broadcasted_iota(jnp.int32, (reqs, tree), 1)
    near = par_ref[...] == at_node - 1
    root = at_node == 0
    pick = jnp.where(root, pick0, jnp.where(near, later(pick1, 1), later(pick2, 2)))
    total = jnp.where(root, total, jnp.where(near, later(total, 1), later(total, 2)))
    gap = jnp.zeros((reqs, 64 - tree), F32)
    stats = jnp.concatenate([total, gap, pick, gap], axis=1)
    for i in range(stat_ref.shape[0]):
        stat_ref[i] = stats
    copy.wait()


def vocab(info, mine, theirs, gain, toks, parents, lead, w, copies):
    nz, nx, rows, cols = mine.shape
    tokens, width = nz * rows, 2 * nx * cols
    vm = pl.BlockSpec(memory_space=pltpu.VMEM)
    return pl.pallas_call(
        vocab_kernel,
        out_shape=(
            jax.ShapeDtypeStruct((tokens, width), BF),
            jax.ShapeDtypeStruct((copies, toks.shape[0], 128), F32),
        ),
        in_specs=[pl.BlockSpec(memory_space=pltpu.SMEM), vm, vm, vm, vm, vm, vm, pl.BlockSpec(memory_space=pl.ANY)],
        out_specs=(pl.BlockSpec(memory_space=pl.ANY), vm),
        scratch_shapes=[
            pltpu.VMEM((tokens, width), BF),
            pltpu.VMEM((tokens, width), BF),
            pltpu.VMEM((width, w.shape[1] - lead.shape[1]), BF),
            pltpu.SemaphoreType.DMA((2,)),
        ],
        compiler_params=pltpu.CompilerParams(vmem_limit_bytes=24 * MB),
        name="vocab",
    )(info, mine, theirs, gain, toks, parents, lead, pltpu.with_memory_space_constraint(w, pltpu.HBM))


def fetch_kernel(w_ref, after_ref, out_ref, sem):
    copy = pltpu.make_async_copy(w_ref.at[:, pl.ds(0, out_ref.shape[1])], out_ref, sem)
    copy.start()
    copy.wait()


def fetch(w, after, cols):
    hbm = pl.BlockSpec(memory_space=pl.ANY)
    return pl.pallas_call(
        fetch_kernel,
        out_shape=jax.ShapeDtypeStruct((w.shape[0], cols), w.dtype),
        in_specs=[hbm, hbm],
        out_specs=pl.BlockSpec(memory_space=pltpu.VMEM),
        scratch_shapes=[pltpu.SemaphoreType.DMA],
        compiler_params=pltpu.CompilerParams(vmem_limit_bytes=2 * MB),
        name="fetch",
    )(pltpu.with_memory_space_constraint(w, pltpu.HBM), after)


def shifted(a, axis, step):
    n = lax.axis_size(axis)
    return lax.ppermute(a, axis, [(i, (i + step) % n) for i in range(n)])


def local(
    queries, new_keys, new_values, cache_keys, cache_values, lengths, parents,
    tree_tokens, residual, out_weight, norm_gain, vocab_weight,
):
    reqs, tree, width = queries.shape
    slots = cache_keys.shape[1]
    y, z, x, core = (lax.axis_index(a) for a in ("dp", "z", "x", "core"))
    ny, nz, nx, nc = (lax.axis_size(a) for a in ("dp", "z", "x", "core"))
    shard = (z * nx + x) * nc + core
    shards = nz * nx * nc
    window = slots * shards // 2
    half = width // nc
    block = half // nx
    tokens = reqs * tree
    swap = [(0, 1), (1, 0)]
    treq = jnp.where((shard >= reqs) & (shard < 2 * reqs), shard - reqs, -1)
    info = jnp.stack([core, shard * slots, treq, z, x, core * nx + x, y, shard * vocab_weight.shape[1]]).astype(jnp.int32)

    args = (lengths, parents, queries, cache_keys, cache_values, new_keys, new_values)
    spread = (nz, nx, nc, out_weight.shape[0], block)
    send, w = attend_half(window, info, *args, w=out_weight, spread=spread)
    got = lax.ppermute(send, "core", swap)
    w = lax.all_to_all(w.reshape(shards, -1, block), ("z", "x", "core"), 0, 0).reshape(-1, block)
    ws = [w] + [shifted(w, "dp", s) for s in range(1, ny)]
    (part,) = attend_half(window, info, *args, got=got)
    part = lax.all_to_all(part, ("z", "x"), 0, 0)
    att = combine(part, tokens // (nz * nx), half)
    own = pile([att] + [shifted(att, "x", s) for s in range(1, nx)], ws)
    other = lax.ppermute(own, "core", swap)
    hid = project(info, own, other, ws, residual, nz * nx).reshape(nz * nx, -1, block)
    hid = lax.all_to_all(hid, ("z", "x"), 0, 0).reshape(nz, nx, -1, block)
    other = lax.ppermute(hid, "core", swap)
    scorer = fetch(vocab_weight, hid, 1536)
    hidden, stats = vocab(info, hid, other, norm_gain.reshape(1, -1), tree_tokens, parents, scorer, vocab_weight, shards)
    stats = jnp.sum(lax.all_to_all(stats, ("z", "x", "core"), 0, 0), axis=0)
    logprob = stats[:, 64:64 + tree] - jnp.log(stats[:, :tree])
    return hidden.reshape(reqs, tree, width), logprob


def solution(mesh):
    sizes = (mesh.shape["dp"], 4, 4, 2)
    grid = Mesh(mesh.devices.reshape(sizes), ("dp", "z", "x", "core"))
    mp = ("z", "x", "core")
    row = P("dp", None, None)
    placed = (
        row, row, row, P("dp", mp, None), P("dp", mp, None), P("dp"), P("dp", None), P("dp", None), row,
        P(("dp",) + mp, None), P(), P(None, mp),
    )
    return jax.shard_map(local, mesh=grid, in_specs=placed, out_specs=(row, P("dp", None)), check_vma=False)
```

```python
import functools

import jax
import jax.numpy as jnp
from jax import lax
from jax.experimental import pallas as pl
from jax.experimental.pallas import tpu as pltpu
from jax.sharding import Mesh, PartitionSpec as P

HEADS = 16
SINK = 4
BF = jnp.bfloat16
F32 = jnp.float32
NT = (((1,), (1,)), ((), ()))
TN = (((0,), (0,)), ((), ()))
CORE, FIRST, TREQ, Z, X, BLOCK, DP, BASE = range(8)
MB = 1 << 20


def attend_kernel(window, add, info_ref, len_ref, par_ref, q_ref, k_ref, v_ref, nk_ref, nv_ref, *refs):
    step = pl.program_id(0)
    if add:
        got_ref, out_ref, anc_ref, new_ref, sem = refs
    else:
        w_ref, out_ref, spread_hbm, anc_ref, new_ref, sem, spread_ref, spread_sem = refs
        nz, nx, nc, _, block = spread_ref.shape
        leave = pltpu.make_async_copy(spread_ref, spread_hbm, spread_sem)

        @pl.when(step == 0)
        def _():
            for c in range(nc):
                for x in range(nx):
                    at = (c * nx + x) * block
                    for z in range(nz):
                        spread_ref[z, x, c] = w_ref[:, at:at + block]
            leave.start()

    first = info_ref[FIRST]
    treq = info_ref[TREQ]
    reqs, tree, width = q_ref.shape
    slots = k_ref.shape[1]
    heads = width // 128
    part = tree // 2
    scale = 128 ** (-0.5) * 1.4426950408889634
    zero = jnp.zeros((tree, 128), BF)
    pairs = [slice(p * 256, (p + 1) * 256) for p in range(heads // 2)]

    def score(r, keys):
        out = []
        for cols in pairs:
            q = q_ref[r, :, cols]
            q = jnp.concatenate(
                [jnp.concatenate([q[:, :128], zero], axis=1), jnp.concatenate([zero, q[:, 128:]], axis=1)], axis=0
            )
            out.append(lax.dot_general(keys(cols), q, NT, preferred_element_type=F32))
        return out

    def weigh(scores, mask):
        exps = [jnp.where(mask, jnp.exp2(s * scale), 0.0) for s in scores]
        dens = [jnp.sum(e, axis=0, keepdims=True) for e in exps]
        dens = [d[:, t * tree:(t + 1) * tree] for d in dens for t in range(2)]
        return [e.astype(BF) for e in exps], jnp.concatenate(dens, axis=0)

    def finish(r, exps, dens, values):
        for p, cols in enumerate(pairs):
            o = lax.dot_general(exps[p], values(cols), TN, preferred_element_type=F32)
            for h, val in ((2 * p, o[:tree, :128]), (2 * p + 1, o[tree:, 128:])):
                for t in range(2):
                    rows = slice(h * part, (h + 1) * part)
                    half = val[t * part:(t + 1) * part]
                    if add:
                        half = half + got_ref[2 * r + t, rows].astype(F32)
                    out_ref[2 * r + t, rows] = half.astype(BF)
        gap = jnp.zeros((heads, 64 - part), F32)
        for t in range(2):
            den = dens[:, t * part:(t + 1) * part]
            if add:
                got = got_ref[2 * r + t, heads * part:].astype(F32)
                den = den + got[:, :part] + got[:, 64:64 + part]
            high = den.astype(BF).astype(F32)
            out_ref[2 * r + t, heads * part:] = jnp.concatenate([high, gap, den - high, gap], axis=1).astype(BF)

    @pl.when(treq < 0)
    def _():
        pos = first + lax.broadcasted_iota(jnp.int32, (slots, 2 * tree), 0)
        scores = [score(r, lambda cols: k_ref[r, :, cols]) for r in range(reqs)]
        weights = []
        for r in range(reqs):
            length = len_ref[step * reqs + r]
            mask = (pos < length) & ((pos < SINK) | (pos >= length - window))
            weights.append(weigh(scores[r], mask))
        for r in range(reqs):
            finish(r, *weights[r], lambda cols: v_ref[r, :, cols])

    @pl.when(treq >= 0)
    def _():
        out_ref[...] = got_ref[...] if add else jnp.zeros_like(out_ref)

        @pl.when(treq // reqs == step)
        def _():
            half = info_ref[CORE] if add else 1 - info_ref[CORE]
            at = pl.ds(pl.multiple_of(half * width, 128), width)
            copies = [
                pltpu.make_async_copy(ref.at[treq, :, at], new_ref.at[i], sem.at[i])
                for i, ref in enumerate((nk_ref, nv_ref))
            ]
            for copy in copies:
                copy.start()
            node = lax.broadcasted_iota(jnp.int32, (1, 128), 1)
            anc_ref[...] = jnp.zeros_like(anc_ref)
            anc_ref[0:1, :] = jnp.where(node == 0, 1.0, 0.0)

            def body(i, carry):
                up = anc_ref[pl.ds(par_ref[treq, i], 1), :]
                anc_ref[pl.ds(i, 1), :] = jnp.where(node == i, 1.0, up)
                return carry

            lax.fori_loop(1, tree, body, 0)
            mask = jnp.transpose(anc_ref[...])[:tree, :tree]
            mask = jnp.concatenate([mask, mask], axis=1) > 0.5
            r = lax.rem(treq, reqs)
            for copy in copies:
                copy.wait()
            weights = weigh(score(r, lambda cols: new_ref[0, :, cols]), mask)
            finish(r, *weights, lambda cols: new_ref[1, :, cols])

    if not add:

        @pl.when(step == pl.num_programs(0) - 1)
        def _():
            leave.wait()


def attend_half(window, info, lengths, parents, q, k, v, nk, nv, got=None, w=None, spread=None):
    reqs, tree, width = q.shape
    slots = k.shape[1]
    half = width // 2
    group = reqs // 2
    add = got is not None
    hidx = (lambda i: i[CORE]) if add else (lambda i: 1 - i[CORE])
    qs = pl.BlockSpec((group, tree, half), lambda r, i, l, p: (r, 0, hidx(i)))
    ks = pl.BlockSpec((group, slots, half), lambda r, i, l, p: (r, 0, hidx(i)))
    ns = pl.BlockSpec(memory_space=pl.ANY)
    lengths, parents, q, k, v, nk, nv = (
        pltpu.with_memory_space_constraint(a, pltpu.HBM) for a in (lengths, parents, q, k, v, nk, nv)
    )
    rows = half // 128 * (tree // 2) + half // 128
    sums = pl.BlockSpec((2 * group, rows, 128), lambda r, i, l, p: (r, 0, 0))
    in_specs = [qs, ks, ks, ns, ns]
    out_specs = [sums]
    out_shape = [jax.ShapeDtypeStruct((2 * reqs, rows, 128), BF)]
    scratch = [pltpu.VMEM((128, 128), F32), pltpu.VMEM((2, tree, half), BF), pltpu.SemaphoreType.DMA((2,))]
    if add:
        extra = (got,)
        in_specs.append(sums)
    else:
        extra = (pltpu.with_memory_space_constraint(w, pltpu.HBM),)
        in_specs.append(pl.BlockSpec(w.shape, lambda r, i, l, p: (0, 0)))
        out_specs.append(pl.BlockSpec(memory_space=pl.ANY))
        scratch += [pltpu.VMEM(spread, w.dtype), pltpu.SemaphoreType.DMA]
        out_shape.append(jax.ShapeDtypeStruct(spread, w.dtype))
    return pl.pallas_call(
        functools.partial(attend_kernel, window, add),
        out_shape=out_shape,
        grid_spec=pltpu.PrefetchScalarGridSpec(
            num_scalar_prefetch=3,
            grid=(reqs // group,),
            in_specs=in_specs,
            out_specs=out_specs,
            scratch_shapes=scratch,
        ),
        compiler_params=pltpu.CompilerParams(vmem_limit_bytes=24 * MB),
        name="attend_mine" if add else "attend_theirs",
    )(info, lengths, parents, q, k, v, nk, nv, *extra)


def combine_kernel(parts_ref, out_ref):
    rows, width = out_ref.shape
    heads = width // 128
    total = jnp.sum(parts_ref[...].astype(F32), axis=0)
    den = total[heads * rows:]
    den = jnp.concatenate([den[:, :rows] + den[:, 64:64 + rows], jnp.ones((heads, 128 - rows), F32)], axis=1)
    den = jnp.transpose(jnp.concatenate([den, jnp.ones((128 - heads, 128), F32)], axis=0))
    for h in range(heads):
        val = total[h * rows:(h + 1) * rows] / den[:rows, h:h + 1]
        out_ref[:, h * 128:(h + 1) * 128] = val.astype(BF)


def combine(parts, rows, width):
    return pl.pallas_call(
        combine_kernel,
        out_shape=jax.ShapeDtypeStruct((rows, width), BF),
        compiler_params=pltpu.CompilerParams(vmem_limit_bytes=16 * MB),
        name="combine",
    )(parts)


def pile_kernel(n, *refs):
    for i in range(n):
        refs[-1][i] = refs[i][...]


def pile(arrays, after):
    shape = (len(arrays),) + arrays[0].shape
    vm = pl.BlockSpec(memory_space=pltpu.VMEM)
    return pl.pallas_call(
        functools.partial(pile_kernel, len(arrays)),
        out_shape=jax.ShapeDtypeStruct(shape, arrays[0].dtype),
        in_specs=[vm] * len(arrays) + [pl.BlockSpec(memory_space=pl.ANY)] * len(after),
        out_specs=vm,
        compiler_params=pltpu.CompilerParams(vmem_limit_bytes=2 * MB),
        name="pile",
    )(*arrays, *after)


def project_kernel(info_ref, own, other, *refs):
    ws, (res_ref, out_ref) = refs[:-2], refs[-2:]
    core, x, y = info_ref[CORE], info_ref[X], info_ref[DP]
    nx, rows, half = own.shape
    ny, deep = len(ws), ws[0].shape[0]
    mine = jnp.concatenate([own[s] for s in range(nx)], axis=0)
    theirs = jnp.concatenate([other[s] for s in range(nx)], axis=0)
    acc = None
    for s in range(ny):
        at = lax.rem(y + ny - s, ny)
        a = jnp.where(core == at // 2, mine, theirs)
        a = jnp.where(at % 2 == 0, a[:, :deep], a[:, deep:])
        part = jnp.dot(a, ws[s][...], preferred_element_type=F32)
        acc = part if acc is None else acc + part
    for s in range(nx):
        at = lax.rem(x + nx - s, nx)
        hid = (res_ref[at].astype(F32) + acc[s * rows:(s + 1) * rows]).astype(BF)
        for i in range(out_ref.shape[0]):
            out_ref[i, at] = hid


def project(info, own, other, ws, residual, copies):
    nx, rows, _ = own.shape
    vm = pl.BlockSpec(memory_space=pltpu.VMEM)
    return pl.pallas_call(
        project_kernel,
        out_shape=jax.ShapeDtypeStruct((copies, nx, rows, ws[0].shape[1]), BF),
        in_specs=[pl.BlockSpec(memory_space=pltpu.SMEM)] + [vm] * (3 + len(ws)),
        out_specs=vm,
        compiler_params=pltpu.CompilerParams(vmem_limit_bytes=8 * MB),
        name="project",
    )(info, own, other, *ws, residual)


def vocab_kernel(
    info_ref, mine_ref, theirs_ref, gain_ref, tok_ref, par_ref, w_ref, more_ref, hid_out, stat_ref, hid_ref, x_ref, rest_ref, sem
):
    lead, others = w_ref.shape[1], rest_ref.shape[1]
    load = pltpu.make_async_copy(more_ref.at[:, pl.ds(lead, others)], rest_ref, sem.at[1])
    load.start()
    core = info_ref[CORE]
    nz, nx, rows, cols = mine_ref.shape
    half = nx * cols
    for z in range(nz):
        rs = slice(z * rows, (z + 1) * rows)
        squares = jnp.zeros((rows, cols), F32)
        for x in range(nx):
            mine, theirs = mine_ref[z, x], theirs_ref[z, x]
            low = jnp.where(core == 0, mine, theirs)
            high = jnp.where(core == 0, theirs, mine)
            hid_ref[rs, x * cols:(x + 1) * cols] = low
            hid_ref[rs, half + x * cols:half + (x + 1) * cols] = high
            squares = squares + low.astype(F32) * low.astype(F32) + high.astype(F32) * high.astype(F32)
        inv = lax.rsqrt(jnp.sum(squares, axis=1, keepdims=True) / (2 * half) + 1e-06)
        for j in range(2 * nx):
            cs = slice(j * cols, (j + 1) * cols)
            x_ref[rs, cs] = (hid_ref[rs, cs].astype(F32) * inv * gain_ref[:, cs]).astype(BF)
    copy = pltpu.make_async_copy(hid_ref, hid_out, sem.at[0])
    copy.start()
    tokens = nz * rows
    reqs, tree = tok_ref.shape
    sums = jnp.zeros((tokens, 128), F32)
    pick1 = jnp.zeros((tokens, 128), F32)
    pick2 = jnp.zeros((tokens, 128), F32)
    pick0 = [jnp.zeros((8, 128), F32) for _ in range(reqs)]
    lane = lax.broadcasted_iota(jnp.int32, (tokens, 128), 1)
    base = info_ref[BASE]
    tok = jnp.concatenate([tok_ref[...].astype(F32), jnp.full((reqs, 128 - tree), -1.0, F32)], axis=1)
    tok = jnp.transpose(tok)
    column = lambda n: jnp.concatenate([tok[n:n + tree, r:r + 1] for r in range(reqs)], axis=0).astype(jnp.int32)
    t1 = column(1) - base - lane
    t2 = column(2) - base - lane
    node = lax.broadcasted_iota(jnp.int32, (8, 128), 0)
    t0 = [jnp.where(node == 0, tok[0:8, r:r + 1].astype(jnp.int32) - base - lane[:8], -1) for r in range(reqs)]
    parts = [(w_ref, at, min(256, lead - at), at) for at in range(0, lead, 256)]
    parts += [(rest_ref, at, min(256, others - at), lead + at) for at in range(0, others, 256)]
    for ref, start, step, at in parts:
        if at == lead:
            load.wait()
        logits = jnp.dot(x_ref[...], ref[:, start:start + step], preferred_element_type=F32)
        for o in range(0, step, 128):
            lg = logits[:, o:o + 128]
            sums = sums + jnp.exp(lg)
            pick1 = jnp.where(t1 == at + o, lg, pick1)
            pick2 = jnp.where(t2 == at + o, lg, pick2)
            for r in range(reqs):
                pick0[r] = jnp.where(t0[r] == at + o, lg[r * tree:r * tree + 8], pick0[r])
    zero = jnp.zeros((tree - 8, 128), F32)
    pick0 = jnp.concatenate([p for r in range(reqs) for p in (pick0[r], zero)], axis=0)

    def by_request(a):
        a = jnp.sum(jnp.transpose(a), axis=0, keepdims=True)
        return jnp.concatenate([a[:, r * tree:(r + 1) * tree] for r in range(reqs)], axis=0)

    def later(a, n):
        return jnp.concatenate([a[:, :n], a[:, :tree - n]], axis=1)

    total, pick1, pick2, pick0 = (by_request(a) for a in (sums, pick1, pick2, pick0))
    at_node = lax.broadcasted_iota(jnp.int32, (reqs, tree), 1)
    near = par_ref[...] == at_node - 1
    root = at_node == 0
    pick = jnp.where(root, pick0, jnp.where(near, later(pick1, 1), later(pick2, 2)))
    total = jnp.where(root, total, jnp.where(near, later(total, 1), later(total, 2)))
    gap = jnp.zeros((reqs, 64 - tree), F32)
    stats = jnp.concatenate([total, gap, pick, gap], axis=1)
    for i in range(stat_ref.shape[0]):
        stat_ref[i] = stats
    copy.wait()


def vocab(info, mine, theirs, gain, toks, parents, lead, w, copies):
    nz, nx, rows, cols = mine.shape
    tokens, width = nz * rows, 2 * nx * cols
    vm = pl.BlockSpec(memory_space=pltpu.VMEM)
    return pl.pallas_call(
        vocab_kernel,
        out_shape=(
            jax.ShapeDtypeStruct((tokens, width), BF),
            jax.ShapeDtypeStruct((copies, toks.shape[0], 128), F32),
        ),
        in_specs=[pl.BlockSpec(memory_space=pltpu.SMEM), vm, vm, vm, vm, vm, vm, pl.BlockSpec(memory_space=pl.ANY)],
        out_specs=(pl.BlockSpec(memory_space=pl.ANY), vm),
        scratch_shapes=[
            pltpu.VMEM((tokens, width), BF),
            pltpu.VMEM((tokens, width), BF),
            pltpu.VMEM((width, w.shape[1] - lead.shape[1]), BF),
            pltpu.SemaphoreType.DMA((2,)),
        ],
        compiler_params=pltpu.CompilerParams(vmem_limit_bytes=24 * MB),
        name="vocab",
    )(info, mine, theirs, gain, toks, parents, lead, pltpu.with_memory_space_constraint(w, pltpu.HBM))


def fetch_kernel(w_ref, after_ref, out_ref, sem):
    copy = pltpu.make_async_copy(w_ref.at[:, pl.ds(0, out_ref.shape[1])], out_ref, sem)
    copy.start()
    copy.wait()


def fetch(w, after, cols):
    hbm = pl.BlockSpec(memory_space=pl.ANY)
    return pl.pallas_call(
        fetch_kernel,
        out_shape=jax.ShapeDtypeStruct((w.shape[0], cols), w.dtype),
        in_specs=[hbm, hbm],
        out_specs=pl.BlockSpec(memory_space=pltpu.VMEM),
        scratch_shapes=[pltpu.SemaphoreType.DMA],
        compiler_params=pltpu.CompilerParams(vmem_limit_bytes=2 * MB),
        name="fetch",
    )(pltpu.with_memory_space_constraint(w, pltpu.HBM), after)


def shifted(a, axis, step):
    n = lax.axis_size(axis)
    return lax.ppermute(a, axis, [(i, (i + step) % n) for i in range(n)])


def local(
    queries, new_keys, new_values, cache_keys, cache_values, lengths, parents,
    tree_tokens, residual, out_weight, norm_gain, vocab_weight,
):
    reqs, tree, width = queries.shape
    slots = cache_keys.shape[1]
    y, z, x, core = (lax.axis_index(a) for a in ("dp", "z", "x", "core"))
    ny, nz, nx, nc = (lax.axis_size(a) for a in ("dp", "z", "x", "core"))
    shard = (z * nx + x) * nc + core
    shards = nz * nx * nc
    window = slots * shards // 2
    half = width // nc
    block = half // nx
    tokens = reqs * tree
    swap = [(0, 1), (1, 0)]
    treq = jnp.where((shard >= reqs) & (shard < 2 * reqs), shard - reqs, -1)
    info = jnp.stack([core, shard * slots, treq, z, x, core * nx + x, y, shard * vocab_weight.shape[1]]).astype(jnp.int32)

    args = (lengths, parents, queries, cache_keys, cache_values, new_keys, new_values)
    spread = (nz, nx, nc, out_weight.shape[0], block)
    send, w = attend_half(window, info, *args, w=out_weight, spread=spread)
    got = lax.ppermute(send, "core", swap)
    w = lax.all_to_all(w.reshape(shards, -1, block), ("z", "x", "core"), 0, 0).reshape(-1, block)
    ws = [w] + [shifted(w, "dp", s) for s in range(1, ny)]
    (part,) = attend_half(window, info, *args, got=got)
    part = lax.all_to_all(part, ("z", "x"), 0, 0)
    att = combine(part, tokens // (nz * nx), half)
    own = pile([att] + [shifted(att, "x", s) for s in range(1, nx)], ws)
    other = lax.ppermute(own, "core", swap)
    rows = tokens // (nz * nx)
    mine = lax.dynamic_slice(
        residual.reshape(nz * nx, rows, width), (z * nx, 0, (core * nx + x) * block), (nx, rows, block)
    )
    hid = project(info, own, other, ws, mine, nz * nx).reshape(nz * nx, -1, block)
    hid = lax.all_to_all(hid, ("z", "x"), 0, 0).reshape(nz, nx, -1, block)
    other = lax.ppermute(hid, "core", swap)
    scorer = fetch(vocab_weight, hid, 1536)
    hidden, stats = vocab(info, hid, other, norm_gain.reshape(1, -1), tree_tokens, parents, scorer, vocab_weight, shards)
    stats = jnp.sum(lax.all_to_all(stats, ("z", "x", "core"), 0, 0), axis=0)
    logprob = stats[:, 64:64 + tree] - jnp.log(stats[:, :tree])
    return hidden.reshape(reqs, tree, width), logprob


def solution(mesh):
    sizes = (mesh.shape["dp"], 4, 4, 2)
    grid = Mesh(mesh.devices.reshape(sizes), ("dp", "z", "x", "core"))
    mp = ("z", "x", "core")
    row = P("dp", None, None)
    placed = (
        row, row, row, P("dp", mp, None), P("dp", mp, None), P("dp"), P("dp", None), P("dp", None), row,
        P(("dp",) + mp, None), P(), P(None, mp),
    )
    return jax.shard_map(local, mesh=grid, in_specs=placed, out_specs=(row, P("dp", None)), check_vma=False)
```

```python
import functools

import jax
import jax.numpy as jnp
from jax import lax
from jax.experimental import pallas as pl
from jax.experimental.pallas import tpu as pltpu
from jax.sharding import Mesh, PartitionSpec as P

HEADS = 16
SINK = 4
BF = jnp.bfloat16
F32 = jnp.float32
NT = (((1,), (1,)), ((), ()))
TN = (((0,), (0,)), ((), ()))
CORE, FIRST, TREQ, Z, X, BLOCK, DP, BASE = range(8)
MB = 1 << 20


def attend_kernel(window, add, info_ref, len_ref, par_ref, q_ref, k_ref, v_ref, nk_ref, nv_ref, *refs):
    step = pl.program_id(0)
    if add:
        got_ref, out_ref, anc_ref, new_ref, sem = refs
    else:
        w_ref, out_ref, spread_hbm, anc_ref, new_ref, sem, spread_ref, spread_sem = refs
        nz, nx, nc, _, block = spread_ref.shape
        leave = pltpu.make_async_copy(spread_ref, spread_hbm, spread_sem)

        @pl.when(step == 0)
        def _():
            for c in range(nc):
                for x in range(nx):
                    at = (c * nx + x) * block
                    for z in range(nz):
                        spread_ref[z, x, c] = w_ref[:, at:at + block]
            leave.start()

    first = info_ref[FIRST]
    treq = info_ref[TREQ]
    reqs, tree, width = q_ref.shape
    slots = k_ref.shape[1]
    heads = width // 128
    part = tree // 2
    scale = 128 ** (-0.5) * 1.4426950408889634
    zero = jnp.zeros((tree, 128), BF)
    pairs = [slice(p * 256, (p + 1) * 256) for p in range(heads // 2)]

    def score(r, keys):
        out = []
        for cols in pairs:
            q = q_ref[r, :, cols]
            q = jnp.concatenate(
                [jnp.concatenate([q[:, :128], zero], axis=1), jnp.concatenate([zero, q[:, 128:]], axis=1)], axis=0
            )
            out.append(lax.dot_general(keys(cols), q, NT, preferred_element_type=F32))
        return out

    def weigh(scores, mask):
        exps = [jnp.where(mask, jnp.exp2(s * scale), 0.0) for s in scores]
        dens = [jnp.sum(e, axis=0, keepdims=True) for e in exps]
        dens = [d[:, t * tree:(t + 1) * tree] for d in dens for t in range(2)]
        return [e.astype(BF) for e in exps], jnp.concatenate(dens, axis=0)

    def finish(r, exps, dens, values):
        for p, cols in enumerate(pairs):
            o = lax.dot_general(exps[p], values(cols), TN, preferred_element_type=F32)
            for h, val in ((2 * p, o[:tree, :128]), (2 * p + 1, o[tree:, 128:])):
                for t in range(2):
                    rows = slice(h * part, (h + 1) * part)
                    half = val[t * part:(t + 1) * part]
                    if add:
                        half = half + got_ref[2 * r + t, rows].astype(F32)
                    out_ref[2 * r + t, rows] = half.astype(BF)
        gap = jnp.zeros((heads, 64 - part), F32)
        for t in range(2):
            den = dens[:, t * part:(t + 1) * part]
            if add:
                got = got_ref[2 * r + t, heads * part:].astype(F32)
                den = den + got[:, :part] + got[:, 64:64 + part]
            high = den.astype(BF).astype(F32)
            out_ref[2 * r + t, heads * part:] = jnp.concatenate([high, gap, den - high, gap], axis=1).astype(BF)

    @pl.when(treq < 0)
    def _():
        pos = first + lax.broadcasted_iota(jnp.int32, (slots, 2 * tree), 0)
        scores = [score(r, lambda cols: k_ref[r, :, cols]) for r in range(reqs)]
        weights = []
        for r in range(reqs):
            length = len_ref[step * reqs + r]
            mask = (pos < length) & ((pos < SINK) | (pos >= length - window))
            weights.append(weigh(scores[r], mask))
        for r in range(reqs):
            finish(r, *weights[r], lambda cols: v_ref[r, :, cols])

    @pl.when(treq >= 0)
    def _():
        out_ref[...] = got_ref[...] if add else jnp.zeros_like(out_ref)

        @pl.when(treq // reqs == step)
        def _():
            half = info_ref[CORE] if add else 1 - info_ref[CORE]
            at = pl.ds(pl.multiple_of(half * width, 128), width)
            copies = [
                pltpu.make_async_copy(ref.at[treq, :, at], new_ref.at[i], sem.at[i])
                for i, ref in enumerate((nk_ref, nv_ref))
            ]
            for copy in copies:
                copy.start()
            node = lax.broadcasted_iota(jnp.int32, (1, 128), 1)
            anc_ref[...] = jnp.zeros_like(anc_ref)
            anc_ref[0:1, :] = jnp.where(node == 0, 1.0, 0.0)

            def body(i, carry):
                up = anc_ref[pl.ds(par_ref[treq, i], 1), :]
                anc_ref[pl.ds(i, 1), :] = jnp.where(node == i, 1.0, up)
                return carry

            lax.fori_loop(1, tree, body, 0)
            mask = jnp.transpose(anc_ref[...])[:tree, :tree]
            mask = jnp.concatenate([mask, mask], axis=1) > 0.5
            r = lax.rem(treq, reqs)
            for copy in copies:
                copy.wait()
            weights = weigh(score(r, lambda cols: new_ref[0, :, cols]), mask)
            finish(r, *weights, lambda cols: new_ref[1, :, cols])

    if not add:

        @pl.when(step == pl.num_programs(0) - 1)
        def _():
            leave.wait()


def attend_half(window, info, lengths, parents, q, k, v, nk, nv, got=None, w=None, spread=None):
    reqs, tree, width = q.shape
    slots = k.shape[1]
    half = width // 2
    group = reqs // 2
    add = got is not None
    hidx = (lambda i: i[CORE]) if add else (lambda i: 1 - i[CORE])
    qs = pl.BlockSpec((group, tree, half), lambda r, i, l, p: (r, 0, hidx(i)))
    ks = pl.BlockSpec((group, slots, half), lambda r, i, l, p: (r, 0, hidx(i)))
    ns = pl.BlockSpec(memory_space=pl.ANY)
    lengths, parents, q, k, v, nk, nv = (
        pltpu.with_memory_space_constraint(a, pltpu.HBM) for a in (lengths, parents, q, k, v, nk, nv)
    )
    rows = half // 128 * (tree // 2) + half // 128
    sums = pl.BlockSpec((2 * group, rows, 128), lambda r, i, l, p: (r, 0, 0))
    in_specs = [qs, ks, ks, ns, ns]
    out_specs = [sums]
    out_shape = [jax.ShapeDtypeStruct((2 * reqs, rows, 128), BF)]
    scratch = [pltpu.VMEM((128, 128), F32), pltpu.VMEM((2, tree, half), BF), pltpu.SemaphoreType.DMA((2,))]
    if add:
        extra = (got,)
        in_specs.append(sums)
    else:
        extra = (pltpu.with_memory_space_constraint(w, pltpu.HBM),)
        in_specs.append(pl.BlockSpec(w.shape, lambda r, i, l, p: (0, 0)))
        out_specs.append(pl.BlockSpec(memory_space=pl.ANY))
        scratch += [pltpu.VMEM(spread, w.dtype), pltpu.SemaphoreType.DMA]
        out_shape.append(jax.ShapeDtypeStruct(spread, w.dtype))
    return pl.pallas_call(
        functools.partial(attend_kernel, window, add),
        out_shape=out_shape,
        grid_spec=pltpu.PrefetchScalarGridSpec(
            num_scalar_prefetch=3,
            grid=(reqs // group,),
            in_specs=in_specs,
            out_specs=out_specs,
            scratch_shapes=scratch,
        ),
        compiler_params=pltpu.CompilerParams(vmem_limit_bytes=24 * MB),
        name="attend_mine" if add else "attend_theirs",
    )(info, lengths, parents, q, k, v, nk, nv, *extra)


def combine_kernel(parts_ref, out_ref):
    rows, width = out_ref.shape
    heads = width // 128
    total = jnp.sum(parts_ref[...].astype(F32), axis=0)
    den = total[heads * rows:]
    den = jnp.concatenate([den[:, :rows] + den[:, 64:64 + rows], jnp.ones((heads, 128 - rows), F32)], axis=1)
    den = jnp.transpose(jnp.concatenate([den, jnp.ones((128 - heads, 128), F32)], axis=0))
    for h in range(heads):
        val = total[h * rows:(h + 1) * rows] / den[:rows, h:h + 1]
        out_ref[:, h * 128:(h + 1) * 128] = val.astype(BF)


def combine(parts, rows, width):
    return pl.pallas_call(
        combine_kernel,
        out_shape=jax.ShapeDtypeStruct((rows, width), BF),
        compiler_params=pltpu.CompilerParams(vmem_limit_bytes=16 * MB),
        name="combine",
    )(parts)


def pile_kernel(n, *refs):
    for i in range(n):
        refs[-1][i] = refs[i][...]


def pile(arrays, after):
    shape = (len(arrays),) + arrays[0].shape
    vm = pl.BlockSpec(memory_space=pltpu.VMEM)
    return pl.pallas_call(
        functools.partial(pile_kernel, len(arrays)),
        out_shape=jax.ShapeDtypeStruct(shape, arrays[0].dtype),
        in_specs=[vm] * len(arrays) + [pl.BlockSpec(memory_space=pl.ANY)] * len(after),
        out_specs=vm,
        compiler_params=pltpu.CompilerParams(vmem_limit_bytes=2 * MB),
        name="pile",
    )(*arrays, *after)


def project_kernel(info_ref, own, other, *refs):
    ws, (res_ref, out_ref) = refs[:-2], refs[-2:]
    core, x, y = info_ref[CORE], info_ref[X], info_ref[DP]
    nx, rows, half = own.shape
    ny, deep = len(ws), ws[0].shape[0]
    mine = jnp.concatenate([own[s] for s in range(nx)], axis=0)
    theirs = jnp.concatenate([other[s] for s in range(nx)], axis=0)
    acc = None
    for s in range(ny):
        at = lax.rem(y + ny - s, ny)
        a = jnp.where(core == at // 2, mine, theirs)
        a = jnp.where(at % 2 == 0, a[:, :deep], a[:, deep:])
        part = jnp.dot(a, ws[s][...], preferred_element_type=F32)
        acc = part if acc is None else acc + part
    for s in range(nx):
        at = lax.rem(x + nx - s, nx)
        hid = (res_ref[at].astype(F32) + acc[s * rows:(s + 1) * rows]).astype(BF)
        for i in range(out_ref.shape[0]):
            out_ref[i, at] = hid


def project(info, own, other, ws, residual, copies):
    nx, rows, _ = own.shape
    vm = pl.BlockSpec(memory_space=pltpu.VMEM)
    return pl.pallas_call(
        project_kernel,
        out_shape=jax.ShapeDtypeStruct((copies, nx, rows, ws[0].shape[1]), BF),
        in_specs=[pl.BlockSpec(memory_space=pltpu.SMEM)] + [vm] * (3 + len(ws)),
        out_specs=vm,
        compiler_params=pltpu.CompilerParams(vmem_limit_bytes=8 * MB),
        name="project",
    )(info, own, other, *ws, residual)


def vocab_kernel(
    info_ref, mine_ref, theirs_ref, gain_ref, tok_ref, par_ref, w_ref, more_ref, hid_out, stat_ref, hid_ref, x_ref, rest_ref, sem
):
    lead, others = w_ref.shape[1], rest_ref.shape[1]
    load = pltpu.make_async_copy(more_ref.at[:, pl.ds(lead, others)], rest_ref, sem.at[1])
    load.start()
    core = info_ref[CORE]
    nz, nx, rows, cols = mine_ref.shape
    half = nx * cols
    for z in range(nz):
        rs = slice(z * rows, (z + 1) * rows)
        squares = jnp.zeros((rows, cols), F32)
        for x in range(nx):
            mine, theirs = mine_ref[z, x], theirs_ref[z, x]
            low = jnp.where(core == 0, mine, theirs)
            high = jnp.where(core == 0, theirs, mine)
            hid_ref[rs, x * cols:(x + 1) * cols] = low
            hid_ref[rs, half + x * cols:half + (x + 1) * cols] = high
            squares = squares + low.astype(F32) * low.astype(F32) + high.astype(F32) * high.astype(F32)
        inv = lax.rsqrt(jnp.sum(squares, axis=1, keepdims=True) / (2 * half) + 1e-06)
        for j in range(2 * nx):
            cs = slice(j * cols, (j + 1) * cols)
            x_ref[rs, cs] = (hid_ref[rs, cs].astype(F32) * inv * gain_ref[:, cs]).astype(BF)
    copy = pltpu.make_async_copy(hid_ref, hid_out, sem.at[0])
    copy.start()
    tokens = nz * rows
    reqs, tree = tok_ref.shape
    sums = jnp.zeros((tokens, 128), F32)
    pick1 = jnp.zeros((tokens, 128), F32)
    pick2 = jnp.zeros((tokens, 128), F32)
    pick0 = [jnp.zeros((8, 128), F32) for _ in range(reqs)]
    lane = lax.broadcasted_iota(jnp.int32, (tokens, 128), 1)
    base = info_ref[BASE]
    tok = jnp.concatenate([tok_ref[...].astype(F32), jnp.full((reqs, 128 - tree), -1.0, F32)], axis=1)
    tok = jnp.transpose(tok)
    column = lambda n: jnp.concatenate([tok[n:n + tree, r:r + 1] for r in range(reqs)], axis=0).astype(jnp.int32)
    t1 = column(1) - base - lane
    t2 = column(2) - base - lane
    node = lax.broadcasted_iota(jnp.int32, (8, 128), 0)
    t0 = [jnp.where(node == 0, tok[0:8, r:r + 1].astype(jnp.int32) - base - lane[:8], -1) for r in range(reqs)]
    parts = [(w_ref, at, min(256, lead - at), at) for at in range(0, lead, 256)]
    parts += [(rest_ref, at, min(256, others - at), lead + at) for at in range(0, others, 256)]
    for ref, start, step, at in parts:
        if at == lead:
            load.wait()
        logits = jnp.dot(x_ref[...], ref[:, start:start + step], preferred_element_type=F32)
        for o in range(0, step, 128):
            lg = logits[:, o:o + 128]
            sums = sums + jnp.exp(lg)
            pick1 = jnp.where(t1 == at + o, lg, pick1)
            pick2 = jnp.where(t2 == at + o, lg, pick2)
            for r in range(reqs):
                pick0[r] = jnp.where(t0[r] == at + o, lg[r * tree:r * tree + 8], pick0[r])
    zero = jnp.zeros((tree - 8, 128), F32)
    pick0 = jnp.concatenate([p for r in range(reqs) for p in (pick0[r], zero)], axis=0)

    def by_request(a):
        a = jnp.sum(jnp.transpose(a), axis=0, keepdims=True)
        return jnp.concatenate([a[:, r * tree:(r + 1) * tree] for r in range(reqs)], axis=0)

    def later(a, n):
        return jnp.concatenate([a[:, :n], a[:, :tree - n]], axis=1)

    total, pick1, pick2, pick0 = (by_request(a) for a in (sums, pick1, pick2, pick0))
    at_node = lax.broadcasted_iota(jnp.int32, (reqs, tree), 1)
    near = par_ref[...] == at_node - 1
    root = at_node == 0
    pick = jnp.where(root, pick0, jnp.where(near, later(pick1, 1), later(pick2, 2)))
    total = jnp.where(root, total, jnp.where(near, later(total, 1), later(total, 2)))
    gap = jnp.zeros((reqs, 64 - tree), F32)
    stats = jnp.concatenate([total, gap, pick, gap], axis=1)
    for i in range(stat_ref.shape[0]):
        stat_ref[i] = stats
    copy.wait()


def vocab(info, mine, theirs, gain, toks, parents, lead, w, copies):
    nz, nx, rows, cols = mine.shape
    tokens, width = nz * rows, 2 * nx * cols
    vm = pl.BlockSpec(memory_space=pltpu.VMEM)
    return pl.pallas_call(
        vocab_kernel,
        out_shape=(
            jax.ShapeDtypeStruct((tokens, width), BF),
            jax.ShapeDtypeStruct((copies, toks.shape[0], 128), F32),
        ),
        in_specs=[pl.BlockSpec(memory_space=pltpu.SMEM), vm, vm, vm, vm, vm, vm, pl.BlockSpec(memory_space=pl.ANY)],
        out_specs=(pl.BlockSpec(memory_space=pl.ANY), vm),
        scratch_shapes=[
            pltpu.VMEM((tokens, width), BF),
            pltpu.VMEM((tokens, width), BF),
            pltpu.VMEM((width, w.shape[1] - lead.shape[1]), BF),
            pltpu.SemaphoreType.DMA((2,)),
        ],
        compiler_params=pltpu.CompilerParams(vmem_limit_bytes=24 * MB),
        name="vocab",
    )(info, mine, theirs, gain, toks, parents, lead, pltpu.with_memory_space_constraint(w, pltpu.HBM))


def settle_kernel(stat_ref, out_ref):
    tree = out_ref.shape[1]
    stats = jnp.sum(stat_ref[...], axis=0)
    out_ref[...] = stats[:, 64:64 + tree] - jnp.log(stats[:, :tree])


def settle(stats, tree):
    return pl.pallas_call(
        settle_kernel,
        out_shape=jax.ShapeDtypeStruct((stats.shape[1], tree), F32),
        compiler_params=pltpu.CompilerParams(vmem_limit_bytes=2 * MB),
        name="settle",
    )(stats)


def fetch_kernel(w_ref, after_ref, out_ref, sem):
    copy = pltpu.make_async_copy(w_ref.at[:, pl.ds(0, out_ref.shape[1])], out_ref, sem)
    copy.start()
    copy.wait()


def fetch(w, after, cols):
    hbm = pl.BlockSpec(memory_space=pl.ANY)
    return pl.pallas_call(
        fetch_kernel,
        out_shape=jax.ShapeDtypeStruct((w.shape[0], cols), w.dtype),
        in_specs=[hbm, hbm],
        out_specs=pl.BlockSpec(memory_space=pltpu.VMEM),
        scratch_shapes=[pltpu.SemaphoreType.DMA],
        compiler_params=pltpu.CompilerParams(vmem_limit_bytes=2 * MB),
        name="fetch",
    )(pltpu.with_memory_space_constraint(w, pltpu.HBM), after)


def shifted(a, axis, step):
    n = lax.axis_size(axis)
    return lax.ppermute(a, axis, [(i, (i + step) % n) for i in range(n)])


def local(
    queries, new_keys, new_values, cache_keys, cache_values, lengths, parents,
    tree_tokens, residual, out_weight, norm_gain, vocab_weight,
):
    reqs, tree, width = queries.shape
    slots = cache_keys.shape[1]
    y, z, x, core = (lax.axis_index(a) for a in ("dp", "z", "x", "core"))
    ny, nz, nx, nc = (lax.axis_size(a) for a in ("dp", "z", "x", "core"))
    shard = (z * nx + x) * nc + core
    shards = nz * nx * nc
    window = slots * shards // 2
    half = width // nc
    block = half // nx
    tokens = reqs * tree
    swap = [(0, 1), (1, 0)]
    treq = jnp.where((shard >= reqs) & (shard < 2 * reqs), shard - reqs, -1)
    info = jnp.stack([core, shard * slots, treq, z, x, core * nx + x, y, shard * vocab_weight.shape[1]]).astype(jnp.int32)

    args = (lengths, parents, queries, cache_keys, cache_values, new_keys, new_values)
    spread = (nz, nx, nc, out_weight.shape[0], block)
    send, w = attend_half(window, info, *args, w=out_weight, spread=spread)
    got = lax.ppermute(send, "core", swap)
    w = lax.all_to_all(w.reshape(shards, -1, block), ("z", "x", "core"), 0, 0).reshape(-1, block)
    ws = [w] + [shifted(w, "dp", s) for s in range(1, ny)]
    (part,) = attend_half(window, info, *args, got=got)
    part = lax.all_to_all(part, ("z", "x"), 0, 0)
    att = combine(part, tokens // (nz * nx), half)
    own = pile([att] + [shifted(att, "x", s) for s in range(1, nx)], ws)
    other = lax.ppermute(own, "core", swap)
    rows = tokens // (nz * nx)
    mine = lax.dynamic_slice(
        residual.reshape(nz * nx, rows, width), (z * nx, 0, (core * nx + x) * block), (nx, rows, block)
    )
    hid = project(info, own, other, ws, mine, nz * nx).reshape(nz * nx, -1, block)
    hid = lax.all_to_all(hid, ("z", "x"), 0, 0).reshape(nz, nx, -1, block)
    other = lax.ppermute(hid, "core", swap)
    scorer = fetch(vocab_weight, hid, 1536)
    hidden, stats = vocab(info, hid, other, norm_gain.reshape(1, -1), tree_tokens, parents, scorer, vocab_weight, shards)
    logprob = settle(lax.all_to_all(stats, ("z", "x", "core"), 0, 0), tree)
    return hidden.reshape(reqs, tree, width), logprob


def solution(mesh):
    sizes = (mesh.shape["dp"], 4, 4, 2)
    grid = Mesh(mesh.devices.reshape(sizes), ("dp", "z", "x", "core"))
    mp = ("z", "x", "core")
    row = P("dp", None, None)
    placed = (
        row, row, row, P("dp", mp, None), P("dp", mp, None), P("dp"), P("dp", None), P("dp", None), row,
        P(("dp",) + mp, None), P(), P(None, mp),
    )
    return jax.shard_map(local, mesh=grid, in_specs=placed, out_specs=(row, P("dp", None)), check_vma=False)
```
